32 devices in a mesh: seq: 8 (over y, x, core), mp: 4 (over z).
Axes of the slice: x: 2, y: 2, z: 4, core: 2. Of those that a mesh axis runs over, the one named last changes fastest.
Arguments:
- tokens: bfloat16 [64, 2048, 1024], P('mp', 'seq'), may hold values from -6 to 6
- cotangent: bfloat16 [64, 2048, 1024], P('mp', 'seq'), may hold values from -6 to 6
- lengths: int32 [64], P('mp'), may hold values from 256 to 2048, as said below
- routed: int32 [64, 256], P('mp', 'seq'), may hold values from 0 to 2047, as said below
- gain_attn: float32 [1024], replicated, may hold values from 0.5 to 1.5
- gain_mlp: float32 [1024], replicated, may hold values from 0.5 to 1.5
- router: float32 [1024], replicated, may hold values from -0.1875 to 0.1875
- w_qkv: bfloat16 [3, 1024, 1024], P(None, None, 'mp'), may hold values from -0.1875 to 0.1875
- w_out: bfloat16 [1024, 1024], P('mp'), may hold values from -1.5 to 1.5
- w_mlp: bfloat16 [4096, 2, 1024], P('mp'), may hold values from -0.1875 to 0.1875
Outputs:
- layer_out: bfloat16 [64, 2048, 1024], P('mp', 'seq')
- grad_tokens: bfloat16 [64, 2048, 1024], P('mp', 'seq')
- grad_gain_attn: float32 [1024], replicated
- grad_gain_mlp: float32 [1024], replicated
- grad_router: float32 [1024], replicated
- grad_qkv: float32 [3, 1024, 1024], P(None, None, 'mp')
- grad_out: float32 [1024, 1024], P('mp')
- grad_mlp: float32 [4096, 2, 1024], P('mp')
The draws below stay inside these ranges and needn't reach their ends.
Inputs may be any that keep to these rules, and one draw needn't show every extreme that they name: `lengths`: multiples of 8; of the two sequences 2 i and 2 i + 1 (aligned pairs) at most one is longer than 1024; among the 16 sequences of each index of mp one has length 2048 and its partner in the pair has length 256. `routed`: entry j of a sequence lies in 8 j to 8 j + 7; entries with j at or past lengths / 8 point at padding.
All inputs are finite; a program needn't handle non-finite values.
Results may differ from the reference program's by a relative error of at most 0.017.
Values may be sent and summed in bfloat16 or wider, within the bound.
No kernel may reach another device: no remote copies, remote signals or barrier semaphores. Data moves between devices by JAX's collectives and lax.ppermute only.
A program may use at most 192 MiB of HBM per device.

```python
import jax
import jax.numpy as jnp
from jax import lax

D = 1024
HEADS = 16
HEAD = 64
FF = 4096
SLOT = 2048
KMAX = 256
GROUP = 16
SEQS = 64


def length_table(key):
    base = jax.random.fold_in(key, 17)
    key_long, key_short, key_which, key_spot = jax.random.split(base, 4)
    pair_count = SEQS // 2
    longer = 8 * jax.random.randint(key_long, (pair_count,), KMAX // 8, SLOT // 8 + 1)
    shorter = 8 * jax.random.randint(key_short, (pair_count,), KMAX // 8, SLOT // 16 + 1)
    which = jax.random.randint(key_which, (pair_count,), 0, 2)
    spot = jax.random.randint(key_spot, (SEQS // GROUP,), 0, GROUP // 2)
    pair_index = jnp.arange(pair_count)
    within = pair_index % (GROUP // 2)
    chosen = within == spot[pair_index // (GROUP // 2)]
    longer = jnp.where(chosen, SLOT, longer)
    shorter = jnp.where(chosen, KMAX, shorter)
    first = jnp.where(which == 0, longer, shorter)
    second = jnp.where(which == 0, shorter, longer)
    return jnp.stack([first, second], axis=1).reshape(SEQS).astype(jnp.int32)


def draw_lengths(key, part):
    return length_table(key)


def draw_routed(key, part):
    base = jax.random.fold_in(key, 29)
    offsets = jax.random.randint(base, (SEQS, KMAX), 0, 8)
    return (8 * jnp.arange(KMAX, dtype=jnp.int32)[None, :] + offsets).astype(jnp.int32)


def levels(rng, extent, cuts, low, largest):
    loudness, own = 1.0, jax.random.fold_in(rng, 6)
    for axis_at, shards_of in cuts:
        heights = jnp.exp(jax.random.uniform(jax.random.fold_in(own, axis_at), (shards_of,), jnp.float32, low / len(cuts), largest / len(cuts)))
        loudness = loudness * jnp.repeat(heights, extent[axis_at] // shards_of).reshape([-1 if axis == axis_at else 1 for axis in range(len(extent))])
    return loudness


def gaussian(stream_key, shape, scale, limit, pieces=(), kind=jnp.bfloat16):
    entries = jax.random.normal(stream_key, shape, jnp.float32) * scale
    if len(pieces) > 0:
        entries = levels(stream_key, shape, pieces, -0.22, 0.18) * entries
    return jnp.clip(entries, min=-limit, max=limit).astype(kind)


def setup_inputs(seed: int = 0) -> dict:
    arg_keys = jax.random.split(jax.random.key(seed), 11)
    return {
        "tokens": gaussian(arg_keys[0], (SEQS, SLOT, D), 1.0, 6.0, ((0, 4), (1, 8))),
        "cotangent": gaussian(arg_keys[1], (SEQS, SLOT, D), 1.0, 6.0, ((0, 4), (1, 8))),
        "lengths": draw_lengths(jax.random.fold_in(arg_keys[10], 71), 0),
        "routed": draw_routed(jax.random.fold_in(arg_keys[10], 71), 0),
        "gain_attn": jnp.clip(1.0 + 0.1 * jax.random.normal(arg_keys[4], (D,), jnp.float32), 0.5, 1.5),
        "gain_mlp": jnp.clip(1.0 + 0.1 * jax.random.normal(arg_keys[5], (D,), jnp.float32), 0.5, 1.5),
        "router": gaussian(arg_keys[6], (D,), D ** -0.5, 0.1875, (), jnp.float32),
        "w_qkv": gaussian(arg_keys[7], (3, D, D), D ** -0.5, 0.1875, ((2, 4),)),
        "w_out": gaussian(arg_keys[8], (D, D), (4 * D // KMAX) ** -0.5, 1.5, ((0, 4),)),
        "w_mlp": gaussian(arg_keys[9], (FF, 2, D), D ** -0.5, 0.1875, ((0, 4),)),
    }


EPSILON = 1e-06
NEGATIVE = -1e+30
BEST = lax.Precision.HIGHEST

@jax.custom_vjp
def low(v):
    return lax.optimization_barrier(v.astype(jnp.bfloat16)).astype(jnp.float32)

@jax.custom_vjp
def low_back(v):
    return v

def low_keep(v):
    return (low(v), None)

def low_pass(kept, grad):
    return (grad,)

def back_keep(v):
    return (v, None)

def back_low(kept, grad):
    return (low(grad),)
low.defvjp(low_keep, low_pass)
low_back.defvjp(back_keep, back_low)

def product(left, right):
    return jnp.dot(left, right, precision=BEST)

def rms_scale(values):
    return lax.rsqrt(lax.optimization_barrier(jnp.mean(values * values, axis=-1, keepdims=True)) + EPSILON)

def sequence_layer(seq_tokens, gain_attn, gain_mlp, router, w_qkv, w_out, w_mlp, positions, live):
    picked = low_back(jnp.take(seq_tokens, positions, axis=0))
    unit_one = picked * rms_scale(picked)
    normed_one = low(unit_one * gain_attn)
    gate = jax.nn.sigmoid(product(picked, router))
    query = low(low_back(product(normed_one, w_qkv[0]))).reshape(KMAX, HEADS, HEAD)
    keys = low(low_back(product(normed_one, w_qkv[1]))).reshape(KMAX, HEADS, HEAD)
    values = low(low_back(product(normed_one, w_qkv[2]))).reshape(KMAX, HEADS, HEAD)
    scores = low_back(HEAD ** (-0.5) * jnp.einsum('qhd,khd->hqk', query, keys, precision=BEST))
    causal = jnp.arange(KMAX)[:, None] >= jnp.arange(KMAX)[None, :]
    scores = jnp.where(causal[None], scores, NEGATIVE)
    weights = low(jax.nn.softmax(scores, axis=-1))
    mixed = jnp.einsum('hqk,khd->qhd', weights, values, precision=BEST).reshape(KMAX, D)
    mixed = low(low_back(mixed))
    attended = low_back(product(mixed, w_out))
    middle = picked + attended
    unit_two = middle * rms_scale(middle)
    normed_two = low(unit_two * gain_mlp)
    upward = low_back(product(normed_two, w_mlp[:, 0, :].T))
    active = low(jax.nn.gelu(upward, approximate=True))
    feed = low_back(product(active, w_mlp[:, 1, :]))
    returned = low(gate[:, None] * (attended + feed)) * live[:, None]
    return seq_tokens.at[positions].add(returned)

def reference(tokens, cotangent, lengths, routed, gain_attn, gain_mlp, router, w_qkv, w_out, w_mlp):
    params = (gain_attn.astype(jnp.float32), gain_mlp.astype(jnp.float32), router.astype(jnp.float32), w_qkv.astype(jnp.float32), w_out.astype(jnp.float32), w_mlp.astype(jnp.float32))

    def step(carry, item):
        seq_tokens, seq_grad, positions, length = item
        live = (jnp.arange(KMAX) < length // 8).astype(jnp.float32)

        def layer(seq_float, gain_one, gain_two, router_w, qkv_w, out_w, mlp_w):
            return sequence_layer(seq_float, gain_one, gain_two, router_w, qkv_w, out_w, mlp_w, positions, live)
        result, pullback = jax.vjp(layer, seq_tokens.astype(jnp.float32), *params)
        grads = pullback(seq_grad.astype(jnp.float32))
        carry = tuple((total + part for total, part in zip(carry, grads[1:])))
        return (carry, (result.astype(jnp.bfloat16), grads[0].astype(jnp.bfloat16)))
    zeros = tuple((jnp.zeros_like(param) for param in params))
    totals, (outputs, input_grad) = lax.scan(step, zeros, (tokens, cotangent, routed, lengths))
    return (outputs, input_grad, totals[0], totals[1], totals[2], totals[3], totals[4], totals[5])
```

```python
import functools

import jax
import jax.numpy as jnp
from jax import lax
from jax.experimental import pallas as pl
from jax.experimental.pallas import tpu as pltpu
from jax.sharding import PartitionSpec as P

HEAD = 64
LANES = 128
EPSILON = 1e-06
NEGATIVE = -1e30
ROOT = 0.7978845608028654
CUBE = 0.044715
SCALE = HEAD**-0.5
F32 = jnp.float32
BF16 = jnp.bfloat16
VMEM_BYTES = 50 * 1024 * 1024

NN = (((1,), (0,)), ((), ()))
NT = (((1,), (1,)), ((), ()))
TN = (((0,), (0,)), ((), ()))

ANY = pl.BlockSpec(memory_space=pl.ANY)
IN_VMEM = pl.BlockSpec(memory_space=pltpu.VMEM)
IN_SMEM = pl.BlockSpec(memory_space=pltpu.SMEM)


def mm(left, right, dims):
    return lax.dot_general(left, right, dims, preferred_element_type=F32)


def cost(flops, bytes_accessed, transcendentals=0):
    return pl.CostEstimate(
        flops=int(flops), bytes_accessed=int(bytes_accessed), transcendentals=int(transcendentals)
    )


def params(semantics=None):
    return pltpu.CompilerParams(dimension_semantics=semantics, vmem_limit_bytes=VMEM_BYTES)


def bit_lists(ranks):
    off = list(range(1, ranks.bit_length() - 1))
    return off, off[::-1]


def exchange(value, offset):
    ranks = lax.axis_size("seq")
    return lax.ppermute(value, "seq", [(i, i ^ offset) for i in range(ranks)])


def ring(value):
    depth = lax.axis_size("mp")
    cycle = [0] + list(range(1, depth, 2)) + list(range(2, depth, 2))[::-1]
    pairs = [(cycle[i], cycle[(i + 1) % depth]) for i in range(depth)]
    return lax.ppermute(value, "mp", pairs)


def joined(arrays):
    return arrays[0] if len(arrays) == 1 else jnp.concatenate(arrays, axis=0)


def gather_places(ranks, bits):
    held = [[0]]
    for bit in bits:
        flat = [i for part in held for i in part]
        held = [flat, [i | (1 << bit) for i in flat]]
    return held + [[i | 1 for i in part] for part in held]


def gather(piece, bits):
    held = [piece[None]]
    for bit in bits:
        whole = joined(held)
        held = [whole, exchange(whole, 1 << bit)]
    return held + [exchange(part, 1) for part in held]


def scatter_order(ranks, bits):
    order = []
    for j in range(ranks // 2):
        index = 0
        for place, bit in enumerate(bits):
            if (j >> (len(bits) - 1 - place)) & 1:
                index |= 1 << bit
        order.append(index)
    return order


def added(left, right):
    return (left.astype(F32) + right.astype(F32)).astype(BF16)


def scatter(keep, send, bits):
    total = added(keep, exchange(send, 1))
    for bit in bits:
        half = total.shape[0] // 2
        total = added(total[:half], exchange(total[half:], 1 << bit))
    return total[0]


def sum_everywhere(value):
    for axis in ("seq", "mp"):
        size = lax.axis_size(axis)
        step = 1
        while step < size:
            value = value + lax.ppermute(value, axis, [(i, i ^ step) for i in range(size)])
            step *= 2
    return value


def select_kernel(place_ref, tokens_ref, grads_ref, out_tokens, out_grads):
    span = tokens_ref.shape[1]
    place = place_ref[0]
    slots = place.shape[0]
    hot = (lax.broadcasted_iota(jnp.int32, (slots, span), 1) == place).astype(BF16)
    out_tokens[0] = mm(hot, tokens_ref[0], NN).astype(BF16)
    out_grads[0] = mm(hot, grads_ref[0], NN).astype(BF16)


def select_rows(place, tokens, cotangent):
    group, span, width = tokens.shape
    slots = place.shape[1]
    shape = jax.ShapeDtypeStruct((group, slots, width), BF16)
    rows = pl.BlockSpec((1, slots, width), lambda g: (g, 0, 0))
    block = pl.BlockSpec((1, span, width), lambda g: (g, 0, 0))
    return pl.pallas_call(
        select_kernel,
        grid=(group,),
        in_specs=[pl.BlockSpec((1, slots, 1), lambda g: (g, 0, 0)), block, block],
        out_specs=[rows, rows],
        out_shape=[shape, shape],
        compiler_params=params(("arbitrary",)),
        cost_estimate=cost(4 * group * slots * span * width, 4 * group * (span + slots) * width),
    )(place[:, :, None], tokens, cotangent)


def add_kernel(place_ref, base_ref, rows_ref, out_ref):
    span = base_ref.shape[1]
    place = place_ref[0]
    slots = place.shape[1]
    hot = (lax.broadcasted_iota(jnp.int32, (span, slots), 0) == place).astype(BF16)
    moved = mm(hot, rows_ref[0], NN)
    out_ref[0] = (base_ref[0].astype(F32) + moved).astype(BF16)


def add_rows(place, base, rows):
    group, span, width = base.shape
    slots = place.shape[1]
    block = pl.BlockSpec((1, span, width), lambda g: (g, 0, 0))
    return pl.pallas_call(
        add_kernel,
        grid=(group,),
        in_specs=[
            pl.BlockSpec((1, 1, slots), lambda g: (g, 0, 0)),
            block,
            pl.BlockSpec((1, slots, width), lambda g: (g, 0, 0)),
        ],
        out_specs=block,
        out_shape=jax.ShapeDtypeStruct(base.shape, BF16),
        compiler_params=params(("arbitrary",)),
        cost_estimate=cost(2 * group * slots * span * width, 4 * group * span * width),
    )(place[:, None, :], base, rows)


def start_all(copies, sems):
    started = []
    for at, (source, target) in enumerate(copies):
        copy = pltpu.make_async_copy(source, target, sems.at[at])
        copy.start()
        started.append(copy)
    return started


def attention_copies(me, sources, places, target):
    if len(sources) == 1:
        return [(sources[0], target)]
    half = len(sources) // 2
    depth = sources[0].shape[2]
    copies = []
    for side in range(2):
        for source, ids in zip(sources[side * half : (side + 1) * half], places[side]):
            for at, index in enumerate(ids):
                start = pl.multiple_of((me ^ index) * depth, depth)
                copies.append(
                    (
                        source.at[at],
                        target.at[pl.ds(2 * side, 2), pl.ds(start, depth), :],
                    )
                )
    return copies


def mlp_copies(me, sources, places, order, targets):
    half = len(sources) // 2
    copies = []
    for place, index in enumerate(order):
        for side in range(2):
            target = targets[side]
            if half == 1:
                depth = target.shape[0] // len(order)
                start = pl.multiple_of((me ^ index) * depth, depth)
                source = sources[side].at[pl.ds(start, depth), :]
            else:
                for array, ids in zip(sources[side * half : (side + 1) * half], places[side]):
                    if index in ids:
                        source = array.at[ids.index(index)]
                        depth = array.shape[1]
            copies.append((source, target.at[pl.ds(place * depth, depth), :]))
    return copies


def row_blocks(rows):
    half = rows // 3
    return (
        (0, half, 0, half),
        (half, 2 * half, 0, 2 * half),
        (2 * half, rows, 2 * half, rows),
    )


def causal(first, last, low, high):
    shape = (last - first, high - low)
    row = lax.broadcasted_iota(jnp.int32, shape, 0) + (first - low)
    return row >= lax.broadcasted_iota(jnp.int32, shape, 1)


def attention_forward_kernel(places, n_sources, has_acc, me_ref, normed_ref, *refs):
    sources, refs = refs[:n_sources], refs[n_sources:]
    if has_acc:
        acc_ref, refs = refs[0], refs[1:]
    attended_ref, heads_ref, mixed_ref, log_ref, held, sems = refs
    copies = start_all(attention_copies(me_ref[0], sources, places, held), sems)
    for copy in copies:
        copy.wait()
    rows = normed_ref.shape[0]
    width = held.shape[2]
    for c in range(3):
        heads_ref[c] = mm(normed_ref[...], held[c], NN).astype(BF16)
    lane = lax.broadcasted_iota(jnp.int32, (1, LANES), 1)
    logs = [jnp.zeros((last - first, LANES), F32) for first, last, low, high in row_blocks(rows)]
    for pair in range(width // LANES):
        lanes = slice(pair * LANES, (pair + 1) * LANES)
        for at, (first, last, low, high) in enumerate(row_blocks(rows)):
            query = heads_ref[0, first:last, lanes]
            keys = heads_ref[1, low:high, lanes]
            values = heads_ref[2, low:high, lanes]
            seen = causal(first, last, low, high)
            out = None
            for side in range(2):
                mine = (lane >= HEAD) if side else (lane < HEAD)
                scores = mm(jnp.where(mine, query, jnp.zeros_like(query)), keys, NT) * SCALE
                scores = jnp.where(seen, scores, NEGATIVE)
                peak = jnp.max(scores, axis=-1, keepdims=True)
                raised = jnp.exp(scores - peak)
                total = jnp.sum(raised, axis=-1, keepdims=True)
                weights = (raised * (1.0 / total)).astype(BF16)
                part = mm(weights, values, NN)
                out = part if out is None else jnp.where(mine, part, out)
                logs[at] = jnp.where(lane == 2 * pair + side, peak + jnp.log(total), logs[at])
            mixed_ref[first:last, lanes] = out.astype(BF16)
    for at, (first, last, low, high) in enumerate(row_blocks(rows)):
        log_ref[first:last, :] = logs[at]
    attended = mm(mixed_ref[...], held[3], NT)
    if has_acc:
        attended = attended + acc_ref[...]
    attended_ref[...] = attended


def attention_forward(me, normed, sources, places, acc):
    rows, width = normed.shape
    columns = sources[0].shape[-1]
    has_acc = acc is not None
    n_sources = len(sources)
    n_copies = 1 if n_sources == 1 else 2 * lax.axis_size("seq")
    flops = 2 * rows * width * columns * 4 + 4 * rows * rows * columns
    return pl.pallas_call(
        functools.partial(attention_forward_kernel, places, n_sources, has_acc),
        in_specs=[IN_SMEM, IN_VMEM] + [ANY] * n_sources + [IN_VMEM] * has_acc,
        out_specs=[IN_VMEM] * 4,
        out_shape=[
            jax.ShapeDtypeStruct((rows, width), F32),
            jax.ShapeDtypeStruct((3, rows, columns), BF16),
            jax.ShapeDtypeStruct((rows, columns), BF16),
            jax.ShapeDtypeStruct((rows, LANES), F32),
        ],
        scratch_shapes=[
            pltpu.VMEM((4, width, columns), BF16),
            pltpu.SemaphoreType.DMA((n_copies,)),
        ],
        input_output_aliases={2 + n_sources: 0} if has_acc else {},
        compiler_params=params(),
        cost_estimate=cost(flops, 8 * rows * width + 8 * width * columns, rows * rows * 4),
    )(me, normed, *sources, *([acc] if has_acc else []))


def attention_backward_kernel(
    places, orders, n_sources, has_acc, me_ref, grad_ref, normed_ref, heads_ref, mixed_ref, log_ref, *refs
):
    sources, refs = refs[:n_sources], refs[n_sources:]
    if has_acc:
        acc_ref, refs = refs[0], refs[1:]
    grad_normed_ref, refs = refs[0], refs[1:]
    outs, refs = refs[:4], refs[4:]
    held, grad_held, grad_heads, sems, out_sems = refs
    me = me_ref[0]
    copies = start_all(attention_copies(me, sources, places, held), sems)
    rows = normed_ref.shape[0]
    width = held.shape[2]
    depth = outs[0].shape[2]
    grad_held[3] = mm(grad_ref[...], mixed_ref[...], TN).astype(BF16)
    for copy in copies:
        copy.wait()
    grad_mixed = mm(grad_ref[...], held[3], NN).astype(BF16)
    lane = lax.broadcasted_iota(jnp.int32, (1, LANES), 1)
    for pair in range(width // LANES):
        lanes = slice(pair * LANES, (pair + 1) * LANES)
        key_parts, value_parts = [], []
        for first, last, low, high in row_blocks(rows):
            query = heads_ref[0, first:last, lanes]
            keys = heads_ref[1, low:high, lanes]
            values = heads_ref[2, low:high, lanes]
            grad_out = grad_mixed[first:last, lanes]
            logs = log_ref[first:last, :]
            seen = causal(first, last, low, high)
            grad_query = grad_keys = grad_values = None
            for side in range(2):
                mine = (lane >= HEAD) if side else (lane < HEAD)
                own_query = jnp.where(mine, query, jnp.zeros_like(query))
                own_grad = jnp.where(mine, grad_out, jnp.zeros_like(grad_out))
                log_total = jnp.sum(
                    jnp.where(lane == 2 * pair + side, logs, 0.0), axis=-1, keepdims=True
                )
                scores = jnp.where(seen, mm(own_query, keys, NT) * SCALE, NEGATIVE)
                shares = jnp.exp(scores - log_total)
                grad_weights = mm(own_grad, values, NT)
                inner = jnp.sum(shares * grad_weights, axis=-1, keepdims=True)
                grad_scores = (shares * (grad_weights - inner)).astype(BF16)
                weights = shares.astype(BF16)
                part_query = mm(grad_scores, keys, NN)
                part_keys = mm(grad_scores, own_query, TN)
                part_values = mm(weights, own_grad, TN)
                if side == 0:
                    grad_query, grad_keys, grad_values = part_query, part_keys, part_values
                else:
                    grad_query = jnp.where(mine, part_query, grad_query)
                    grad_keys = grad_keys + part_keys
                    grad_values = grad_values + part_values
            grad_heads[0, first:last, lanes] = (grad_query * SCALE).astype(BF16)
            key_parts.append(grad_keys)
            value_parts.append(grad_values)
        half = rows // 3
        for c, parts, scale in ((1, key_parts, SCALE), (2, value_parts, 1.0)):
            early = parts[0] + parts[1][:half]
            for at, value in enumerate((early, parts[1][half:], parts[2])):
                grad_heads[c, at * half : (at + 1) * half, lanes] = (value * scale).astype(BF16)
    grad_normed = mm(grad_heads[0], held[0], NT)
    for c in range(1, 3):
        grad_normed = grad_normed + mm(grad_heads[c], held[c], NT)
    if has_acc:
        grad_normed = grad_normed + acc_ref[...]
    grad_normed_ref[...] = grad_normed
    for c in range(3):
        grad_held[c] = mm(normed_ref[...], grad_heads[c], TN).astype(BF16)
    copies = []
    for side in range(2):
        for core in range(2):
            for at, index in enumerate(orders[side]):
                start = pl.multiple_of((me ^ (index | core)) * depth, depth)
                copies.append(
                    (
                        grad_held.at[pl.ds(2 * side, 2), pl.ds(start, depth), :],
                        outs[2 * side + core].at[at],
                    )
                )
    for copy in start_all(copies, out_sems):
        copy.wait()


def attention_backward(me, grad, normed, heads, mixed, logs, sources, places, orders, acc):
    rows, width = normed.shape
    columns = mixed.shape[-1]
    ranks = lax.axis_size("seq")
    has_acc = acc is not None
    n_sources = len(sources)
    n_copies = 1 if n_sources == 1 else 2 * ranks
    piece = jax.ShapeDtypeStruct((ranks // 2, 2, width // ranks, columns), BF16)
    flops = 2 * rows * width * columns * 8 + 10 * rows * rows * columns
    return pl.pallas_call(
        functools.partial(attention_backward_kernel, places, orders, n_sources, has_acc),
        in_specs=[IN_SMEM] + [IN_VMEM] * 5 + [ANY] * n_sources + [IN_VMEM] * has_acc,
        out_specs=[IN_VMEM] + [ANY] * 4,
        out_shape=[jax.ShapeDtypeStruct((rows, width), F32)] + [piece] * 4,
        scratch_shapes=[
            pltpu.VMEM((4, width, columns), BF16),
            pltpu.VMEM((4, width, columns), BF16),
            pltpu.VMEM((3, rows, columns), BF16),
            pltpu.SemaphoreType.DMA((n_copies,)),
            pltpu.SemaphoreType.DMA((2 * ranks,)),
        ],
        input_output_aliases={6 + n_sources: 0} if has_acc else {},
        compiler_params=params(),
        cost_estimate=cost(flops, 12 * rows * width + 16 * width * columns, rows * rows * 4),
    )(me, grad, normed, heads, mixed, logs, *sources, *([acc] if has_acc else []))


def mlp_kernel(places, order, orders, n_sources, has_acc, me_ref, normed_ref, grad_ref, *refs):
    sources, refs = refs[:n_sources], refs[n_sources:]
    if has_acc:
        feed_in, grad_in, refs = refs[0], refs[1], refs[2:]
    feed_ref, grad_normed_ref, refs = refs[0], refs[1], refs[2:]
    outs, refs = refs[:4], refs[4:]
    up_held, down_held, active_held, upward_held, sems = refs
    copies = start_all(
        mlp_copies(me_ref[0], sources, places, order, (up_held, down_held)), sems
    )
    hidden = up_held.shape[0]
    depth = hidden // len(order)
    step = max(depth, min(256, hidden))
    waited = 0
    for start in range(0, hidden, step):
        ready = 2 * ((start + step) // depth)
        for copy in copies[waited:ready]:
            copy.wait()
        waited = ready
        chunk = slice(start, start + step)
        upward = mm(normed_ref[...], up_held[chunk], NT)
        square = upward * upward
        bent = jnp.tanh(ROOT * upward * (1.0 + CUBE * square))
        active = (0.5 * upward * (1.0 + bent)).astype(BF16)
        slope = 0.5 * (1.0 + bent) + 0.5 * ROOT * upward * (1.0 - bent * bent) * (
            1.0 + 3.0 * CUBE * square
        )
        grad_active = mm(grad_ref[...], down_held[chunk], NT)
        grad_upward = (grad_active * slope).astype(BF16)
        active_held[:, chunk] = active
        upward_held[:, chunk] = grad_upward
        up_rows = mm(grad_upward, normed_ref[...], TN).astype(BF16)
        down_rows = mm(active, grad_ref[...], TN).astype(BF16)
        for at in range(step // depth):
            index = order[start // depth + at]
            rows = slice(at * depth, (at + 1) * depth)
            core = index & 1
            outs[core][orders[0].index(index & ~1)] = up_rows[rows]
            outs[2 + core][orders[1].index(index & ~1)] = down_rows[rows]
    feed = mm(active_held[...], down_held[...], NN)
    grad_normed = mm(upward_held[...], up_held[...], NN)
    if has_acc:
        feed = feed + feed_in[...]
        grad_normed = grad_normed + grad_in[...]
    feed_ref[...] = feed
    grad_normed_ref[...] = grad_normed


def mlp(me, normed, grad, sources, hidden, places, order, orders, acc):
    rows, width = normed.shape
    ranks = lax.axis_size("seq")
    depth = hidden // ranks
    has_acc = acc is not None
    n_sources = len(sources)
    piece = jax.ShapeDtypeStruct((ranks // 2, depth, width), BF16)
    total = jax.ShapeDtypeStruct((rows, width), F32)
    return pl.pallas_call(
        functools.partial(mlp_kernel, places, order, orders, n_sources, has_acc),
        in_specs=[IN_SMEM] + [IN_VMEM] * 2 + [ANY] * n_sources + [IN_VMEM] * (2 * has_acc),
        out_specs=[IN_VMEM] * 6,
        out_shape=[total, total] + [piece] * 4,
        scratch_shapes=[
            pltpu.VMEM((hidden, width), BF16),
            pltpu.VMEM((hidden, width), BF16),
            pltpu.VMEM((rows, hidden), BF16),
            pltpu.VMEM((rows, hidden), BF16),
            pltpu.SemaphoreType.DMA((2 * ranks,)),
        ],
        input_output_aliases={3 + n_sources: 0, 4 + n_sources: 1} if has_acc else {},
        compiler_params=params(),
        cost_estimate=cost(
            12 * rows * width * hidden, 20 * rows * width + 8 * width * hidden, rows * hidden
        ),
    )(me, normed, grad, *sources, *(acc if has_acc else []))


def place_attention_kernel(places, n_sources, me_ref, *refs):
    sources, refs = refs[:n_sources], refs[n_sources:]
    qkv_ref, out_ref, held, sems = refs
    for copy in start_all(attention_copies(me_ref[0], sources, places, held), sems):
        copy.wait()
    for c in range(3):
        qkv_ref[c] = held[c].astype(F32)
    out_ref[...] = held[3].astype(F32).T


def place_attention(me, sources, places, width):
    columns = sources[0].shape[-1]
    n_sources = len(sources)
    return pl.pallas_call(
        functools.partial(place_attention_kernel, places, n_sources),
        in_specs=[IN_SMEM] + [ANY] * n_sources,
        out_specs=[IN_VMEM] * 2,
        out_shape=[
            jax.ShapeDtypeStruct((3, width, columns), F32),
            jax.ShapeDtypeStruct((columns, width), F32),
        ],
        scratch_shapes=[
            pltpu.VMEM((4, width, columns), BF16),
            pltpu.SemaphoreType.DMA((2 * lax.axis_size("seq"),)),
        ],
        compiler_params=params(),
        cost_estimate=cost(0, 24 * width * columns),
    )(me, *sources)


def place_mlp_kernel(places, order, n_sources, me_ref, *refs):
    sources, refs = refs[:n_sources], refs[n_sources:]
    up_ref, down_ref, up_held, down_held, sems = refs
    me = me_ref[0]
    copies = mlp_copies(me, sources, places, order, (up_held, down_held))
    depth = sources[0].shape[1]
    moved = []
    for at, (source, unused) in enumerate(copies):
        start = pl.multiple_of((me ^ order[at // 2]) * depth, depth)
        moved.append((source, (up_held, down_held)[at % 2].at[pl.ds(start, depth), :]))
    for copy in start_all(moved, sems):
        copy.wait()
    up_ref[...] = up_held[...].astype(F32)
    down_ref[...] = down_held[...].astype(F32)


def place_mlp(me, sources, places, order, hidden):
    width = sources[0].shape[-1]
    n_sources = len(sources)
    whole = jax.ShapeDtypeStruct((hidden, width), F32)
    return pl.pallas_call(
        functools.partial(place_mlp_kernel, places, order, n_sources),
        in_specs=[IN_SMEM] + [ANY] * n_sources,
        out_specs=[IN_VMEM] * 2,
        out_shape=[whole, whole],
        scratch_shapes=[
            pltpu.VMEM((hidden, width), BF16),
            pltpu.VMEM((hidden, width), BF16),
            pltpu.SemaphoreType.DMA((2 * lax.axis_size("seq"),)),
        ],
        compiler_params=params(),
        cost_estimate=cost(0, 12 * hidden * width),
    )(me, *sources)


def rms_scale(values):
    return lax.rsqrt(jnp.mean(values * values, axis=-1, keepdims=True) + EPSILON)


def norm_back(grad_normed, unit_rows, scale, gain):
    scaled = gain * grad_normed
    return scale * (scaled - unit_rows * jnp.mean(unit_rows * scaled, axis=-1, keepdims=True))


def pack(first_longer, got):
    ranks, held, slots, width = got.shape
    longer = jnp.where(first_longer, got[:, 0], got[:, 1])
    shorter = jnp.where(first_longer, got[: ranks // 2, 1], got[: ranks // 2, 0])
    return jnp.concatenate(
        [longer.reshape(ranks * slots, width), shorter.reshape(ranks * slots // 2, width)]
    )


def unpack(first_longer, packed, ranks):
    rows, width = packed.shape
    half = rows // 3
    longer = packed[: 2 * half]
    shorter = jnp.concatenate([packed[2 * half :], jnp.zeros((half, width), packed.dtype)])
    both = jnp.stack(
        [
            jnp.where(first_longer, longer, shorter),
            jnp.where(first_longer, shorter, longer),
        ]
    )
    return both.reshape(1, 2, ranks, 2 * half // ranks, width)


def on_device(tokens, cotangent, lengths, routed, gain_attn, gain_mlp, router, w_qkv, w_out, w_mlp):
    group, span, width = tokens.shape
    slots = routed.shape[1]
    ranks = lax.axis_size("seq")
    depth = lax.axis_size("mp")
    held = group // ranks
    columns = w_qkv.shape[2]
    hidden = w_mlp.shape[0]
    me = lax.axis_index("seq")
    me_array = me.astype(jnp.int32)[None]
    up_bits, down_bits = bit_lists(ranks)
    places = (gather_places(ranks, up_bits), gather_places(ranks, down_bits))
    orders = (scatter_order(ranks, up_bits), scatter_order(ranks, down_bits))
    order = orders[0] + [i | 1 for i in orders[0]]

    own_attn = jnp.concatenate([w_qkv, w_out.T[None]])
    own_up, own_down = w_mlp[:, 0, :], w_mlp[:, 1, :]
    piece_attn = lax.dynamic_slice_in_dim(own_attn, me * (width // ranks), width // ranks, 1)
    piece_up = lax.dynamic_slice_in_dim(own_up, me * (hidden // ranks), hidden // ranks, 0)
    piece_down = lax.dynamic_slice_in_dim(own_down, me * (hidden // ranks), hidden // ranks, 0)
    moving = (piece_attn[:2], piece_attn[2:], piece_up, piece_down)
    attn_shards, mlp_shards = [[own_attn]], [[own_up, own_down]]
    for unused in range(1, depth):
        moving = tuple(ring(part) for part in moving)
        attn_shards.append(gather(moving[0], up_bits) + gather(moving[1], down_bits))
        mlp_shards.append(gather(moving[2], up_bits) + gather(moving[3], down_bits))

    slot = lax.broadcasted_iota(jnp.int32, routed.shape, 1)
    live = me * slots + slot < (lengths // 8)[:, None]
    place = jnp.where(live, slot * 8 + routed % 8, -1)
    chosen, chosen_grad = select_rows(place, tokens, cotangent)
    pair = lax.dynamic_slice_in_dim(lengths, me * held, held, 0)
    first_longer = pair[0] >= pair[1]

    def to_holder(value):
        return lax.all_to_all(
            value.reshape(ranks, held, slots, width), "seq", split_axis=0, concat_axis=0, tiled=True
        )

    def to_position(value):
        back = lax.all_to_all(
            unpack(first_longer, value, ranks), "seq", split_axis=2, concat_axis=0, tiled=True
        )
        return back.reshape(group, slots, width)

    picked = pack(first_longer, to_holder(chosen)).astype(F32)
    grad_rows = pack(first_longer, to_holder(chosen_grad)).astype(F32)

    scale_one = rms_scale(picked)
    unit_one = picked * scale_one
    normed_one = (unit_one * gain_attn).astype(BF16)
    gate = jax.nn.sigmoid(jnp.sum(picked * router, axis=-1, keepdims=True))
    grad_feed = (gate * grad_rows).astype(BF16)
    attended, saved = None, []
    for shard in attn_shards:
        attended, *rest = attention_forward(me_array, normed_one, shard, places, attended)
        saved.append(rest)
    middle = picked + attended
    scale_two = rms_scale(middle)
    unit_two = middle * scale_two
    normed_two = (unit_two * gain_mlp).astype(BF16)

    feed_sums, mlp_grads = None, []
    for shard in mlp_shards:
        feed, grad_normed_two, *rest = mlp(
            me_array, normed_two, grad_feed, shard, hidden, places, order, orders, feed_sums
        )
        feed_sums = (feed, grad_normed_two)
        mlp_grads.append(
            (scatter(rest[0], rest[1], up_bits), scatter(rest[2], rest[3], down_bits))
        )
    feed, grad_normed_two = feed_sums
    delta = attended + feed
    layer_out = add_rows(place, tokens, to_position((gate * delta).astype(BF16)))

    grad_logit = jnp.sum(grad_rows * delta, axis=-1, keepdims=True) * gate * (1.0 - gate)
    router_part = jnp.sum(grad_logit * picked, axis=0)
    grad_middle = norm_back(grad_normed_two, unit_two, scale_two, gain_mlp)
    mlp_gain_part = jnp.sum(grad_normed_two * unit_two, axis=0)
    grad_attended = (gate * grad_rows + grad_middle).astype(BF16)

    grad_normed_one, attn_grads = None, [None] * depth
    for k in list(range(1, depth)) + [0]:
        grad_normed_one, *rest = attention_backward(
            me_array,
            grad_attended,
            normed_one,
            *saved[k],
            attn_shards[k],
            places,
            orders,
            grad_normed_one,
        )
        attn_grads[k] = (
            scatter(rest[0], rest[1], up_bits),
            scatter(rest[2], rest[3], down_bits),
        )
    attn_gain_part = jnp.sum(grad_normed_one * unit_one, axis=0)
    grad_picked = (
        grad_middle
        + norm_back(grad_normed_one, unit_one, scale_one, gain_attn)
        + grad_logit * router
    ).astype(BF16)
    grad_tokens = add_rows(place, cotangent, to_position(grad_picked))

    def collect(parts):
        totals = parts[1 % depth]
        for k in list(range(2, depth)) + [0]:
            if depth > 1:
                totals = tuple(added(ring(t), p) for t, p in zip(totals, parts[k]))
        return gather(totals[0], up_bits) + gather(totals[1], down_bits)

    grad_up, grad_down = place_mlp(me_array, collect(mlp_grads), places, order, hidden)
    grad_qkv, grad_out = place_attention(me_array, collect(attn_grads), places, width)
    grad_mlp = jnp.stack([grad_up, grad_down], axis=1)
    small = sum_everywhere(jnp.stack([attn_gain_part, mlp_gain_part, router_part]))
    return (
        layer_out,
        grad_tokens,
        small[0],
        small[1],
        small[2],
        grad_qkv,
        grad_out,
        grad_mlp,
    )


def solution(mesh):
    placed = (
        P("mp", "seq", None),
        P("mp", "seq", None),
        P("mp"),
        P("mp", "seq"),
        P(),
        P(),
        P(),
        P(None, None, "mp"),
        P("mp", None),
        P("mp", None, None),
    )
    return jax.shard_map(
        on_device,
        mesh=mesh,
        in_specs=placed,
        out_specs=(
            P("mp", "seq", None),
            P("mp", "seq", None),
            P(),
            P(),
            P(),
            P(None, None, "mp"),
            P("mp", None),
            P("mp", None, None),
        ),
        check_vma=False,
    )
```

```python
import functools

import jax
import jax.numpy as jnp
from jax import lax
from jax.experimental import pallas as pl
from jax.experimental.pallas import tpu as pltpu
from jax.sharding import PartitionSpec as P

HEAD = 64
LANES = 128
EPSILON = 1e-06
NEGATIVE = -1e30
ROOT = 0.7978845608028654
CUBE = 0.044715
SCALE = HEAD**-0.5
F32 = jnp.float32
BF16 = jnp.bfloat16
VMEM_BYTES = 36 * 1024 * 1024

NN = (((1,), (0,)), ((), ()))
NT = (((1,), (1,)), ((), ()))
TN = (((0,), (0,)), ((), ()))

IN_HBM = pl.BlockSpec(memory_space=pltpu.HBM)
IN_VMEM = pl.BlockSpec(memory_space=pltpu.VMEM)
IN_SMEM = pl.BlockSpec(memory_space=pltpu.SMEM)


def mm(left, right, dims):
    return lax.dot_general(left, right, dims, preferred_element_type=F32)


def cost(flops, bytes_accessed, transcendentals=0):
    return pl.CostEstimate(
        flops=int(flops), bytes_accessed=int(bytes_accessed), transcendentals=int(transcendentals)
    )


def params(semantics=None):
    return pltpu.CompilerParams(dimension_semantics=semantics, vmem_limit_bytes=VMEM_BYTES)


def combos(bits):
    found = [0]
    for bit in bits:
        found = [i | extra for i in found for extra in (0, 1 << bit)]
    return found


def exchange_plan(chips, shared):
    bits = list(range(chips.bit_length() - 1))
    if not shared:
        return ((bits, []), (bits[::-1], []))
    cut = len(bits) // 2
    return ((bits[:cut], bits[cut:]), (bits[cut:], bits[:cut]))


def exchange(value, offset):
    ranks = lax.axis_size("seq")
    return lax.ppermute(value, "seq", [(i, i ^ offset) for i in range(ranks)])


def across(value, bit):
    return exchange(value, 2 << bit)


def other_core(value):
    return exchange(value, 1)


def ring(value):
    depth = lax.axis_size("mp")
    cycle = [0] + list(range(1, depth, 2)) + list(range(2, depth, 2))[::-1]
    pairs = [(cycle[i], cycle[(i + 1) % depth]) for i in range(depth)]
    return lax.ppermute(value, "mp", pairs)


def joined(arrays):
    return arrays[0] if len(arrays) == 1 else jnp.concatenate(arrays, axis=0)


def gather_places(plan):
    bits, kept = plan
    held = [combos(kept)]
    for bit in bits:
        flat = [i for part in held for i in part]
        held = [flat, [i | (1 << bit) for i in flat]]
    return held


def scatter_order(plan):
    return combos(plan[0] + plan[1])


def added(left, right):
    return (left.astype(F32) + right.astype(F32)).astype(BF16)


def swapped(value, at, count):
    shape = value.shape
    parts = value.reshape((2**at, 2, 2 ** (count - at - 1)) + shape[1:])
    return jnp.concatenate([parts[:, 1:], parts[:, :1]], axis=1).reshape(shape)


class Pipe:
    def __init__(self):
        self.slot = 0
        self.flights = []

    def launch(self, chain):
        self.advance(chain, None)

    def advance(self, chain, got):
        try:
            arrays, slots = chain.send(got)
        except StopIteration:
            return
        self.flights.append((chain, arrays, self.slot + slots))

    def step(self, outs):
        self.slot += 1
        due = [f for f in self.flights if f[2] <= self.slot]
        self.flights = [f for f in self.flights if f[2] > self.slot]
        outs, got = lax.optimization_barrier((outs, [f[1] for f in due]))
        for flight, arrays in zip(due, got):
            self.advance(flight[0], arrays)
        return outs

    def drain(self):
        while self.flights:
            due, self.flights = self.flights, []
            self.slot = max(self.slot, min(f[2] for f in due))
            for flight in due:
                self.advance(flight[0], flight[1])


def gather_chain(pieces, plans, done):
    held = [[part] for part in pieces]
    for at in range(max(len(plan[0]) for plan in plans)):
        whole = [joined(parts) for parts in held]
        got = yield [across(w, plan[0][at]) for w, plan in zip(whole, plans)], 1
        held = [[w, g] for w, g in zip(whole, got)]
    done(held[0] + held[1])


def weights_chain(pipe, pieces, split, plans, count, done):
    for k in range(1, count):
        pieces = yield [ring(part) for part in pieces], 1
        pipe.launch(gather_chain(split(pieces), plans, functools.partial(done, k)))


def scatter_chain(parts, plans, done):
    lows, highs = parts[::2], parts[1::2]
    steps = max(len(plan[0]) for plan in plans)
    for at in range(steps):
        got = yield [across(part, plan[0][at]) for part, plan in zip(highs, plans)], 1
        if at + 1 < steps:
            half = lows[0].shape[0] // 2
            highs = [added(t[half:], g[half:]) for t, g in zip(lows, got)]
            lows = [added(t[:half], g[:half]) for t, g in zip(lows, got)]
        else:
            lows = [added(t, g) for t, g in zip(lows, got)]
    done(lows)


class Collect:
    def __init__(self, pipe, count, plans, done):
        self.pipe, self.count, self.plans, self.done = pipe, count, plans, done
        self.parts, self.next, self.sums, self.busy = {}, 1 % count, None, False

    def ready(self, k, totals):
        self.parts[k] = totals
        self.go()

    def go(self):
        if self.busy or self.next is None or self.next not in self.parts:
            return
        part = joined(self.parts[self.next])
        self.sums = part if self.sums is None else added(self.sums, part)
        if self.next == 0:
            self.next = None
            half = self.sums.shape[0] // 2
            self.pipe.launch(self.spread([self.sums[:half], self.sums[half:]]))
            return
        self.next = (self.next + 1) % self.count
        self.busy = True
        self.pipe.launch(self.hop())

    def hop(self):
        (self.sums,) = yield [ring(self.sums)], 1
        self.busy = False
        self.go()

    def spread(self, totals):
        counts = [len(plan[1]) for plan in self.plans]
        for at in range(max(counts)):
            got = yield [across(t, plan[1][at]) for t, plan in zip(totals, self.plans)], 1
            totals = [added(t, swapped(g, at, n)) for t, g, n in zip(totals, got, counts)]
        self.pipe.launch(gather_chain(totals, self.plans, self.cores))

    def cores(self, held):
        def chain():
            got = yield [other_core(part) for part in held], 1
            self.done(held + got)

        self.pipe.launch(chain())


def sum_everywhere(value):
    for axis in ("seq", "mp"):
        size = lax.axis_size(axis)
        step = 1
        while step < size:
            value = value + lax.ppermute(value, axis, [(i, i ^ step) for i in range(size)])
            step *= 2
    return value


def select_kernel(place_ref, base_ref, out_ref):
    span = base_ref.shape[1]
    for at in range(base_ref.shape[0]):
        place = place_ref[at]
        hot = lax.broadcasted_iota(jnp.int32, (place.shape[0], span), 1) == place
        out_ref[at] = mm(hot.astype(BF16), base_ref[at], NN).astype(BF16)


def together(group, span):
    size = max(1, min(group, 1024 // span))
    while group % size:
        size -= 1
    return size


def select_rows(place, base):
    group, span, width = base.shape
    slots = place.shape[1]
    size = together(group, span)
    return pl.pallas_call(
        select_kernel,
        grid=(group // size,),
        in_specs=[
            pl.BlockSpec((size, slots, 1), lambda g: (g, 0, 0)),
            pl.BlockSpec((size, span, width), lambda g: (g, 0, 0)),
        ],
        out_specs=pl.BlockSpec((size, slots, width), lambda g: (g, 0, 0)),
        out_shape=jax.ShapeDtypeStruct((group, slots, width), BF16),
        compiler_params=params(("arbitrary",)),
        cost_estimate=cost(2 * group * slots * span * width, 2 * group * (span + slots) * width),
    )(place[:, :, None], base)


def add_kernel(place_ref, base_ref, rows_ref, out_ref):
    span = base_ref.shape[1]
    for at in range(base_ref.shape[0]):
        place = place_ref[at]
        hot = lax.broadcasted_iota(jnp.int32, (span, place.shape[1]), 0) == place
        moved = mm(hot.astype(BF16), rows_ref[at], NN)
        out_ref[at] = (base_ref[at].astype(F32) + moved).astype(BF16)


def add_rows(place, base, rows):
    group, span, width = base.shape
    slots = place.shape[1]
    size = together(group, span)
    block = pl.BlockSpec((size, span, width), lambda g: (g, 0, 0))
    return pl.pallas_call(
        add_kernel,
        grid=(group // size,),
        in_specs=[
            pl.BlockSpec((size, 1, slots), lambda g: (g, 0, 0)),
            block,
            pl.BlockSpec((size, slots, width), lambda g: (g, 0, 0)),
        ],
        out_specs=block,
        out_shape=jax.ShapeDtypeStruct(base.shape, BF16),
        compiler_params=params(("arbitrary",)),
        cost_estimate=cost(2 * group * slots * span * width, 4 * group * span * width),
    )(place[:, None, :], base, rows)


def start_all(copies, sems):
    started = []
    for at, (source, target) in enumerate(copies):
        copy = pltpu.make_async_copy(source, target, sems.at[at])
        copy.start()
        started.append(copy)
    return started


def attention_copies(chip, sources, places, target):
    if len(sources) == 1:
        return [(sources[0], target)]
    half = len(sources) // 2
    depth = sources[0].shape[2]
    copies = []
    for side in range(2):
        for source, ids in zip(sources[side * half : (side + 1) * half], places[side]):
            for at, index in enumerate(ids):
                start = pl.multiple_of((chip ^ index) * depth, depth)
                copies.append(
                    (
                        source.at[at],
                        target.at[pl.ds(2 * side, 2), pl.ds(start, depth), :],
                    )
                )
    return copies


def mlp_copies(chip, sources, places, order, targets):
    half = len(sources) // 2
    copies = []
    for place, index in enumerate(order):
        for side in range(2):
            target = targets[side]
            if half == 1:
                depth = target.shape[0] // len(order)
                start = pl.multiple_of((chip ^ index) * depth, depth)
                source = sources[side].at[pl.ds(start, depth), :]
            else:
                for array, ids in zip(sources[side * half : (side + 1) * half], places[side]):
                    if index in ids:
                        source = array.at[ids.index(index)]
                        depth = array.shape[1]
            copies.append((source, target.at[pl.ds(place * depth, depth), :]))
    return copies


def row_blocks(rows):
    blocks = []
    for start in (0, rows // 2):
        half = rows // 6
        for first, last, low, high in ((0, 1, 0, 1), (1, 2, 0, 2), (2, 3, 2, 3)):
            blocks.append(tuple(start + half * at for at in (first, last, low, high)))
    return blocks


def causal(first, last, low, high):
    shape = (last - first, high - low)
    row = lax.broadcasted_iota(jnp.int32, shape, 0) + (first - low)
    return row >= lax.broadcasted_iota(jnp.int32, shape, 1)


def head_groups(columns):
    lanes = min(LANES, columns)
    return [
        (slice(at, at + lanes), at // HEAD, lanes // HEAD) for at in range(0, columns, lanes)
    ]


def own_lanes(value, side, heads):
    if heads == 1:
        return value
    lane = lax.broadcasted_iota(jnp.int32, (1, value.shape[1]), 1)
    mine = (lane >= HEAD) if side else (lane < HEAD)
    return jnp.where(mine, value, jnp.zeros_like(value))


def finish(total, last, outs):
    if not last:
        outs[0][...] = total
        return
    half = total.shape[0] // 2
    outs[0][...] = total[:half]
    outs[1][...] = total[half:].astype(BF16)


def sum_shapes(rows, width, last):
    if not last:
        return [jax.ShapeDtypeStruct((rows, width), F32)]
    return [
        jax.ShapeDtypeStruct((rows // 2, width), F32),
        jax.ShapeDtypeStruct((rows // 2, width), BF16),
    ]


def attention_forward_kernel(places, n_sources, has_acc, last, chip_ref, normed_ref, *refs):
    sources, refs = refs[:n_sources], refs[n_sources:]
    if has_acc:
        acc_ref, refs = refs[0], refs[1:]
    sums, refs = refs[: 1 + last], refs[1 + last :]
    heads_ref, mixed_ref, log_ref, held, sems = refs
    for copy in start_all(attention_copies(chip_ref[0], sources, places, held), sems):
        copy.wait()
    rows = normed_ref.shape[0]
    for c in range(3):
        heads_ref[c] = mm(normed_ref[...], held[c], NN).astype(BF16)
    lane = lax.broadcasted_iota(jnp.int32, (1, LANES), 1)
    for first, end, low, high in row_blocks(rows):
        seen = causal(first, end, low, high)
        logs = jnp.zeros((end - first, LANES), F32)
        for lanes, head, heads in head_groups(held.shape[2]):
            query = heads_ref[0, first:end, lanes]
            keys = heads_ref[1, low:high, lanes]
            values = heads_ref[2, low:high, lanes]
            out = None
            for side in range(heads):
                scores = mm(own_lanes(query, side, heads), keys, NT) * SCALE
                scores = jnp.where(seen, scores, NEGATIVE)
                peak = jnp.max(scores, axis=-1, keepdims=True)
                raised = jnp.exp(scores - peak)
                total = jnp.sum(raised, axis=-1, keepdims=True)
                weights = (raised * (1.0 / total)).astype(BF16)
                part = own_lanes(mm(weights, values, NN), side, heads)
                out = part if out is None else out + part
                logs = jnp.where(lane == head + side, peak + jnp.log(total), logs)
            mixed_ref[first:end, lanes] = out.astype(BF16)
        log_ref[first:end, :] = logs
    attended = mm(mixed_ref[...], held[3], NT)
    if has_acc:
        attended = attended + acc_ref[...]
    finish(attended, last, sums)


def attention_forward(chip, normed, sources, places, acc, last):
    rows, width = normed.shape
    columns = sources[0].shape[-1]
    has_acc = acc is not None
    n_sources = len(sources)
    n_copies = 1 if n_sources == 1 else lax.axis_size("seq")
    flops = 2 * rows * width * columns * 4 + rows * rows * columns
    return pl.pallas_call(
        functools.partial(attention_forward_kernel, places, n_sources, has_acc, last),
        in_specs=[IN_SMEM, IN_VMEM] + [IN_HBM] * n_sources + [IN_VMEM] * has_acc,
        out_specs=[IN_VMEM] * (4 + last),
        out_shape=sum_shapes(rows, width, last)
        + [
            jax.ShapeDtypeStruct((3, rows, columns), BF16),
            jax.ShapeDtypeStruct((rows, columns), BF16),
            jax.ShapeDtypeStruct((rows, LANES), F32),
        ],
        scratch_shapes=[
            pltpu.VMEM((4, width, columns), BF16),
            pltpu.SemaphoreType.DMA((n_copies,)),
        ],
        input_output_aliases={2 + n_sources: 0} if has_acc and not last else {},
        compiler_params=params(),
        cost_estimate=cost(flops, 8 * rows * width + 8 * width * columns, rows * rows * 2),
    )(chip, normed, *sources, *([acc] if has_acc else []))


def attention_backward_kernel(
    places,
    orders,
    n_sources,
    has_acc,
    last,
    chip_ref,
    grad_ref,
    normed_ref,
    heads_ref,
    mixed_ref,
    log_ref,
    *refs,
):
    sources, refs = refs[:n_sources], refs[n_sources:]
    if has_acc:
        acc_ref, refs = refs[0], refs[1:]
    sums, refs = refs[: 1 + last], refs[1 + last :]
    outs, refs = refs[:4], refs[4:]
    held, grad_held, grad_heads, sems, out_sems = refs
    chip = chip_ref[0]
    copies = start_all(attention_copies(chip, sources, places, held), sems)
    rows = normed_ref.shape[0]
    width = held.shape[2]
    depth = outs[0].shape[2]
    grad_held[3] = mm(grad_ref[...], mixed_ref[...], TN).astype(BF16)
    for copy in copies:
        copy.wait()
    grad_mixed = mm(grad_ref[...], held[3], NN).astype(BF16)
    lane = lax.broadcasted_iota(jnp.int32, (1, LANES), 1)
    for lanes, head, heads in head_groups(width):
        key_parts, value_parts = [], []
        for first, end, low, high in row_blocks(rows):
            query = heads_ref[0, first:end, lanes]
            keys = heads_ref[1, low:high, lanes]
            values = heads_ref[2, low:high, lanes]
            grad_out = grad_mixed[first:end, lanes]
            logs = log_ref[first:end, :]
            seen = causal(first, end, low, high)
            grad_query = grad_keys = grad_values = None
            for side in range(heads):
                own_query = own_lanes(query, side, heads)
                own_grad = own_lanes(grad_out, side, heads)
                log_total = jnp.sum(
                    jnp.where(lane == head + side, logs, 0.0), axis=-1, keepdims=True
                )
                scores = jnp.where(seen, mm(own_query, keys, NT) * SCALE, NEGATIVE)
                shares = jnp.exp(scores - log_total)
                grad_weights = mm(own_grad, values, NT)
                inner = jnp.sum(shares * grad_weights, axis=-1, keepdims=True)
                grad_scores = (shares * (grad_weights - inner)).astype(BF16)
                weights = shares.astype(BF16)
                part_query = own_lanes(mm(grad_scores, keys, NN), side, heads)
                part_keys = mm(grad_scores, own_query, TN)
                part_values = mm(weights, own_grad, TN)
                if side == 0:
                    grad_query, grad_keys, grad_values = part_query, part_keys, part_values
                else:
                    grad_query = grad_query + part_query
                    grad_keys = grad_keys + part_keys
                    grad_values = grad_values + part_values
            grad_heads[0, first:end, lanes] = (grad_query * SCALE).astype(BF16)
            key_parts.append(grad_keys)
            value_parts.append(grad_values)
        half = rows // 6
        for c, parts, scale in ((1, key_parts, SCALE), (2, value_parts, 1.0)):
            for pair in range(2):
                one, two, three = parts[3 * pair : 3 * pair + 3]
                for at, value in enumerate((one + two[:half], two[half:], three)):
                    start = (3 * pair + at) * half
                    grad_heads[c, start : start + half, lanes] = (value * scale).astype(BF16)
    copies = []
    for side, pieces in ((1, (2, 3)), (0, (0, 1))):
        for c in pieces:
            if c < 3:
                grad_held[c] = mm(normed_ref[...], grad_heads[c], TN).astype(BF16)
        for at, index in enumerate(orders[side]):
            start = pl.multiple_of((chip ^ index) * depth, depth)
            high, at = divmod(at, len(orders[side]) // 2)
            copy = pltpu.make_async_copy(
                grad_held.at[pl.ds(2 * side, 2), pl.ds(start, depth), :],
                outs[2 * side + high].at[at],
                out_sems.at[len(copies)],
            )
            copy.start()
            copies.append(copy)
    grad_normed = mm(grad_heads[0], held[0], NT)
    for c in range(1, 3):
        grad_normed = grad_normed + mm(grad_heads[c], held[c], NT)
    if has_acc:
        grad_normed = grad_normed + acc_ref[...]
    finish(grad_normed, last, sums)
    for copy in copies:
        copy.wait()


def attention_backward(chip, grad, normed, saved, sources, places, orders, acc, last):
    rows, width = normed.shape
    columns = sources[0].shape[-1]
    chips = lax.axis_size("seq") // 2
    has_acc = acc is not None
    n_sources = len(sources)
    n_copies = 1 if n_sources == 1 else 2 * chips
    piece = jax.ShapeDtypeStruct((chips // 2, 2, width // chips, columns), BF16)
    flops = 2 * rows * width * columns * 8 + 3 * rows * rows * columns
    return pl.pallas_call(
        functools.partial(
            attention_backward_kernel, places, orders, n_sources, has_acc, last
        ),
        in_specs=[IN_SMEM] + [IN_VMEM] * 5 + [IN_HBM] * n_sources + [IN_VMEM] * has_acc,
        out_specs=[IN_VMEM] * (1 + last) + [IN_HBM] * 4,
        out_shape=sum_shapes(rows, width, last) + [piece] * 4,
        scratch_shapes=[
            pltpu.VMEM((4, width, columns), BF16),
            pltpu.VMEM((4, width, columns), BF16),
            pltpu.VMEM((3, rows, columns), BF16),
            pltpu.SemaphoreType.DMA((n_copies,)),
            pltpu.SemaphoreType.DMA((2 * chips,)),
        ],
        input_output_aliases={6 + n_sources: 0} if has_acc and not last else {},
        compiler_params=params(),
        cost_estimate=cost(flops, 12 * rows * width + 16 * width * columns, rows * rows * 2),
    )(chip, grad, normed, *saved, *sources, *([acc] if has_acc else []))


def mlp_kernel(places, order, orders, n_sources, has_acc, last, chip_ref, normed_ref, grad_ref, *refs):
    sources, refs = refs[:n_sources], refs[n_sources:]
    if has_acc:
        acc_in, refs = refs[:2], refs[2:]
    sums, refs = refs[: 2 + 2 * last], refs[2 + 2 * last :]
    outs, refs = refs[:4], refs[4:]
    up_held, down_held, up_grad, down_grad, active_held, upward_held, sems, out_sems = refs
    copies = start_all(mlp_copies(chip_ref[0], sources, places, order, (up_held, down_held)), sems)
    hidden = up_held.shape[0]
    depth = hidden // len(order)
    step = max(depth, min(256, hidden))
    waited = 0
    leaving = []
    for start in range(0, hidden, step):
        ready = 2 * ((start + step) // depth)
        for copy in copies[waited:ready]:
            copy.wait()
        waited = ready
        chunk = slice(start, start + step)
        upward = mm(normed_ref[...], up_held[chunk], NT)
        square = upward * upward
        bent = jnp.tanh(ROOT * upward * (1.0 + CUBE * square))
        active = (0.5 * upward * (1.0 + bent)).astype(BF16)
        slope = 0.5 * (1.0 + bent) + 0.5 * ROOT * upward * (1.0 - bent * bent) * (
            1.0 + 3.0 * CUBE * square
        )
        grad_active = mm(grad_ref[...], down_held[chunk], NT)
        grad_upward = (grad_active * slope).astype(BF16)
        active_held[:, chunk] = active
        upward_held[:, chunk] = grad_upward
        up_grad[chunk] = mm(grad_upward, normed_ref[...], TN).astype(BF16)
        down_grad[chunk] = mm(active, grad_ref[...], TN).astype(BF16)
        for at in range(start // depth, (start + step) // depth):
            for side, grads in enumerate((up_grad, down_grad)):
                place = orders[side].index(order[at])
                high, place = divmod(place, len(order) // 2)
                copy = pltpu.make_async_copy(
                    grads.at[pl.ds(at * depth, depth), :],
                    outs[2 * side + high].at[place],
                    out_sems.at[2 * at + side],
                )
                copy.start()
                leaving.append(copy)
    for i, (left, right) in enumerate(((active_held, down_held), (upward_held, up_held))):
        total = mm(left[...], right[...], NN)
        if has_acc:
            total = total + acc_in[i][...]
        finish(total, last, sums[i * (1 + last) : (i + 1) * (1 + last)])
    for copy in leaving:
        copy.wait()


def mlp(chip, normed, grad, sources, hidden, places, order, orders, acc, last):
    rows, width = normed.shape
    chips = len(order)
    depth = hidden // chips
    has_acc = acc is not None
    n_sources = len(sources)
    piece = jax.ShapeDtypeStruct((chips // 2, depth, width), BF16)
    aliased = {3 + n_sources: 0, 4 + n_sources: 1} if has_acc and not last else {}
    return pl.pallas_call(
        functools.partial(mlp_kernel, places, order, orders, n_sources, has_acc, last),
        in_specs=[IN_SMEM] + [IN_VMEM] * 2 + [IN_HBM] * n_sources + [IN_VMEM] * (2 * has_acc),
        out_specs=[IN_VMEM] * (2 + 2 * last) + [IN_HBM] * 4,
        out_shape=sum_shapes(rows, width, last) * 2 + [piece] * 4,
        scratch_shapes=[pltpu.VMEM((hidden, width), BF16)] * 4
        + [pltpu.VMEM((rows, hidden), BF16)] * 2
        + [
            pltpu.SemaphoreType.DMA((2 * chips,)),
            pltpu.SemaphoreType.DMA((2 * chips,)),
        ],
        input_output_aliases=aliased,
        compiler_params=params(),
        cost_estimate=cost(
            12 * rows * width * hidden, 20 * rows * width + 8 * width * hidden, rows * hidden
        ),
    )(chip, normed, grad, *sources, *(acc if has_acc else []))


def place_attention_kernel(places, n_sources, chip_ref, core_ref, *refs):
    sources, refs = refs[:n_sources], refs[n_sources:]
    qkv_ref, out_ref, held, sems = refs
    half = n_sources // 2
    copies = []
    for which, core in enumerate((core_ref[0], 1 - core_ref[0])):
        copies += attention_copies(
            chip_ref[0], sources[which * half : (which + 1) * half], places, held.at[core]
        )
    for copy in start_all(copies, sems):
        copy.wait()
    columns = held.shape[3]
    for c in range(3):
        qkv_ref[c] = jnp.concatenate([held[0, c], held[1, c]], axis=-1).astype(F32)
    for core in range(2):
        out_ref[core * columns : (core + 1) * columns, :] = held[core, 3].astype(F32).T


def place_attention(chip, core, sources, places, width):
    columns = sources[0].shape[-1]
    n_sources = len(sources)
    return pl.pallas_call(
        functools.partial(place_attention_kernel, places, n_sources),
        in_specs=[IN_SMEM, IN_SMEM] + [IN_HBM] * n_sources,
        out_specs=[IN_VMEM] * 2,
        out_shape=[
            jax.ShapeDtypeStruct((3, width, 2 * columns), F32),
            jax.ShapeDtypeStruct((2 * columns, width), F32),
        ],
        scratch_shapes=[
            pltpu.VMEM((2, 4, width, columns), BF16),
            pltpu.SemaphoreType.DMA((2 * lax.axis_size("seq"),)),
        ],
        compiler_params=params(),
        cost_estimate=cost(0, 48 * width * columns),
    )(chip, core, *sources)


def place_mlp_kernel(places, order, n_sources, chip_ref, core_ref, *refs):
    sources, refs = refs[:n_sources], refs[n_sources:]
    out_ref, up_held, down_held, out_held, sems, out_sems = refs
    chip, core = chip_ref[0], core_ref[0]
    hidden, width = up_held.shape[1:]
    half = n_sources // 2
    copies = []
    for which in range(2):
        targets = (up_held.at[which], down_held.at[which])
        copies += mlp_copies(
            chip, sources[which * half : (which + 1) * half], places, order, targets
        )
    copies = start_all(copies, sems)
    depth = hidden // len(order)
    tiles = width // LANES
    size = depth * 2 * tiles
    moved = []
    for which in range(2):
        for at, index in enumerate(order):
            base = len(moved)
            for side, part in enumerate((up_held, down_held)):
                copies[2 * base + side].wait()
                rows = part[which, at * depth : (at + 1) * depth, :].astype(F32)
                for tile in range(tiles):
                    out_held[pl.ds(base * size + 2 * tile + side, depth, stride=2 * tiles), :] = (
                        rows[:, tile * LANES : (tile + 1) * LANES]
                    )
            block = ((core if which == 0 else 1 - core) * len(order) + (chip ^ index)) * size
            copy = pltpu.make_async_copy(
                out_held.at[pl.ds(base * size, size), :],
                out_ref.at[pl.ds(pl.multiple_of(block, size), size), :],
                out_sems.at[base],
            )
            copy.start()
            moved.append(copy)
    for copy in moved:
        copy.wait()


def place_mlp(chip, core, sources, places, order, hidden):
    width = sources[0].shape[-1]
    n_sources = len(sources)
    tiles = width // LANES
    chips = len(order)
    rows = pl.pallas_call(
        functools.partial(place_mlp_kernel, places, order, n_sources),
        in_specs=[IN_SMEM, IN_SMEM] + [IN_HBM] * n_sources,
        out_specs=IN_HBM,
        out_shape=jax.ShapeDtypeStruct((hidden * 2 * tiles, LANES), F32),
        scratch_shapes=[
            pltpu.VMEM((2, hidden // 2, width), BF16),
            pltpu.VMEM((2, hidden // 2, width), BF16),
            pltpu.VMEM((hidden * 2 * tiles, LANES), F32),
            pltpu.SemaphoreType.DMA((4 * chips,)),
            pltpu.SemaphoreType.DMA((2 * chips,)),
        ],
        compiler_params=params(),
        cost_estimate=cost(0, 12 * hidden * width),
    )(chip, core, *sources)
    shaped = rows.reshape(hidden, tiles, 2, LANES)
    return shaped.transpose(0, 2, 1, 3).reshape(hidden, 2, width)


def rms_scale(values):
    return lax.rsqrt(jnp.mean(values * values, axis=-1, keepdims=True) + EPSILON)


def norm_back(grad_normed, unit_rows, scale, gain):
    scaled = gain * grad_normed
    return scale * (scaled - unit_rows * jnp.mean(unit_rows * scaled, axis=-1, keepdims=True))


def pack(first_longer, got):
    ranks, held, slots, width = got.shape
    longer = jnp.where(first_longer, got[:, 0], got[:, 1])
    shorter = jnp.where(first_longer, got[: ranks // 2, 1], got[: ranks // 2, 0])
    return jnp.concatenate(
        [longer.reshape(ranks * slots, width), shorter.reshape(ranks * slots // 2, width)]
    )


def unpack(first_longer, packed, ranks):
    rows, width = packed.shape
    half = rows // 3
    longer = packed[: 2 * half]
    shorter = jnp.concatenate([packed[2 * half :], jnp.zeros((half, width), packed.dtype)])
    both = jnp.stack(
        [
            jnp.where(first_longer, longer, shorter),
            jnp.where(first_longer, shorter, longer),
        ]
    )
    return both.reshape(1, 2, ranks, 2 * half // ranks, width)


def on_device(tokens, cotangent, lengths, routed, gain_attn, gain_mlp, router, w_qkv, w_out, w_mlp):
    group, span, width = tokens.shape
    slots = routed.shape[1]
    ranks = lax.axis_size("seq")
    count = lax.axis_size("mp")
    held = group // ranks
    chips = ranks // 2
    columns = w_qkv.shape[2] // 2
    hidden = w_mlp.shape[0] // 2
    me = lax.axis_index("seq").astype(jnp.int32)
    chip, core = me // 2, me % 2
    chip_array, core_array = chip[None], core[None]
    whole_plans, shared_plans = exchange_plan(chips, False), exchange_plan(chips, True)
    places = [gather_places(plan) for plan in whole_plans]
    orders = [scatter_order(plan) for plan in whole_plans]
    shared_places = [gather_places(plan) for plan in shared_plans]
    shared_orders = [scatter_order(plan) for plan in shared_plans]
    order = orders[0]
    pipe = Pipe()

    attn_shards, mlp_shards = {}, {}
    own_attn = jnp.concatenate([w_qkv, w_out.T[None]])
    own_attn = lax.dynamic_slice_in_dim(own_attn, core * columns, columns, 2)
    piece = lax.dynamic_slice_in_dim(own_attn, chip * (width // chips), width // chips, 1)
    attn_shards[0] = [own_attn]
    pipe.launch(
        weights_chain(
            pipe,
            [piece[None]],
            lambda parts: [parts[0][:, :2], parts[0][:, 2:]],
            whole_plans,
            count,
            attn_shards.__setitem__,
        )
    )

    slot = lax.broadcasted_iota(jnp.int32, routed.shape, 1)
    live = me * slots + slot < (lengths // 8)[:, None]
    place = jnp.where(live, slot * 8 + routed % 8, -1)
    pair = lax.dynamic_slice_in_dim(lengths, me * held, held, 0)
    first_longer = pair[0] >= pair[1]
    rows = {}

    def to_holder(value, name):
        value = value.reshape(ranks, held, slots, width)
        got = yield [lax.all_to_all(value, "seq", split_axis=0, concat_axis=0, tiled=True)], 1
        rows[name] = pack(first_longer, got[0]).astype(F32)

    def to_position(value, name):
        value = unpack(first_longer, value, ranks)
        got = yield [lax.all_to_all(value, "seq", split_axis=2, concat_axis=0, tiled=True)], 1
        rows[name] = got[0].reshape(group, slots, width)

    def both_cores(value):
        return jnp.concatenate([value, other_core(value)])

    chosen, cotangent = pipe.step((select_rows(place, tokens), cotangent))
    pipe.launch(to_holder(chosen, "picked"))
    chosen_grad, w_mlp = pipe.step((select_rows(place, cotangent), w_mlp))

    picked = rows["picked"]
    scale_one = rms_scale(picked)
    unit_one = picked * scale_one
    normed_one = both_cores((unit_one * gain_attn).astype(BF16))
    gate = jax.nn.sigmoid(jnp.sum(picked * router, axis=-1, keepdims=True))
    own_mlp = lax.dynamic_slice_in_dim(w_mlp, core * hidden, hidden, 0)
    own_up, own_down = own_mlp[:, 0, :], own_mlp[:, 1, :]
    piece = jnp.stack(
        [
            lax.dynamic_slice_in_dim(part, chip * (hidden // chips), hidden // chips, 0)
            for part in (own_up, own_down)
        ]
    )
    mlp_shards[0] = [own_up, own_down]
    attended, saved = None, []
    for k in range(count):
        while k not in attn_shards:
            normed_one = pipe.step(normed_one)
        out = attention_forward(
            chip_array, normed_one, attn_shards[k], places, attended, k == count - 1
        )
        if k == 0:
            out, piece = pipe.step((out, piece))
            pipe.launch(
                weights_chain(
                    pipe,
                    [piece],
                    lambda parts: [parts[0][:1], parts[0][1:]],
                    whole_plans,
                    count,
                    mlp_shards.__setitem__,
                )
            )
        else:
            out = pipe.step(out)
        if k == max(0, count - 2):
            pipe.launch(to_holder(chosen_grad, "grads"))
        attended, sent, saved_one = out[0], out[-4], out[-3:]
        saved.append(saved_one)
    while "grads" not in rows:
        attended = pipe.step(attended)
    grad_rows = rows["grads"]
    attended = attended + other_core(sent).astype(F32)
    grad_feed = both_cores((gate * grad_rows).astype(BF16))
    middle = picked + attended
    scale_two = rms_scale(middle)
    unit_two = middle * scale_two
    normed_two = both_cores((unit_two * gain_mlp).astype(BF16))

    sums, done = None, {}
    mlp_sums = Collect(pipe, count, whole_plans, functools.partial(done.__setitem__, "mlp"))
    attn_sums = Collect(pipe, count, shared_plans, functools.partial(done.__setitem__, "attn"))
    for k in range(count):
        while k not in mlp_shards:
            normed_two = pipe.step(normed_two)
        out = mlp(
            chip_array,
            normed_two,
            grad_feed,
            mlp_shards[k],
            hidden,
            places,
            order,
            orders,
            sums,
            k == count - 1,
        )
        out = pipe.step(out)
        sums = out[:-4]
        pipe.launch(scatter_chain(out[-4:], whole_plans, functools.partial(mlp_sums.ready, k)))
    grad_normed_two = sums[2] + other_core(sums[3]).astype(F32)
    feed = sums[0] + other_core(sums[1]).astype(F32)
    grad_middle = norm_back(grad_normed_two, unit_two, scale_two, gain_mlp)
    grad_attended = both_cores((gate * grad_rows + grad_middle).astype(BF16))
    delta = attended + feed
    pipe.launch(to_position((gate * delta).astype(BF16), "out"))
    grad_logit = jnp.sum(grad_rows * delta, axis=-1, keepdims=True) * gate * (1.0 - gate)
    router_part = jnp.sum(grad_logit * picked, axis=0)
    mlp_gain_part = jnp.sum(grad_normed_two * unit_two, axis=0)

    grad_sum = None
    for at, k in enumerate(list(range(1, count)) + [0]):
        out = attention_backward(
            chip_array,
            grad_attended,
            normed_one,
            saved[k],
            attn_shards[k],
            places,
            shared_orders,
            grad_sum,
            at == count - 1,
        )
        out = pipe.step(out)
        grad_sum = out[0]
        pipe.launch(scatter_chain(out[-4:], shared_plans, functools.partial(attn_sums.ready, k)))
    grad_normed_one = grad_sum + other_core(out[1]).astype(F32)
    grad_picked = (
        grad_middle
        + norm_back(grad_normed_one, unit_one, scale_one, gain_attn)
        + grad_logit * router
    ).astype(BF16)
    pipe.launch(to_position(grad_picked, "back"))
    attn_gain_part = jnp.sum(grad_normed_one * unit_one, axis=0)
    small = sum_everywhere(jnp.stack([attn_gain_part, mlp_gain_part, router_part]))
    layer_out = pipe.step(add_rows(place, tokens, rows["out"]))
    grad_tokens = pipe.step(add_rows(place, cotangent, rows["back"]))
    while "mlp" not in done:
        grad_tokens = pipe.step(grad_tokens)
    grad_mlp = place_mlp(chip_array, core_array, done["mlp"], places, order, 2 * hidden)
    pipe.drain()
    grad_qkv, grad_out = place_attention(
        chip_array, core_array, done["attn"], shared_places, width
    )
    return (
        layer_out,
        grad_tokens,
        small[0],
        small[1],
        small[2],
        grad_qkv,
        grad_out,
        grad_mlp,
    )


def solution(mesh):
    placed = (
        P("mp", "seq", None),
        P("mp", "seq", None),
        P("mp"),
        P("mp", "seq"),
        P(),
        P(),
        P(),
        P(None, None, "mp"),
        P("mp", None),
        P("mp", None, None),
    )
    return jax.shard_map(
        on_device,
        mesh=mesh,
        in_specs=placed,
        out_specs=(
            P("mp", "seq", None),
            P("mp", "seq", None),
            P(),
            P(),
            P(),
            P(None, None, "mp"),
            P("mp", None),
            P("mp", None, None),
        ),
        check_vma=False,
    )
```

```python
import functools

import jax
import jax.numpy as jnp
from jax import lax
from jax.experimental import pallas as pl
from jax.experimental.pallas import tpu as pltpu
from jax.sharding import PartitionSpec as P

HEAD = 64
LANES = 128
EPSILON = 1e-06
NEGATIVE = -1e30
ROOT = 0.7978845608028654
CUBE = 0.044715
SCALE = HEAD**-0.5
LAST = 1
DELAY = 4
F32 = jnp.float32
BF16 = jnp.bfloat16
VMEM_BYTES = 32 * 1024 * 1024

NN = (((1,), (0,)), ((), ()))
NT = (((1,), (1,)), ((), ()))
TN = (((0,), (0,)), ((), ()))

IN_HBM = pl.BlockSpec(memory_space=pltpu.HBM)
IN_VMEM = pl.BlockSpec(memory_space=pltpu.VMEM)
IN_SMEM = pl.BlockSpec(memory_space=pltpu.SMEM)


def mm(left, right, dims):
    return lax.dot_general(left, right, dims, preferred_element_type=F32)


def cost(flops, bytes_accessed, transcendentals=0):
    return pl.CostEstimate(
        flops=int(flops), bytes_accessed=int(bytes_accessed), transcendentals=int(transcendentals)
    )


def in_hbm(arrays):
    return [pltpu.with_memory_space_constraint(array, pltpu.HBM) for array in arrays]


def params(semantics=None):
    return pltpu.CompilerParams(dimension_semantics=semantics, vmem_limit_bytes=VMEM_BYTES)


def combos(bits):
    found = [0]
    for bit in bits:
        found = [i | extra for i in found for extra in (0, 1 << bit)]
    return found


def exchange_plan(chips, shared):
    bits = list(range(chips.bit_length() - 1))
    return (bits[: len(bits) // 2], bits[len(bits) // 2 :]) if shared else (bits, [])


def reversed_bits(chip, chips):
    count = chips.bit_length() - 1
    return sum(((chip >> bit) & 1) << (count - 1 - bit) for bit in range(count))


def across(value, bit):
    ranks = lax.axis_size("seq")
    last = (ranks // 2).bit_length() - 2
    pairs = [(i, i ^ (2 << (last - bit if i % 2 else bit))) for i in range(ranks)]
    return lax.ppermute(value, "seq", pairs)


def other_core(value):
    ranks = lax.axis_size("seq")
    return lax.ppermute(value, "seq", [(i, i ^ 1) for i in range(ranks)])


def ring(value, turn=1):
    depth = lax.axis_size("mp")
    cycle = [0] + list(range(1, depth, 2)) + list(range(2, depth, 2))[::-1]
    pairs = [(cycle[i], cycle[(i + turn) % depth]) for i in range(depth)]
    return lax.ppermute(value, "mp", pairs)


def joined(arrays):
    return arrays[0] if len(arrays) == 1 else jnp.concatenate(arrays, axis=0)


def gather_places(plan):
    bits, kept = plan
    held = [combos(kept)]
    for bit in bits:
        flat = [i for part in held for i in part]
        held = [flat, [i | (1 << bit) for i in flat]]
    return held


def scatter_order(plan):
    return combos(plan[0] + plan[1])


def added(*parts):
    total = parts[0].astype(F32)
    for part in parts[1:]:
        total = total + part.astype(F32)
    return total.astype(BF16)


def swapped(value, at, count):
    shape = value.shape
    parts = value.reshape((2**at, 2, 2 ** (count - at - 1)) + shape[1:])
    return jnp.concatenate([parts[:, 1:], parts[:, :1]], axis=1).reshape(shape)


class Pipe:
    def __init__(self):
        self.slot = 0
        self.flights = []

    def launch(self, chain):
        self.advance(chain, None)

    def advance(self, chain, got):
        try:
            arrays, slots = chain.send(got)
        except StopIteration:
            return
        self.flights.append((chain, arrays, self.slot + slots))

    def step(self, outs):
        self.slot += 1
        due = [f for f in self.flights if f[2] <= self.slot]
        self.flights = [f for f in self.flights if f[2] > self.slot]
        outs, got = lax.optimization_barrier((outs, [f[1] for f in due]))
        for flight, arrays in zip(due, got):
            self.advance(flight[0], arrays)
        return outs

    def drain(self):
        while self.flights:
            due, self.flights = self.flights, []
            self.slot = max(self.slot, min(f[2] for f in due))
            for flight in due:
                self.advance(flight[0], flight[1])


def gather_chain(piece, plan, done, last=1, pause=0):
    held = [piece]
    for at, bit in enumerate(plan[0]):
        if at and pause:
            yield [], pause
        whole = joined(held)
        (got,) = yield [across(whole, bit)], (last if at == len(plan[0]) - 1 else 1)
        held = [whole, got]
    done(held)


def weights_chain(pipe, piece, turn, shards, plan, done, first=1):
    for at, k in enumerate(shards):
        (piece,) = yield [ring(piece, turn)], (1 if at else first)
        pipe.launch(gather_chain(piece, plan, functools.partial(done, k)))


def scatter_chain(low, high, plan, done, wait=0):
    if wait:
        low, high = yield [low, high], wait
    lows = [low]
    for at, bit in enumerate(plan[0]):
        (got,) = yield [across(high, bit)], 1
        lows = lows + [got]
        if at + 1 < len(plan[0]):
            half = got.shape[0] // 2
            high = added(*[part[half:] for part in lows])
            lows = [part[:half] for part in lows]
    done(lows)


class Collect:
    def __init__(self, pipe, count, plan, done):
        self.pipe, self.count, self.plan, self.done = pipe, count, plan, done
        self.parts, self.next, self.sums, self.busy = {}, 1 % count, None, False

    def ready(self, k, totals):
        self.parts[k] = totals
        self.go()

    def go(self):
        if self.busy or self.next is None or self.next not in self.parts:
            return
        parts = self.parts[self.next] + ([] if self.sums is None else [self.sums])
        self.sums = added(*parts)
        if self.next == 0:
            self.next = None
            self.finish(self.sums)
            return
        self.next = (self.next + 1) % self.count
        self.busy = True
        self.pipe.launch(self.hop())

    def hop(self):
        (self.sums,) = yield [ring(self.sums)], 1
        self.busy = False
        self.go()

    def finish(self, total):
        self.pipe.launch(self.spread(total))

    def spread(self, total):
        kept = self.plan[1]
        for at, bit in enumerate(kept):
            (got,) = yield [across(total, bit)], 1
            total = added(total, swapped(got, at, len(kept)))
        self.pipe.launch(gather_chain(total, self.plan, self.cores, 1 if kept else LAST))

    def cores(self, held):
        def chain():
            got = yield [other_core(part) for part in held], 1
            self.done(held + got)

        self.pipe.launch(chain())


class CollectBothWays(Collect):
    def __init__(self, pipe, count, plan, done):
        super().__init__(pipe, count, plan, done)
        half = count // 2
        self.ways = [[-1, list(range(half, 0, -1))], [1, list(range(half + 1, count))]]
        self.moving, self.arrived = [None, None], []

    def go(self):
        for way in range(2):
            turn, waiting = self.ways[way]
            if not waiting or waiting[0] not in self.parts or self.moving[way] == "busy":
                continue
            parts = self.parts[waiting.pop(0)]
            parts = parts if self.moving[way] is None else parts + [self.moving[way]]
            first = self.moving[way] is None
            self.moving[way] = "busy"
            self.pipe.launch(self.travel(way, turn, parts, len(waiting) * first))
        if not (self.ways[0][1] or self.ways[1][1]) and 0 in self.parts:
            if len(self.arrived) == sum(1 for w in (self.count // 2, self.count - self.count // 2 - 1) if w):
                if self.next is not None:
                    self.next = None
                    self.finish(added(*self.parts[0], *self.arrived))

    def travel(self, way, turn, parts, wait):
        if wait:
            parts = yield parts, wait
        value = parts[0] if len(parts) == 1 else added(*parts)
        (value,) = yield [ring(value, turn)], 1
        self.moving[way] = value
        if not self.ways[way][1]:
            self.arrived.append(value)
        self.go()


def sum_chain(value, done):
    steps = [("seq", [1])]
    for axis, first in (("seq", 2), ("mp", 1)):
        while first < lax.axis_size(axis):
            steps.append((axis, [first, 2 * first][: 2 if 2 * first < lax.axis_size(axis) else 1]))
            first *= 4
    for at, (axis, bits) in enumerate(steps):
        size = lax.axis_size(axis)
        offsets = [a ^ b for b in [0, *bits[1:]] for a in (0, bits[0])]
        got = [lax.ppermute(value, axis, [(i, i ^ o) for i in range(size)]) for o in offsets[1:]]
        if at:
            got = yield got, (2 if at == 1 else 1)
        parts = [value, *got]
        while len(parts) > 1:
            parts = [a + b for a, b in zip(parts[::2], parts[1::2])]
        value = parts[0]
    done(value)


def select_kernel(place_ref, base_ref, out_ref):
    span = base_ref.shape[1]
    for at in range(base_ref.shape[0]):
        place = place_ref[at]
        hot = lax.broadcasted_iota(jnp.int32, (place.shape[0], span), 1) == place
        out_ref[at] = mm(hot.astype(BF16), base_ref[at], NN).astype(BF16)


def together(group, span):
    size = max(1, min(group, 1024 // span))
    while group % size:
        size -= 1
    return size


def select_rows(place, base):
    group, span, width = base.shape
    slots = place.shape[1]
    size = together(group, span)
    return pl.pallas_call(
        select_kernel,
        grid=(group // size,),
        in_specs=[
            pl.BlockSpec((size, slots, 1), lambda g: (g, 0, 0)),
            pl.BlockSpec((size, span, width), lambda g: (g, 0, 0)),
        ],
        out_specs=pl.BlockSpec((size, slots, width), lambda g: (g, 0, 0)),
        out_shape=jax.ShapeDtypeStruct((group, slots, width), BF16),
        compiler_params=params(("arbitrary",)),
        cost_estimate=cost(2 * group * slots * span * width, 2 * group * (span + slots) * width),
    )(place[:, :, None], pltpu.with_memory_space_constraint(base, pltpu.HBM))


def add_kernel(place_ref, base_ref, rows_ref, out_ref):
    span = base_ref.shape[1]
    for at in range(base_ref.shape[0]):
        place = place_ref[at]
        hot = lax.broadcasted_iota(jnp.int32, (span, place.shape[1]), 0) == place
        moved = mm(hot.astype(BF16), rows_ref[at], NN)
        out_ref[at] = (base_ref[at].astype(F32) + moved).astype(BF16)


def add_rows(place, base, rows):
    group, span, width = base.shape
    slots = place.shape[1]
    size = together(group, span)
    block = pl.BlockSpec((size, span, width), lambda g: (g, 0, 0))
    return pl.pallas_call(
        add_kernel,
        grid=(group // size,),
        in_specs=[
            pl.BlockSpec((size, 1, slots), lambda g: (g, 0, 0)),
            block,
            pl.BlockSpec((size, slots, width), lambda g: (g, 0, 0)),
        ],
        out_specs=block,
        out_shape=jax.ShapeDtypeStruct(base.shape, BF16),
        compiler_params=params(("arbitrary",)),
        cost_estimate=cost(2 * group * slots * span * width, 4 * group * span * width),
    )(place[:, None, :], pltpu.with_memory_space_constraint(base, pltpu.HBM), rows)


def start_all(copies, sems):
    started = []
    for at, (source, target) in enumerate(copies):
        copy = pltpu.make_async_copy(source, target, sems.at[at])
        copy.start()
        started.append(copy)
    return started


def attention_copies(chip, sources, places, target, outward=False):
    if len(sources) == 1:
        return [(sources[0].at[3] if outward else sources[0], target)]
    depth = sources[0].shape[2]
    copies = []
    for source, ids in zip(sources, places):
        for at, index in enumerate(ids):
            rows = pl.ds(pl.multiple_of((chip ^ index) * depth, depth), depth)
            if outward:
                copies.append((source.at[at, 3], target.at[rows, :]))
            else:
                copies.append((source.at[at], target.at[:, rows, :]))
    return copies


def mlp_copies(chip, sources, places, order, targets, own):
    copies = []
    for place, index in enumerate(order):
        for side in range(2):
            target = targets[side]
            depth = target.shape[0] // len(order)
            if own:
                start = pl.multiple_of((chip ^ index) * depth, depth)
                source = sources[side].at[pl.ds(start, depth), :]
            else:
                for array, ids in zip(sources, places):
                    if index in ids:
                        source = array.at[ids.index(index), side]
            copies.append((source, target.at[pl.ds(place * depth, depth), :]))
    return copies


def row_blocks(rows):
    blocks = []
    for start in (0, rows // 2):
        half = rows // 6
        for first, last, low, high in ((0, 1, 0, 1), (1, 2, 0, 2), (2, 3, 2, 3)):
            blocks.append(tuple(start + half * at for at in (first, last, low, high)))
    return blocks


def causal(first, last, low, high):
    shape = (last - first, high - low)
    row = lax.broadcasted_iota(jnp.int32, shape, 0) + (first - low)
    return row >= lax.broadcasted_iota(jnp.int32, shape, 1)


def head_groups(columns):
    lanes = min(LANES, columns)
    return [
        (slice(at, at + lanes), at // HEAD, lanes // HEAD) for at in range(0, columns, lanes)
    ]


def own_lanes(value, side, heads):
    if heads == 1:
        return value
    lane = lax.broadcasted_iota(jnp.int32, (1, value.shape[1]), 1)
    mine = (lane >= HEAD) if side else (lane < HEAD)
    return jnp.where(mine, value, jnp.zeros_like(value))


def finish(total, last, outs):
    if not last:
        outs[0][...] = total
        return
    half = total.shape[0] // 2
    outs[0][...] = total[:half]
    outs[1][...] = total[half:].astype(BF16)


def sum_shapes(rows, width, last):
    if not last:
        return [jax.ShapeDtypeStruct((rows, width), F32)]
    return [
        jax.ShapeDtypeStruct((rows // 2, width), F32),
        jax.ShapeDtypeStruct((rows // 2, width), BF16),
    ]


def attention_forward_kernel(places, counts, chip_ref, normed_ref, *refs):
    sources = []
    for count in counts:
        sources.append(refs[:count])
        refs = refs[count:]
    others, refs = refs[: len(counts) - 1], refs[len(counts) - 1 :]
    heads_ref, mixed_ref, log_ref, *refs = refs
    sums, (held, *out_held, sems) = (refs[:2], refs[2:]) if len(counts) > 1 else ([], refs)
    chip = chip_ref[0]
    copies = attention_copies(chip, sources[-1], places, held)
    n_own = len(copies)
    for at, shard in enumerate(sources[:-1]):
        copies += attention_copies(chip, shard, places, out_held[0].at[at], True)
    copies = start_all(copies, sems)
    for copy in copies[:n_own]:
        copy.wait()
    rows = normed_ref.shape[0]
    columns = held.shape[2]
    heads_all = mm(normed_ref[...], jnp.concatenate([held[c] for c in range(3)], axis=-1), NN)
    for c in range(3):
        heads_ref[c] = heads_all[:, c * columns : (c + 1) * columns].astype(BF16)
    lane = lax.broadcasted_iota(jnp.int32, (1, LANES), 1)
    for first, end, low, high in row_blocks(rows):
        seen = causal(first, end, low, high)
        logs = jnp.zeros((end - first, LANES), F32)
        for lanes, head, heads in head_groups(columns):
            query = heads_ref[0, first:end, lanes]
            keys = heads_ref[1, low:high, lanes]
            values = heads_ref[2, low:high, lanes]
            out = None
            for side in range(heads):
                scores = mm(own_lanes(query, side, heads), keys, NT) * SCALE
                scores = jnp.where(seen, scores, NEGATIVE)
                peak = jnp.max(scores, axis=-1, keepdims=True)
                raised = jnp.exp(scores - peak)
                total = jnp.sum(raised, axis=-1, keepdims=True)
                weights = (raised * (1.0 / total)).astype(BF16)
                part = own_lanes(mm(weights, values, NN), side, heads)
                out = part if out is None else out + part
                logs = jnp.where(lane == head + side, peak + jnp.log(total), logs)
            mixed_ref[first:end, lanes] = out.astype(BF16)
        log_ref[first:end, :] = logs
    for copy in copies[n_own:]:
        copy.wait()
    if len(counts) > 1:
        mixed = [part[...] for part in others] + [mixed_ref[...]]
        outward = [out_held[0][at] for at in range(len(counts) - 1)] + [held[3]]
        attended = mm(
            jnp.concatenate(mixed, axis=-1), jnp.concatenate(outward, axis=-1), NT
        )
        finish(attended, True, sums)


def attention_forward(chip, normed, shards, places, mixed):
    rows, width = normed.shape
    columns = shards[0][0].shape[-1]
    counts = [len(shard) for shard in shards]
    last = len(shards) > 1
    sources = [source for shard in shards for source in shard]
    chips = lax.axis_size("seq") // 2
    flops = 2 * rows * width * columns * (3 + last * len(shards)) + rows * rows * columns
    scratch = [pltpu.VMEM((4, width, columns), BF16)]
    if last:
        scratch.append(pltpu.VMEM((len(shards) - 1, width, columns), BF16))
    return pl.pallas_call(
        functools.partial(attention_forward_kernel, places, counts),
        in_specs=[IN_SMEM, IN_VMEM] + [IN_HBM] * len(sources) + [IN_VMEM] * len(mixed),
        out_specs=[IN_VMEM] * (3 + 2 * last),
        out_shape=[
            jax.ShapeDtypeStruct((3, rows, columns), BF16),
            jax.ShapeDtypeStruct((rows, columns), BF16),
            jax.ShapeDtypeStruct((rows, LANES), F32),
        ]
        + (sum_shapes(rows, width, True) if last else []),
        scratch_shapes=scratch + [pltpu.SemaphoreType.DMA((chips * len(shards),))],
        compiler_params=params(),
        cost_estimate=cost(flops, 2 * rows * width + 8 * width * columns, rows * rows * 2),
    )(chip, normed, *in_hbm(sources), *mixed)


def attention_backward_kernel(
    places,
    order,
    n_sources,
    has_acc,
    last,
    chip_ref,
    grad_ref,
    normed_ref,
    heads_ref,
    mixed_ref,
    log_ref,
    *refs,
):
    sources, refs = refs[:n_sources], refs[n_sources:]
    if has_acc:
        acc_ref, refs = refs[0], refs[1:]
    sums, refs = refs[: 1 + last], refs[1 + last :]
    outs, refs = refs[:2], refs[2:]
    held, grad_held, grad_heads, sems, out_sems = refs
    chip = chip_ref[0]
    copies = start_all(attention_copies(chip, sources, places, held), sems)
    rows = normed_ref.shape[0]
    width = held.shape[2]
    depth = outs[0].shape[2]
    grad_held[3] = mm(mixed_ref[...], grad_ref[...], TN).astype(BF16).T
    for copy in copies:
        copy.wait()
    grad_mixed = mm(grad_ref[...], held[3], NN).astype(BF16)
    lane = lax.broadcasted_iota(jnp.int32, (1, LANES), 1)
    for lanes, head, heads in head_groups(width):
        key_parts, value_parts = [], []
        for first, end, low, high in row_blocks(rows):
            query = heads_ref[0, first:end, lanes]
            keys = heads_ref[1, low:high, lanes]
            values = heads_ref[2, low:high, lanes]
            grad_out = grad_mixed[first:end, lanes]
            logs = log_ref[first:end, :]
            seen = causal(first, end, low, high)
            grad_query = grad_keys = grad_values = None
            for side in range(heads):
                own_query = own_lanes(query, side, heads)
                own_grad = own_lanes(grad_out, side, heads)
                log_total = jnp.sum(
                    jnp.where(lane == head + side, logs, 0.0), axis=-1, keepdims=True
                )
                scores = jnp.where(seen, mm(own_query, keys, NT) * SCALE, NEGATIVE)
                shares = jnp.exp(scores - log_total)
                grad_weights = mm(own_grad, values, NT)
                inner = jnp.sum(shares * grad_weights, axis=-1, keepdims=True)
                grad_scores = (shares * (grad_weights - inner)).astype(BF16)
                weights = shares.astype(BF16)
                part_query = own_lanes(mm(grad_scores, keys, NN), side, heads)
                part_keys = mm(grad_scores, own_query, TN)
                part_values = mm(weights, own_grad, TN)
                if side == 0:
                    grad_query, grad_keys, grad_values = part_query, part_keys, part_values
                else:
                    grad_query = grad_query + part_query
                    grad_keys = grad_keys + part_keys
                    grad_values = grad_values + part_values
            grad_heads[0, first:end, lanes] = (grad_query * SCALE).astype(BF16)
            key_parts.append(grad_keys)
            value_parts.append(grad_values)
        half = rows // 6
        for c, parts, scale in ((1, key_parts, SCALE), (2, value_parts, 1.0)):
            for pair in range(2):
                one, two, three = parts[3 * pair : 3 * pair + 3]
                for at, value in enumerate((one + two[:half], two[half:], three)):
                    start = (3 * pair + at) * half
                    grad_heads[c, start : start + half, lanes] = (value * scale).astype(BF16)
    grad_all = jnp.concatenate([grad_heads[c] for c in range(3)], axis=-1)
    grad_qkv = mm(grad_all, normed_ref[...], TN).astype(BF16)
    for c in range(3):
        grad_held[c] = grad_qkv[c * width : (c + 1) * width].T
    copies = []
    for at, index in enumerate(order):
        start = pl.multiple_of((chip ^ index) * depth, depth)
        high, at = divmod(at, len(order) // 2)
        copies.append((grad_held.at[:, pl.ds(start, depth), :], outs[high].at[at]))
    copies = start_all(copies, out_sems)
    grad_normed = mm(grad_all, jnp.concatenate([held[c] for c in range(3)], axis=-1), NT)
    if has_acc:
        grad_normed = grad_normed + acc_ref[...]
    finish(grad_normed, last, sums)
    for copy in copies:
        copy.wait()


def attention_backward(chip, grad, normed, saved, sources, places, order, acc, last):
    rows, width = normed.shape
    columns = sources[0].shape[-1]
    chips = lax.axis_size("seq") // 2
    has_acc = acc is not None
    n_sources = len(sources)
    n_copies = 1 if n_sources == 1 else chips
    piece = jax.ShapeDtypeStruct((chips // 2, 4, width // chips, columns), BF16)
    flops = 2 * rows * width * columns * 8 + 3 * rows * rows * columns
    return pl.pallas_call(
        functools.partial(
            attention_backward_kernel, places, order, n_sources, has_acc, last
        ),
        in_specs=[IN_SMEM] + [IN_VMEM] * 5 + [IN_HBM] * n_sources + [IN_VMEM] * has_acc,
        out_specs=[IN_VMEM] * (1 + last) + [IN_HBM] * 2,
        out_shape=sum_shapes(rows, width, last) + [piece] * 2,
        scratch_shapes=[
            pltpu.VMEM((4, width, columns), BF16),
            pltpu.VMEM((4, width, columns), BF16),
            pltpu.VMEM((3, rows, columns), BF16),
            pltpu.SemaphoreType.DMA((n_copies,)),
            pltpu.SemaphoreType.DMA((chips,)),
        ],
        input_output_aliases={6 + n_sources: 0} if has_acc and not last else {},
        compiler_params=params(),
        cost_estimate=cost(flops, 12 * rows * width + 16 * width * columns, rows * rows * 2),
    )(chip, grad, normed, *saved, *in_hbm(sources), *([acc] if has_acc else []))


def mlp_kernel(places, order, n_sources, has_acc, last, chip_ref, normed_ref, grad_ref, *refs):
    sources, refs = refs[:n_sources], refs[n_sources:]
    if has_acc:
        acc_in, refs = refs[:2], refs[2:]
    sums, refs = refs[: 2 + 2 * last], refs[2 + 2 * last :]
    outs, refs = refs[:2], refs[2:]
    up_held, down_held, up_grad, down_grad, active_held, upward_held, sems, out_sems = refs
    own = not has_acc
    copies = mlp_copies(chip_ref[0], sources, places, order, (up_held, down_held), own)
    copies = start_all(copies, sems)
    hidden = up_held.shape[0]
    depth = hidden // len(order)
    step = max(depth, min(256, hidden))
    waited = 0
    leaving = []
    for start in range(0, hidden, step):
        ready = 2 * ((start + step) // depth)
        for copy in copies[waited:ready]:
            copy.wait()
        waited = ready
        chunk = slice(start, start + step)
        upward = mm(normed_ref[...], up_held[chunk], NT)
        square = upward * upward
        bent = jnp.tanh(ROOT * upward * (1.0 + CUBE * square))
        active = (0.5 * upward * (1.0 + bent)).astype(BF16)
        slope = 0.5 * (1.0 + bent) + 0.5 * ROOT * upward * (1.0 - bent * bent) * (
            1.0 + 3.0 * CUBE * square
        )
        grad_active = mm(grad_ref[...], down_held[chunk], NT)
        grad_upward = (grad_active * slope).astype(BF16)
        active_held[:, chunk] = active
        upward_held[:, chunk] = grad_upward
        up_grad[chunk] = mm(grad_upward, normed_ref[...], TN).astype(BF16)
        down_grad[chunk] = mm(active, grad_ref[...], TN).astype(BF16)
        for at in range(start // depth, (start + step) // depth):
            for side, grads in enumerate((up_grad, down_grad)):
                high, place = divmod(at, len(order) // 2)
                copy = pltpu.make_async_copy(
                    grads.at[pl.ds(at * depth, depth), :],
                    outs[high].at[place, side],
                    out_sems.at[2 * at + side],
                )
                copy.start()
                leaving.append(copy)
    for i, (left, right) in enumerate(((active_held, down_held), (upward_held, up_held))):
        total = mm(left[...], right[...], NN)
        if has_acc:
            total = total + acc_in[i][...]
        finish(total, last, sums[i * (1 + last) : (i + 1) * (1 + last)])
    for copy in leaving:
        copy.wait()


def mlp(chip, normed, grad, sources, hidden, places, order, acc, last):
    rows, width = normed.shape
    chips = len(order)
    depth = hidden // chips
    has_acc = acc is not None
    n_sources = len(sources)
    piece = jax.ShapeDtypeStruct((chips // 2, 2, depth, width), BF16)
    aliased = {3 + n_sources: 0, 4 + n_sources: 1} if has_acc and not last else {}
    return pl.pallas_call(
        functools.partial(mlp_kernel, places, order, n_sources, has_acc, last),
        in_specs=[IN_SMEM] + [IN_VMEM] * 2 + [IN_HBM] * n_sources + [IN_VMEM] * (2 * has_acc),
        out_specs=[IN_VMEM] * (2 + 2 * last) + [IN_HBM] * 2,
        out_shape=sum_shapes(rows, width, last) * 2 + [piece] * 2,
        scratch_shapes=[pltpu.VMEM((hidden, width), BF16)] * 4
        + [pltpu.VMEM((rows, hidden), BF16)] * 2
        + [
            pltpu.SemaphoreType.DMA((2 * chips,)),
            pltpu.SemaphoreType.DMA((2 * chips,)),
        ],
        input_output_aliases=aliased,
        compiler_params=params(),
        cost_estimate=cost(
            12 * rows * width * hidden, 20 * rows * width + 8 * width * hidden, rows * hidden
        ),
    )(chip, normed, grad, *in_hbm(sources), *(acc if has_acc else []))


def place_attention_kernel(places, n_sources, chip_ref, core_ref, *refs):
    sources, refs = refs[:n_sources], refs[n_sources:]
    qkv_ref, out_ref, held, sems = refs
    half = n_sources // 2
    copies = []
    for which, core in enumerate((core_ref[0], 1 - core_ref[0])):
        copies += attention_copies(
            chip_ref[which], sources[which * half : (which + 1) * half], places, held.at[core]
        )
    for copy in start_all(copies, sems):
        copy.wait()
    columns = held.shape[3]
    for c in range(3):
        qkv_ref[c] = jnp.concatenate([held[0, c], held[1, c]], axis=-1).astype(F32)
    for core in range(2):
        out_ref[core * columns : (core + 1) * columns, :] = held[core, 3].astype(F32).T


def place_attention(chip, core, sources, places, width):
    columns = sources[0].shape[-1]
    n_sources = len(sources)
    return pl.pallas_call(
        functools.partial(place_attention_kernel, places, n_sources),
        in_specs=[IN_SMEM, IN_SMEM] + [IN_HBM] * n_sources,
        out_specs=[IN_VMEM] * 2,
        out_shape=[
            jax.ShapeDtypeStruct((3, width, 2 * columns), F32),
            jax.ShapeDtypeStruct((2 * columns, width), F32),
        ],
        scratch_shapes=[
            pltpu.VMEM((2, 4, width, columns), BF16),
            pltpu.SemaphoreType.DMA((2 * lax.axis_size("seq"),)),
        ],
        compiler_params=params(),
        cost_estimate=cost(0, 48 * width * columns),
    )(chip, core, *in_hbm(sources))


def place_mlp_kernel(places, order, n_sources, chip_ref, core_ref, *refs):
    sources, refs = refs[:n_sources], refs[n_sources:]
    out_ref, up_held, down_held, out_held, sems, out_sems = refs
    core = core_ref[0]
    hidden, width = up_held.shape[1:]
    half = n_sources // 2
    copies = []
    for which in range(2):
        targets = (up_held.at[which], down_held.at[which])
        copies += mlp_copies(
            chip_ref[which],
            sources[which * half : (which + 1) * half],
            places,
            order,
            targets,
            False,
        )
    copies = start_all(copies, sems)
    depth = hidden // len(order)
    tiles = width // LANES
    size = depth * 2 * tiles
    moved = []
    for which in range(2):
        for at, index in enumerate(order):
            base = len(moved)
            for side, part in enumerate((up_held, down_held)):
                copies[2 * base + side].wait()
                rows = part[which, at * depth : (at + 1) * depth, :].astype(F32)
                for tile in range(tiles):
                    out_held[pl.ds(base * size + 2 * tile + side, depth, stride=2 * tiles), :] = (
                        rows[:, tile * LANES : (tile + 1) * LANES]
                    )
            block = ((core if which == 0 else 1 - core) * len(order) + (chip_ref[which] ^ index)) * size
            copy = pltpu.make_async_copy(
                out_held.at[pl.ds(base * size, size), :],
                out_ref.at[pl.ds(pl.multiple_of(block, size), size), :],
                out_sems.at[base],
            )
            copy.start()
            moved.append(copy)
    for copy in moved:
        copy.wait()


def place_mlp(chip, core, sources, places, order, hidden):
    width = sources[0].shape[-1]
    n_sources = len(sources)
    tiles = width // LANES
    chips = len(order)
    rows = pl.pallas_call(
        functools.partial(place_mlp_kernel, places, order, n_sources),
        in_specs=[IN_SMEM, IN_SMEM] + [IN_HBM] * n_sources,
        out_specs=IN_HBM,
        out_shape=jax.ShapeDtypeStruct((hidden * 2 * tiles, LANES), F32),
        scratch_shapes=[
            pltpu.VMEM((2, hidden // 2, width), BF16),
            pltpu.VMEM((2, hidden // 2, width), BF16),
            pltpu.VMEM((hidden * 2 * tiles, LANES), F32),
            pltpu.SemaphoreType.DMA((4 * chips,)),
            pltpu.SemaphoreType.DMA((2 * chips,)),
        ],
        compiler_params=params(),
        cost_estimate=cost(0, 12 * hidden * width),
    )(chip, core, *in_hbm(sources))
    shaped = rows.reshape(hidden, tiles, 2, LANES)
    return shaped.transpose(0, 2, 1, 3).reshape(hidden, 2, width)


def rms_scale(values):
    return lax.rsqrt(jnp.mean(values * values, axis=-1, keepdims=True) + EPSILON)


def norm_back(grad_normed, unit_rows, scale, gain):
    scaled = gain * grad_normed
    return scale * (scaled - unit_rows * jnp.mean(unit_rows * scaled, axis=-1, keepdims=True))


def pack(first_longer, got):
    ranks, held, slots, width = got.shape
    longer = jnp.where(first_longer, got[:, 0], got[:, 1])
    shorter = jnp.where(first_longer, got[: ranks // 2, 1], got[: ranks // 2, 0])
    return jnp.concatenate(
        [longer.reshape(ranks * slots, width), shorter.reshape(ranks * slots // 2, width)]
    )


def unpack(first_longer, packed, ranks):
    rows, width = packed.shape
    half = rows // 3
    longer = packed[: 2 * half]
    shorter = jnp.concatenate([packed[2 * half :], jnp.zeros((half, width), packed.dtype)])
    both = jnp.stack(
        [
            jnp.where(first_longer, longer, shorter),
            jnp.where(first_longer, shorter, longer),
        ]
    )
    return both.reshape(1, 2, ranks, 2 * half // ranks, width)


def on_device(tokens, cotangent, lengths, routed, gain_attn, gain_mlp, router, w_qkv, w_out, w_mlp):
    group, span, width = tokens.shape
    slots = routed.shape[1]
    ranks = lax.axis_size("seq")
    count = lax.axis_size("mp")
    held = group // ranks
    chips = ranks // 2
    columns = w_qkv.shape[2] // 2
    hidden = w_mlp.shape[0] // 2
    me = lax.axis_index("seq").astype(jnp.int32)
    core = me % 2
    turned = reversed_bits(me // 2, chips)
    chip = jnp.where(core == 0, me // 2, turned)
    chip_array, core_array = chip[None], core[None]
    both_chips = jnp.stack([chip, jnp.where(core == 0, turned, me // 2)])
    whole, shared = exchange_plan(chips, False), exchange_plan(chips, True)
    whole_places, shared_places = gather_places(whole), gather_places(shared)
    whole_order, shared_order = scatter_order(whole), scatter_order(shared)
    pipe = Pipe()

    attn_shards, mlp_shards = {}, {}
    own_attn = jnp.concatenate([w_qkv, w_out.T[None]])
    own_attn = lax.dynamic_slice_in_dim(own_attn, core * columns, columns, 2)
    attn_shards[0] = [own_attn]

    def pieces_of(part, axis, plan):
        size = part.shape[axis] // chips
        return jnp.stack(
            [
                lax.dynamic_slice_in_dim(part, (chip ^ i) * size, size, axis)
                for i in combos(plan[1])
            ]
        )

    piece = pieces_of(own_attn, 1, shared)
    near, far = list(range(1, count // 2 + 1)), list(range(count - 1, count // 2, -1))
    for turn, ks in ((1, near), (-1, far)):
        pipe.launch(weights_chain(pipe, piece, turn, ks, shared, attn_shards.__setitem__))

    slot = lax.broadcasted_iota(jnp.int32, routed.shape, 1)
    live = me * slots + slot < (lengths // 8)[:, None]
    place = jnp.where(live, slot * 8 + routed % 8, -1)
    pair = lax.dynamic_slice_in_dim(lengths, me * held, held, 0)
    first_longer = pair[0] >= pair[1]
    rows = {}

    def to_holder(value, name):
        value = value.reshape(ranks, held, slots, width)
        got = yield [lax.all_to_all(value, "seq", split_axis=0, concat_axis=0, tiled=True)], 1
        rows[name] = pack(first_longer, got[0]).astype(F32)

    def to_position(value, name):
        value = unpack(first_longer, value, ranks)
        got = yield [lax.all_to_all(value, "seq", split_axis=2, concat_axis=0, tiled=True)], 1
        rows[name] = got[0].reshape(group, slots, width)

    def both_cores(value):
        return jnp.concatenate([value, other_core(value)])

    pipe.launch(to_holder(select_rows(place, tokens), "picked"))
    own_mlp = lax.dynamic_slice_in_dim(w_mlp, core * hidden, hidden, 0)
    own_up, own_down = own_mlp[:, 0, :], own_mlp[:, 1, :]
    start = core * hidden + chip * (hidden // chips)
    piece = lax.dynamic_slice_in_dim(w_mlp, start, hidden // chips, 0)
    piece = jnp.swapaxes(piece, 0, 1)[None]
    chosen_grad, cotangent, own_up, own_down, piece = pipe.step(
        (select_rows(place, cotangent), cotangent, own_up, own_down, piece)
    )

    picked = rows["picked"]
    scale_one = rms_scale(picked)
    unit_one = picked * scale_one
    normed_one = both_cores((unit_one * gain_attn).astype(BF16))
    gate = jax.nn.sigmoid(jnp.sum(picked * router, axis=-1, keepdims=True))
    mlp_shards[0] = [own_up, own_down]
    saved, grad_feed = {}, None
    fetched = [[0]] + [[k, count - k] if count - k > k else [k] for k in near]
    for at, batch in enumerate(fetched):
        while not all(k in attn_shards for k in batch):
            normed_one = pipe.step(normed_one)
        outs = []
        for k in batch:
            final = k == fetched[-1][-1]
            before = list(saved) if final else []
            shards = [attn_shards[other] for other in before] + [attn_shards[k]]
            mixed = [saved[other][1] for other in before]
            out = attention_forward(chip_array, normed_one, shards, shared_places, mixed)
            saved[k] = out[:3]
            outs.append(out)
        if at == 0:
            outs, piece, chosen_grad, normed_one = pipe.step((outs, piece, chosen_grad, normed_one))
            for turn, ks in ((1, near), (-1, far)):
                pipe.launch(weights_chain(pipe, piece, turn, ks, whole, mlp_shards.__setitem__))
            pipe.launch(to_holder(chosen_grad, "grads"))
        elif at == len(fetched) - 1:
            grad_feed = both_cores((gate * rows["grads"]).astype(BF16))
            outs, grad_feed = pipe.step((outs, grad_feed))
        else:
            outs, normed_one = pipe.step((outs, normed_one))
        for k, out in zip(batch, outs):
            saved[k] = out[:3]
    attended, sent = outs[-1][3:]
    grad_rows = rows["grads"]
    attended = attended + other_core(sent).astype(F32)
    middle = picked + attended
    scale_two = rms_scale(middle)
    unit_two = middle * scale_two
    normed_two = both_cores((unit_two * gain_mlp).astype(BF16))

    sums, done = None, {}
    mlp_sums = Collect(pipe, count, whole, functools.partial(done.__setitem__, "mlp"))
    attn_sums = CollectBothWays(pipe, count, shared, functools.partial(done.__setitem__, "attn"))
    for k in range(count):
        while k not in mlp_shards:
            normed_two = pipe.step(normed_two)
        out = mlp(
            chip_array,
            normed_two,
            grad_feed,
            mlp_shards[k],
            hidden,
            whole_places,
            whole_order,
            sums,
            k == count - 1,
        )
        out = pipe.step(out)
        sums = out[:-2]
        pipe.launch(scatter_chain(*out[-2:], whole, functools.partial(mlp_sums.ready, k), 0 if k else DELAY))
    grad_normed_two = sums[2] + other_core(sums[3]).astype(F32)
    feed = sums[0] + other_core(sums[1]).astype(F32)
    grad_middle = norm_back(grad_normed_two, unit_two, scale_two, gain_mlp)
    grad_attended = both_cores((gate * grad_rows + grad_middle).astype(BF16))
    delta = attended + feed
    returned = (gate * delta).astype(BF16)
    grad_logit = jnp.sum(grad_rows * delta, axis=-1, keepdims=True) * gate * (1.0 - gate)
    router_part = jnp.sum(grad_logit * picked, axis=0)
    mlp_gain_part = jnp.sum(grad_normed_two * unit_two, axis=0)

    grad_sum = None
    for at, k in enumerate(near[::-1] + far[::-1] + [0]):
        out = attention_backward(
            chip_array,
            grad_attended,
            normed_one,
            saved[k],
            attn_shards[k],
            shared_places,
            shared_order,
            grad_sum,
            at == count - 1,
        )
        out = pipe.step(out)
        grad_sum = out[0]
        if at == count - 1:
            other = other_core(out[1])
        pipe.launch(scatter_chain(*out[-2:], shared, functools.partial(attn_sums.ready, k)))
        if at == max(0, count - 2):
            pipe.launch(to_position(returned, "out"))
    grad_normed_one = grad_sum + other.astype(F32)
    grad_picked = (
        grad_middle
        + norm_back(grad_normed_one, unit_one, scale_one, gain_attn)
        + grad_logit * router
    ).astype(BF16)
    pipe.launch(to_position(grad_picked, "back"))
    attn_gain_part = jnp.sum(grad_normed_one * unit_one, axis=0)
    pipe.launch(
        sum_chain(
            jnp.stack([attn_gain_part, mlp_gain_part, router_part]),
            functools.partial(done.__setitem__, "small"),
        )
    )
    layer_out = pipe.step(add_rows(place, tokens, rows["out"]))
    grad_tokens = pipe.step(add_rows(place, cotangent, rows["back"]))
    while "mlp" not in done:
        pipe.step(())
    grad_mlp = pipe.step(place_mlp(both_chips, core_array, done["mlp"], whole_places, whole_order, 2 * hidden))
    pipe.drain()
    grad_qkv, grad_out = place_attention(
        both_chips, core_array, done["attn"], shared_places, width
    )
    small = done["small"]
    return (
        layer_out,
        grad_tokens,
        small[0],
        small[1],
        small[2],
        grad_qkv,
        grad_out,
        grad_mlp,
    )


def solution(mesh):
    placed = (
        P("mp", "seq", None),
        P("mp", "seq", None),
        P("mp"),
        P("mp", "seq"),
        P(),
        P(),
        P(),
        P(None, None, "mp"),
        P("mp", None),
        P("mp", None, None),
    )
    return jax.shard_map(
        on_device,
        mesh=mesh,
        in_specs=placed,
        out_specs=(
            P("mp", "seq", None),
            P("mp", "seq", None),
            P(),
            P(),
            P(),
            P(None, None, "mp"),
            P("mp", None),
            P("mp", None, None),
        ),
        check_vma=False,
    )
```

```python
import functools

import jax
import jax.numpy as jnp
from jax import lax
from jax.experimental import pallas as pl
from jax.experimental.pallas import tpu as pltpu
from jax.sharding import PartitionSpec as P

HEAD = 64
LANES = 128
EPSILON = 1e-06
NEGATIVE = -1e30
ROOT = 0.7978845608028654
CUBE = 0.044715
SCALE = HEAD**-0.5
LAST = 1
DELAY = 4
F32 = jnp.float32
BF16 = jnp.bfloat16
VMEM_BYTES = 32 * 1024 * 1024

NN = (((1,), (0,)), ((), ()))
NT = (((1,), (1,)), ((), ()))
TN = (((0,), (0,)), ((), ()))

IN_HBM = pl.BlockSpec(memory_space=pltpu.HBM)
IN_VMEM = pl.BlockSpec(memory_space=pltpu.VMEM)
IN_SMEM = pl.BlockSpec(memory_space=pltpu.SMEM)


def mm(left, right, dims):
    return lax.dot_general(left, right, dims, preferred_element_type=F32)


def cost(flops, bytes_accessed, transcendentals=0):
    return pl.CostEstimate(
        flops=int(flops), bytes_accessed=int(bytes_accessed), transcendentals=int(transcendentals)
    )


def in_hbm(arrays):
    return [pltpu.with_memory_space_constraint(array, pltpu.HBM) for array in arrays]


def params(semantics=None):
    return pltpu.CompilerParams(dimension_semantics=semantics, vmem_limit_bytes=VMEM_BYTES)


def combos(bits):
    found = [0]
    for bit in bits:
        found = [i | extra for i in found for extra in (0, 1 << bit)]
    return found


def exchange_plan(chips, shared):
    bits = list(range(chips.bit_length() - 1))
    return (bits[: len(bits) // 2], bits[len(bits) // 2 :]) if shared else (bits, [])


def reversed_bits(chip, chips):
    count = chips.bit_length() - 1
    return sum(((chip >> bit) & 1) << (count - 1 - bit) for bit in range(count))


def across(value, bit):
    ranks = lax.axis_size("seq")
    last = (ranks // 2).bit_length() - 2
    pairs = [(i, i ^ (2 << (last - bit if i % 2 else bit))) for i in range(ranks)]
    return lax.ppermute(value, "seq", pairs)


def other_core(value):
    ranks = lax.axis_size("seq")
    return lax.ppermute(value, "seq", [(i, i ^ 1) for i in range(ranks)])


def ring(value, turn=1):
    depth = lax.axis_size("mp")
    cycle = [0] + list(range(1, depth, 2)) + list(range(2, depth, 2))[::-1]
    pairs = [(cycle[i], cycle[(i + turn) % depth]) for i in range(depth)]
    return lax.ppermute(value, "mp", pairs)


def joined(arrays):
    return arrays[0] if len(arrays) == 1 else jnp.concatenate(arrays, axis=0)


def gather_places(plan):
    bits, kept = plan
    held = [combos(kept)]
    for bit in bits:
        flat = [i for part in held for i in part]
        held = [flat, [i | (1 << bit) for i in flat]]
    return held


def scatter_order(plan):
    return combos(plan[0] + plan[1])


def added(*parts):
    total = parts[0].astype(F32)
    for part in parts[1:]:
        total = total + part.astype(F32)
    return total.astype(BF16)


def swapped(value, at, count):
    shape = value.shape
    parts = value.reshape((2**at, 2, 2 ** (count - at - 1)) + shape[1:])
    return jnp.concatenate([parts[:, 1:], parts[:, :1]], axis=1).reshape(shape)


class Pipe:
    def __init__(self):
        self.slot = 0
        self.flights = []

    def launch(self, chain):
        self.advance(chain, None)

    def advance(self, chain, got):
        try:
            arrays, slots = chain.send(got)
        except StopIteration:
            return
        self.flights.append((chain, arrays, self.slot + slots))

    def step(self, outs):
        self.slot += 1
        due = [f for f in self.flights if f[2] <= self.slot]
        self.flights = [f for f in self.flights if f[2] > self.slot]
        outs, got = lax.optimization_barrier((outs, [f[1] for f in due]))
        for flight, arrays in zip(due, got):
            self.advance(flight[0], arrays)
        return outs

    def drain(self):
        while self.flights:
            due, self.flights = self.flights, []
            self.slot = max(self.slot, min(f[2] for f in due))
            for flight in due:
                self.advance(flight[0], flight[1])


def gather_chain(piece, plan, done, last=1, pause=0):
    held = [piece]
    for at, bit in enumerate(plan[0]):
        if at and pause:
            yield [], pause
        whole = joined(held)
        (got,) = yield [across(whole, bit)], (last if at == len(plan[0]) - 1 else 1)
        held = [whole, got]
    done(held)


def weights_chain(pipe, piece, turn, shards, plan, done, first=1):
    for at, k in enumerate(shards):
        (piece,) = yield [ring(piece, turn)], (1 if at else first)
        pipe.launch(gather_chain(piece, plan, functools.partial(done, k)))


def scatter_chain(low, high, plan, done, wait=0):
    if wait:
        low, high = yield [low, high], wait
    lows = [low]
    for at, bit in enumerate(plan[0]):
        (got,) = yield [across(high, bit)], 1
        lows = lows + [got]
        if at + 1 < len(plan[0]):
            half = got.shape[0] // 2
            high = added(*[part[half:] for part in lows])
            lows = [part[:half] for part in lows]
    done(lows)


class Collect:
    def __init__(self, pipe, count, plan, done):
        self.pipe, self.count, self.plan, self.done = pipe, count, plan, done
        self.parts, self.next, self.sums, self.busy = {}, 1 % count, None, False

    def ready(self, k, totals):
        self.parts[k] = totals
        self.go()

    def go(self):
        if self.busy or self.next is None or self.next not in self.parts:
            return
        parts = self.parts[self.next] + ([] if self.sums is None else [self.sums])
        self.sums = added(*parts)
        if self.next == 0:
            self.next = None
            self.finish(self.sums)
            return
        self.next = (self.next + 1) % self.count
        self.busy = True
        self.pipe.launch(self.hop())

    def hop(self):
        (self.sums,) = yield [ring(self.sums)], 1
        self.busy = False
        self.go()

    def finish(self, total):
        self.pipe.launch(self.spread(total))

    def spread(self, total):
        kept = self.plan[1]
        for at, bit in enumerate(kept):
            (got,) = yield [across(total, bit)], 1
            total = added(total, swapped(got, at, len(kept)))
        self.pipe.launch(gather_chain(total, self.plan, self.cores, 1 if kept else LAST))

    def cores(self, held):
        def chain():
            got = yield [other_core(part) for part in held], 1
            self.done(held + got)

        self.pipe.launch(chain())


class CollectBothWays(Collect):
    def __init__(self, pipe, count, plan, done):
        super().__init__(pipe, count, plan, done)
        half = count // 2
        self.ways = [[-1, list(range(half, 0, -1))], [1, list(range(half + 1, count))]]
        self.moving, self.arrived = [None, None], []

    def go(self):
        for way in range(2):
            turn, waiting = self.ways[way]
            if not waiting or waiting[0] not in self.parts or self.moving[way] == "busy":
                continue
            parts = self.parts[waiting.pop(0)]
            parts = parts if self.moving[way] is None else parts + [self.moving[way]]
            self.moving[way] = "busy"
            self.pipe.launch(self.travel(way, turn, parts))
        if not (self.ways[0][1] or self.ways[1][1]) and 0 in self.parts:
            if len(self.arrived) == sum(1 for w in (self.count // 2, self.count - self.count // 2 - 1) if w):
                if self.next is not None:
                    self.next = None
                    self.finish(added(*self.parts[0], *self.arrived))

    def travel(self, way, turn, parts):
        value = parts[0] if len(parts) == 1 else added(*parts)
        (value,) = yield [ring(value, turn)], 1 + way
        self.moving[way] = value
        if not self.ways[way][1]:
            self.arrived.append(value)
        self.go()


def sum_axis(value, axis, bits):
    size = lax.axis_size(axis)
    for first in range(0, len(bits), 2):
        now = bits[first : first + 2]
        offsets = [a ^ b for b in [0, *now[1:]] for a in (0, now[0])]
        parts = [value]
        parts += [lax.ppermute(value, axis, [(i, i ^ o) for i in range(size)]) for o in offsets[1:]]
        while len(parts) > 1:
            parts = [a + b for a, b in zip(parts[::2], parts[1::2])]
        value = parts[0]
    return value


def bits_of(size, first):
    return [1 << bit for bit in range(first, size.bit_length() - 1)]


def select_kernel(place_ref, base_ref, out_ref):
    span = base_ref.shape[1]
    for at in range(base_ref.shape[0]):
        place = place_ref[at]
        hot = lax.broadcasted_iota(jnp.int32, (place.shape[0], span), 1) == place
        out_ref[at] = mm(hot.astype(BF16), base_ref[at], NN).astype(BF16)


def together(group, span):
    size = max(1, min(group, 2048 // span))
    while group % size:
        size -= 1
    return size


def select_rows(place, base):
    group, span, width = base.shape
    slots = place.shape[1]
    size = together(group, span)
    return pl.pallas_call(
        select_kernel,
        grid=(group // size,),
        in_specs=[
            pl.BlockSpec((size, slots, 1), lambda g: (g, 0, 0)),
            pl.BlockSpec((size, span, width), lambda g: (g, 0, 0)),
        ],
        out_specs=pl.BlockSpec((size, slots, width), lambda g: (g, 0, 0)),
        out_shape=jax.ShapeDtypeStruct((group, slots, width), BF16),
        compiler_params=params(("arbitrary",)),
        cost_estimate=cost(2 * group * slots * span * width, 2 * group * (span + slots) * width),
    )(place[:, :, None], pltpu.with_memory_space_constraint(base, pltpu.HBM))


def add_kernel(place_ref, base_ref, rows_ref, out_ref):
    span = base_ref.shape[1]
    for at in range(base_ref.shape[0]):
        place = place_ref[at]
        hot = lax.broadcasted_iota(jnp.int32, (span, place.shape[1]), 0) == place
        moved = mm(hot.astype(BF16), rows_ref[at], NN)
        out_ref[at] = (base_ref[at].astype(F32) + moved).astype(BF16)


def add_rows(place, base, rows):
    group, span, width = base.shape
    slots = place.shape[1]
    size = together(group, span)
    block = pl.BlockSpec((size, span, width), lambda g: (g, 0, 0))
    return pl.pallas_call(
        add_kernel,
        grid=(group // size,),
        in_specs=[
            pl.BlockSpec((size, 1, slots), lambda g: (g, 0, 0)),
            block,
            pl.BlockSpec((size, slots, width), lambda g: (g, 0, 0)),
        ],
        out_specs=block,
        out_shape=jax.ShapeDtypeStruct(base.shape, BF16),
        compiler_params=params(("arbitrary",)),
        cost_estimate=cost(2 * group * slots * span * width, 4 * group * span * width),
    )(place[:, None, :], pltpu.with_memory_space_constraint(base, pltpu.HBM), rows)


def start_all(copies, sems):
    started = []
    for at, (source, target) in enumerate(copies):
        copy = pltpu.make_async_copy(source, target, sems.at[at])
        copy.start()
        started.append(copy)
    return started


def attention_copies(chip, sources, places, target, outward=False):
    if len(sources) == 1:
        return [(sources[0].at[3] if outward else sources[0], target)]
    depth = sources[0].shape[2]
    copies = []
    for source, ids in zip(sources, places):
        for at, index in enumerate(ids):
            rows = pl.ds(pl.multiple_of((chip ^ index) * depth, depth), depth)
            if outward:
                copies.append((source.at[at, 3], target.at[rows, :]))
            else:
                copies.append((source.at[at], target.at[:, rows, :]))
    return copies


def mlp_copies(chip, sources, places, order, targets, own):
    copies = []
    for place, index in enumerate(order):
        for side in range(2):
            target = targets[side]
            depth = target.shape[0] // len(order)
            if own:
                start = pl.multiple_of((chip ^ index) * depth, depth)
                source = sources[side].at[pl.ds(start, depth), :]
            else:
                for array, ids in zip(sources, places):
                    if index in ids:
                        source = array.at[ids.index(index), side]
            copies.append((source, target.at[pl.ds(place * depth, depth), :]))
    return copies


def row_blocks(rows):
    blocks = []
    for start in (0, rows // 2):
        half = rows // 6
        for first, last, low, high in ((0, 1, 0, 1), (1, 2, 0, 2), (2, 3, 2, 3)):
            blocks.append(tuple(start + half * at for at in (first, last, low, high)))
    return blocks


def causal(first, last, low, high):
    shape = (last - first, high - low)
    row = lax.broadcasted_iota(jnp.int32, shape, 0) + (first - low)
    return row >= lax.broadcasted_iota(jnp.int32, shape, 1)


def head_groups(columns):
    lanes = min(LANES, columns)
    return [
        (slice(at, at + lanes), at // HEAD, lanes // HEAD) for at in range(0, columns, lanes)
    ]


def own_lanes(value, side, heads):
    if heads == 1:
        return value
    lane = lax.broadcasted_iota(jnp.int32, (1, value.shape[1]), 1)
    mine = (lane >= HEAD) if side else (lane < HEAD)
    return jnp.where(mine, value, jnp.zeros_like(value))


def finish(total, last, outs):
    if not last:
        outs[0][...] = total
        return
    half = total.shape[0] // 2
    outs[0][...] = total[:half]
    outs[1][...] = total[half:].astype(BF16)


def sum_shapes(rows, width, last):
    if not last:
        return [jax.ShapeDtypeStruct((rows, width), F32)]
    return [
        jax.ShapeDtypeStruct((rows // 2, width), F32),
        jax.ShapeDtypeStruct((rows // 2, width), BF16),
    ]


def attention_forward_kernel(places, counts, chip_ref, normed_ref, *refs):
    sources = []
    for count in counts:
        sources.append(refs[:count])
        refs = refs[count:]
    others, refs = refs[: len(counts) - 1], refs[len(counts) - 1 :]
    heads_ref, mixed_ref, log_ref, *refs = refs
    sums, (held, *out_held, sems) = (refs[:2], refs[2:]) if len(counts) > 1 else ([], refs)
    chip = chip_ref[0]
    copies = attention_copies(chip, sources[-1], places, held)
    n_own = len(copies)
    for at, shard in enumerate(sources[:-1]):
        copies += attention_copies(chip, shard, places, out_held[0].at[at], True)
    copies = start_all(copies, sems)
    for copy in copies[:n_own]:
        copy.wait()
    rows = normed_ref.shape[0]
    columns = held.shape[2]
    heads_all = mm(normed_ref[...], jnp.concatenate([held[c] for c in range(3)], axis=-1), NN)
    for c in range(3):
        heads_ref[c] = heads_all[:, c * columns : (c + 1) * columns].astype(BF16)
    lane = lax.broadcasted_iota(jnp.int32, (1, LANES), 1)
    for first, end, low, high in row_blocks(rows):
        seen = causal(first, end, low, high)
        logs = jnp.zeros((end - first, LANES), F32)
        for lanes, head, heads in head_groups(columns):
            query = heads_ref[0, first:end, lanes]
            keys = heads_ref[1, low:high, lanes]
            values = heads_ref[2, low:high, lanes]
            out = None
            for side in range(heads):
                scores = mm(own_lanes(query, side, heads), keys, NT) * SCALE
                scores = jnp.where(seen, scores, NEGATIVE)
                peak = jnp.max(scores, axis=-1, keepdims=True)
                raised = jnp.exp(scores - peak)
                total = jnp.sum(raised, axis=-1, keepdims=True)
                weights = (raised * (1.0 / total)).astype(BF16)
                part = own_lanes(mm(weights, values, NN), side, heads)
                out = part if out is None else out + part
                logs = jnp.where(lane == head + side, peak + jnp.log(total), logs)
            mixed_ref[first:end, lanes] = out.astype(BF16)
        log_ref[first:end, :] = logs
    for copy in copies[n_own:]:
        copy.wait()
    if len(counts) > 1:
        mixed = [part[...] for part in others] + [mixed_ref[...]]
        outward = [out_held[0][at] for at in range(len(counts) - 1)] + [held[3]]
        attended = mm(
            jnp.concatenate(mixed, axis=-1), jnp.concatenate(outward, axis=-1), NT
        )
        finish(attended, True, sums)


def attention_forward(chip, normed, shards, places, mixed):
    rows, width = normed.shape
    columns = shards[0][0].shape[-1]
    counts = [len(shard) for shard in shards]
    last = len(shards) > 1
    sources = [source for shard in shards for source in shard]
    chips = lax.axis_size("seq") // 2
    flops = 2 * rows * width * columns * (3 + last * len(shards)) + rows * rows * columns
    scratch = [pltpu.VMEM((4, width, columns), BF16)]
    if last:
        scratch.append(pltpu.VMEM((len(shards) - 1, width, columns), BF16))
    return pl.pallas_call(
        functools.partial(attention_forward_kernel, places, counts),
        in_specs=[IN_SMEM, IN_VMEM] + [IN_HBM] * len(sources) + [IN_VMEM] * len(mixed),
        out_specs=[IN_VMEM] * (3 + 2 * last),
        out_shape=[
            jax.ShapeDtypeStruct((3, rows, columns), BF16),
            jax.ShapeDtypeStruct((rows, columns), BF16),
            jax.ShapeDtypeStruct((rows, LANES), F32),
        ]
        + (sum_shapes(rows, width, True) if last else []),
        scratch_shapes=scratch + [pltpu.SemaphoreType.DMA((chips * len(shards),))],
        compiler_params=params(),
        cost_estimate=cost(flops, 2 * rows * width + 8 * width * columns, rows * rows * 2),
    )(chip, normed, *in_hbm(sources), *mixed)


def attention_backward_kernel(
    places,
    order,
    n_sources,
    has_acc,
    last,
    chip_ref,
    grad_ref,
    normed_ref,
    heads_ref,
    mixed_ref,
    log_ref,
    *refs,
):
    sources, refs = refs[:n_sources], refs[n_sources:]
    if has_acc:
        acc_ref, refs = refs[0], refs[1:]
    sums, refs = refs[: 1 + last], refs[1 + last :]
    outs, refs = refs[:2], refs[2:]
    held, grad_held, grad_heads, sems, out_sems = refs
    chip = chip_ref[0]
    copies = start_all(attention_copies(chip, sources, places, held), sems)
    rows = normed_ref.shape[0]
    width = held.shape[2]
    depth = outs[0].shape[2]
    grad_held[3] = mm(mixed_ref[...], grad_ref[...], TN).astype(BF16).T
    for copy in copies:
        copy.wait()
    grad_mixed = mm(grad_ref[...], held[3], NN).astype(BF16)
    lane = lax.broadcasted_iota(jnp.int32, (1, LANES), 1)
    for lanes, head, heads in head_groups(width):
        key_parts, value_parts = [], []
        for first, end, low, high in row_blocks(rows):
            query = heads_ref[0, first:end, lanes]
            keys = heads_ref[1, low:high, lanes]
            values = heads_ref[2, low:high, lanes]
            grad_out = grad_mixed[first:end, lanes]
            logs = log_ref[first:end, :]
            seen = causal(first, end, low, high)
            grad_query = grad_keys = grad_values = None
            for side in range(heads):
                own_query = own_lanes(query, side, heads)
                own_grad = own_lanes(grad_out, side, heads)
                log_total = jnp.sum(
                    jnp.where(lane == head + side, logs, 0.0), axis=-1, keepdims=True
                )
                scores = jnp.where(seen, mm(own_query, keys, NT) * SCALE, NEGATIVE)
                shares = jnp.exp(scores - log_total)
                grad_weights = mm(own_grad, values, NT)
                inner = jnp.sum(shares * grad_weights, axis=-1, keepdims=True)
                grad_scores = (shares * (grad_weights - inner)).astype(BF16)
                weights = shares.astype(BF16)
                part_query = own_lanes(mm(grad_scores, keys, NN), side, heads)
                part_keys = mm(grad_scores, own_query, TN)
                part_values = mm(weights, own_grad, TN)
                if side == 0:
                    grad_query, grad_keys, grad_values = part_query, part_keys, part_values
                else:
                    grad_query = grad_query + part_query
                    grad_keys = grad_keys + part_keys
                    grad_values = grad_values + part_values
            grad_heads[0, first:end, lanes] = (grad_query * SCALE).astype(BF16)
            key_parts.append(grad_keys)
            value_parts.append(grad_values)
        half = rows // 6
        for c, parts, scale in ((1, key_parts, SCALE), (2, value_parts, 1.0)):
            for pair in range(2):
                one, two, three = parts[3 * pair : 3 * pair + 3]
                for at, value in enumerate((one + two[:half], two[half:], three)):
                    start = (3 * pair + at) * half
                    grad_heads[c, start : start + half, lanes] = (value * scale).astype(BF16)
    grad_all = jnp.concatenate([grad_heads[c] for c in range(3)], axis=-1)
    grad_qkv = mm(grad_all, normed_ref[...], TN).astype(BF16)
    for c in range(3):
        grad_held[c] = grad_qkv[c * width : (c + 1) * width].T
    copies = []
    for at, index in enumerate(order):
        start = pl.multiple_of((chip ^ index) * depth, depth)
        high, at = divmod(at, len(order) // 2)
        copies.append((grad_held.at[:, pl.ds(start, depth), :], outs[high].at[at]))
    copies = start_all(copies, out_sems)
    grad_normed = mm(grad_all, jnp.concatenate([held[c] for c in range(3)], axis=-1), NT)
    if has_acc:
        grad_normed = grad_normed + acc_ref[...]
    finish(grad_normed, last, sums)
    for copy in copies:
        copy.wait()


def attention_backward(chip, grad, normed, saved, sources, places, order, acc, last):
    rows, width = normed.shape
    columns = sources[0].shape[-1]
    chips = lax.axis_size("seq") // 2
    has_acc = acc is not None
    n_sources = len(sources)
    n_copies = 1 if n_sources == 1 else chips
    piece = jax.ShapeDtypeStruct((chips // 2, 4, width // chips, columns), BF16)
    flops = 2 * rows * width * columns * 8 + 3 * rows * rows * columns
    return pl.pallas_call(
        functools.partial(
            attention_backward_kernel, places, order, n_sources, has_acc, last
        ),
        in_specs=[IN_SMEM] + [IN_VMEM] * 5 + [IN_HBM] * n_sources + [IN_VMEM] * has_acc,
        out_specs=[IN_VMEM] * (1 + last) + [IN_HBM] * 2,
        out_shape=sum_shapes(rows, width, last) + [piece] * 2,
        scratch_shapes=[
            pltpu.VMEM((4, width, columns), BF16),
            pltpu.VMEM((4, width, columns), BF16),
            pltpu.VMEM((3, rows, columns), BF16),
            pltpu.SemaphoreType.DMA((n_copies,)),
            pltpu.SemaphoreType.DMA((chips,)),
        ],
        input_output_aliases={6 + n_sources: 0} if has_acc and not last else {},
        compiler_params=params(),
        cost_estimate=cost(flops, 12 * rows * width + 16 * width * columns, rows * rows * 2),
    )(chip, grad, normed, *saved, *in_hbm(sources), *([acc] if has_acc else []))


def mlp_kernel(places, order, n_sources, has_acc, last, chip_ref, normed_ref, grad_ref, *refs):
    sources, refs = refs[:n_sources], refs[n_sources:]
    if has_acc:
        acc_in, refs = refs[:2], refs[2:]
    sums, refs = refs[: 2 + 2 * last], refs[2 + 2 * last :]
    outs, refs = refs[:2], refs[2:]
    up_held, down_held, up_grad, down_grad, active_held, upward_held, sems, out_sems = refs
    own = not has_acc
    copies = mlp_copies(chip_ref[0], sources, places, order, (up_held, down_held), own)
    copies = start_all(copies, sems)
    hidden = up_held.shape[0]
    depth = hidden // len(order)
    step = max(depth, min(256, hidden))
    waited = 0
    leaving = []
    for start in range(0, hidden, step):
        ready = 2 * ((start + step) // depth)
        for copy in copies[waited:ready]:
            copy.wait()
        waited = ready
        chunk = slice(start, start + step)
        upward = mm(normed_ref[...], up_held[chunk], NT)
        square = upward * upward
        bent = jnp.tanh(ROOT * upward * (1.0 + CUBE * square))
        active = (0.5 * upward * (1.0 + bent)).astype(BF16)
        slope = 0.5 * (1.0 + bent) + 0.5 * ROOT * upward * (1.0 - bent * bent) * (
            1.0 + 3.0 * CUBE * square
        )
        grad_active = mm(grad_ref[...], down_held[chunk], NT)
        grad_upward = (grad_active * slope).astype(BF16)
        active_held[:, chunk] = active
        upward_held[:, chunk] = grad_upward
        up_grad[chunk] = mm(grad_upward, normed_ref[...], TN).astype(BF16)
        down_grad[chunk] = mm(active, grad_ref[...], TN).astype(BF16)
        for at in range(start // depth, (start + step) // depth):
            for side, grads in enumerate((up_grad, down_grad)):
                high, place = divmod(at, len(order) // 2)
                copy = pltpu.make_async_copy(
                    grads.at[pl.ds(at * depth, depth), :],
                    outs[high].at[place, side],
                    out_sems.at[2 * at + side],
                )
                copy.start()
                leaving.append(copy)
    for i, (left, right) in enumerate(((active_held, down_held), (upward_held, up_held))):
        total = mm(left[...], right[...], NN)
        if has_acc:
            total = total + acc_in[i][...]
        finish(total, last, sums[i * (1 + last) : (i + 1) * (1 + last)])
    for copy in leaving:
        copy.wait()


def mlp(chip, normed, grad, sources, hidden, places, order, acc, last):
    rows, width = normed.shape
    chips = len(order)
    depth = hidden // chips
    has_acc = acc is not None
    n_sources = len(sources)
    piece = jax.ShapeDtypeStruct((chips // 2, 2, depth, width), BF16)
    aliased = {3 + n_sources: 0, 4 + n_sources: 1} if has_acc and not last else {}
    return pl.pallas_call(
        functools.partial(mlp_kernel, places, order, n_sources, has_acc, last),
        in_specs=[IN_SMEM] + [IN_VMEM] * 2 + [IN_HBM] * n_sources + [IN_VMEM] * (2 * has_acc),
        out_specs=[IN_VMEM] * (2 + 2 * last) + [IN_HBM] * 2,
        out_shape=sum_shapes(rows, width, last) * 2 + [piece] * 2,
        scratch_shapes=[pltpu.VMEM((hidden, width), BF16)] * 4
        + [pltpu.VMEM((rows, hidden), BF16)] * 2
        + [
            pltpu.SemaphoreType.DMA((2 * chips,)),
            pltpu.SemaphoreType.DMA((2 * chips,)),
        ],
        input_output_aliases=aliased,
        compiler_params=params(),
        cost_estimate=cost(
            12 * rows * width * hidden, 20 * rows * width + 8 * width * hidden, rows * hidden
        ),
    )(chip, normed, grad, *in_hbm(sources), *(acc if has_acc else []))


def place_attention_kernel(places, n_sources, chip_ref, core_ref, *refs):
    sources, refs = refs[:n_sources], refs[n_sources:]
    qkv_ref, out_ref, held, sems = refs
    half = n_sources // 2
    copies = []
    for which, core in enumerate((core_ref[0], 1 - core_ref[0])):
        copies += attention_copies(
            chip_ref[which], sources[which * half : (which + 1) * half], places, held.at[core]
        )
    for copy in start_all(copies, sems):
        copy.wait()
    columns = held.shape[3]
    for c in range(3):
        qkv_ref[c] = jnp.concatenate([held[0, c], held[1, c]], axis=-1).astype(F32)
    for core in range(2):
        out_ref[core * columns : (core + 1) * columns, :] = held[core, 3].astype(F32).T


def place_attention(chip, core, sources, places, width):
    columns = sources[0].shape[-1]
    n_sources = len(sources)
    return pl.pallas_call(
        functools.partial(place_attention_kernel, places, n_sources),
        in_specs=[IN_SMEM, IN_SMEM] + [IN_HBM] * n_sources,
        out_specs=[IN_VMEM] * 2,
        out_shape=[
            jax.ShapeDtypeStruct((3, width, 2 * columns), F32),
            jax.ShapeDtypeStruct((2 * columns, width), F32),
        ],
        scratch_shapes=[
            pltpu.VMEM((2, 4, width, columns), BF16),
            pltpu.SemaphoreType.DMA((2 * lax.axis_size("seq"),)),
        ],
        compiler_params=params(),
        cost_estimate=cost(0, 48 * width * columns),
    )(chip, core, *in_hbm(sources))


def place_mlp_kernel(places, order, n_sources, chip_ref, core_ref, *refs):
    sources, refs = refs[:n_sources], refs[n_sources:]
    out_ref, up_held, down_held, out_held, sems, out_sems = refs
    core = core_ref[0]
    hidden, width = up_held.shape[1:]
    half = n_sources // 2
    copies = []
    for which in range(2):
        targets = (up_held.at[which], down_held.at[which])
        copies += mlp_copies(
            chip_ref[which],
            sources[which * half : (which + 1) * half],
            places,
            order,
            targets,
            False,
        )
    copies = start_all(copies, sems)
    depth = hidden // len(order)
    tiles = width // LANES
    size = depth * 2 * tiles
    moved = []
    for which in range(2):
        for at, index in enumerate(order):
            base = len(moved)
            for side, part in enumerate((up_held, down_held)):
                copies[2 * base + side].wait()
                rows = part[which, at * depth : (at + 1) * depth, :].astype(F32)
                for tile in range(tiles):
                    out_held[pl.ds(base * size + 2 * tile + side, depth, stride=2 * tiles), :] = (
                        rows[:, tile * LANES : (tile + 1) * LANES]
                    )
            block = ((core if which == 0 else 1 - core) * len(order) + (chip_ref[which] ^ index)) * size
            copy = pltpu.make_async_copy(
                out_held.at[pl.ds(base * size, size), :],
                out_ref.at[pl.ds(pl.multiple_of(block, size), size), :],
                out_sems.at[base],
            )
            copy.start()
            moved.append(copy)
    for copy in moved:
        copy.wait()


def place_mlp(chip, core, sources, places, order, hidden):
    width = sources[0].shape[-1]
    n_sources = len(sources)
    tiles = width // LANES
    chips = len(order)
    rows = pl.pallas_call(
        functools.partial(place_mlp_kernel, places, order, n_sources),
        in_specs=[IN_SMEM, IN_SMEM] + [IN_HBM] * n_sources,
        out_specs=IN_HBM,
        out_shape=jax.ShapeDtypeStruct((hidden * 2 * tiles, LANES), F32),
        scratch_shapes=[
            pltpu.VMEM((2, hidden // 2, width), BF16),
            pltpu.VMEM((2, hidden // 2, width), BF16),
            pltpu.VMEM((hidden * 2 * tiles, LANES), F32),
            pltpu.SemaphoreType.DMA((4 * chips,)),
            pltpu.SemaphoreType.DMA((2 * chips,)),
        ],
        compiler_params=params(),
        cost_estimate=cost(0, 12 * hidden * width),
    )(chip, core, *in_hbm(sources))
    shaped = rows.reshape(hidden, tiles, 2, LANES)
    return shaped.transpose(0, 2, 1, 3).reshape(hidden, 2, width)


def rms_scale(values):
    return lax.rsqrt(jnp.mean(values * values, axis=-1, keepdims=True) + EPSILON)


def norm_back(grad_normed, unit_rows, scale, gain):
    scaled = gain * grad_normed
    return scale * (scaled - unit_rows * jnp.mean(unit_rows * scaled, axis=-1, keepdims=True))


def pack(first_longer, got):
    ranks, held, slots, width = got.shape
    longer = jnp.where(first_longer, got[:, 0], got[:, 1])
    shorter = jnp.where(first_longer, got[: ranks // 2, 1], got[: ranks // 2, 0])
    return jnp.concatenate(
        [longer.reshape(ranks * slots, width), shorter.reshape(ranks * slots // 2, width)]
    )


def unpack(first_longer, packed, ranks):
    rows, width = packed.shape
    half = rows // 3
    longer = packed[: 2 * half]
    shorter = jnp.concatenate([packed[2 * half :], jnp.zeros((half, width), packed.dtype)])
    both = jnp.stack(
        [
            jnp.where(first_longer, longer, shorter),
            jnp.where(first_longer, shorter, longer),
        ]
    )
    return both.reshape(1, 2, ranks, 2 * half // ranks, width)


def on_device(tokens, cotangent, lengths, routed, gain_attn, gain_mlp, router, w_qkv, w_out, w_mlp):
    group, span, width = tokens.shape
    slots = routed.shape[1]
    ranks = lax.axis_size("seq")
    count = lax.axis_size("mp")
    held = group // ranks
    chips = ranks // 2
    columns = w_qkv.shape[2] // 2
    hidden = w_mlp.shape[0] // 2
    me = lax.axis_index("seq").astype(jnp.int32)
    core = me % 2
    turned = reversed_bits(me // 2, chips)
    chip = jnp.where(core == 0, me // 2, turned)
    chip_array, core_array = chip[None], core[None]
    both_chips = jnp.stack([chip, jnp.where(core == 0, turned, me // 2)])
    whole, shared = exchange_plan(chips, False), exchange_plan(chips, True)
    whole_places, shared_places = gather_places(whole), gather_places(shared)
    whole_order, shared_order = scatter_order(whole), scatter_order(shared)
    pipe = Pipe()

    attn_shards, mlp_shards = {}, {}
    own_attn = jnp.concatenate([w_qkv, w_out.T[None]])
    own_attn = lax.dynamic_slice_in_dim(own_attn, core * columns, columns, 2)
    attn_shards[0] = [own_attn]

    def pieces_of(part, axis, plan):
        size = part.shape[axis] // chips
        return jnp.stack(
            [
                lax.dynamic_slice_in_dim(part, (chip ^ i) * size, size, axis)
                for i in combos(plan[1])
            ]
        )

    piece = pieces_of(own_attn, 1, shared)
    near, far = list(range(1, count // 2 + 1)), list(range(count - 1, count // 2, -1))
    for turn, ks in ((1, near), (-1, far)):
        pipe.launch(weights_chain(pipe, piece, turn, ks, shared, attn_shards.__setitem__))

    slot = lax.broadcasted_iota(jnp.int32, routed.shape, 1)
    live = me * slots + slot < (lengths // 8)[:, None]
    place = jnp.where(live, slot * 8 + routed % 8, -1)
    pair = lax.dynamic_slice_in_dim(lengths, me * held, held, 0)
    first_longer = pair[0] >= pair[1]
    rows = {}

    def to_holder(value, name):
        value = value.reshape(ranks, held, slots, width)
        got = yield [lax.all_to_all(value, "seq", split_axis=0, concat_axis=0, tiled=True)], 1
        rows[name] = pack(first_longer, got[0]).astype(F32)

    def to_position(value, name):
        value = unpack(first_longer, value, ranks)
        got = yield [lax.all_to_all(value, "seq", split_axis=2, concat_axis=0, tiled=True)], 1
        rows[name] = got[0].reshape(group, slots, width)

    def both_cores(value):
        return jnp.concatenate([value, other_core(value)])

    pipe.launch(to_holder(select_rows(place, tokens), "picked"))
    own_mlp = lax.dynamic_slice_in_dim(w_mlp, core * hidden, hidden, 0)
    own_up, own_down = own_mlp[:, 0, :], own_mlp[:, 1, :]
    chosen_grad, cotangent, own_up, own_down = pipe.step(
        (select_rows(place, cotangent), cotangent, own_up, own_down)
    )
    piece = jnp.stack([pieces_of(part, 0, whole) for part in (own_up, own_down)], axis=1)

    picked = rows["picked"]
    scale_one = rms_scale(picked)
    unit_one = picked * scale_one
    normed_one = both_cores((unit_one * gain_attn).astype(BF16))
    gate = jax.nn.sigmoid(jnp.sum(picked * router, axis=-1, keepdims=True))
    mlp_shards[0] = [own_up, own_down]
    saved, grad_feed = {}, None
    fetched = [[0]] + [[k, count - k] if count - k > k else [k] for k in near]
    for at, batch in enumerate(fetched):
        while not all(k in attn_shards for k in batch):
            normed_one = pipe.step(normed_one)
        outs = []
        for k in batch:
            final = k == fetched[-1][-1]
            before = list(saved) if final else []
            shards = [attn_shards[other] for other in before] + [attn_shards[k]]
            mixed = [saved[other][1] for other in before]
            out = attention_forward(chip_array, normed_one, shards, shared_places, mixed)
            saved[k] = out[:3]
            outs.append(out)
        if at == 0:
            outs, piece, chosen_grad, normed_one = pipe.step((outs, piece, chosen_grad, normed_one))
            for turn, ks in ((1, near), (-1, far)):
                pipe.launch(weights_chain(pipe, piece, turn, ks, whole, mlp_shards.__setitem__))
            pipe.launch(to_holder(chosen_grad, "grads"))
        elif at == len(fetched) - 1:
            grad_feed = both_cores((gate * rows["grads"]).astype(BF16))
            outs, grad_feed = pipe.step((outs, grad_feed))
        else:
            outs, normed_one = pipe.step((outs, normed_one))
        for k, out in zip(batch, outs):
            saved[k] = out[:3]
    attended, sent = outs[-1][3:]
    grad_rows = rows["grads"]
    attended = attended + other_core(sent).astype(F32)
    middle = picked + attended
    scale_two = rms_scale(middle)
    unit_two = middle * scale_two
    normed_two = both_cores((unit_two * gain_mlp).astype(BF16))

    sums, done = None, {}
    mlp_sums = Collect(pipe, count, whole, functools.partial(done.__setitem__, "mlp"))
    attn_sums = CollectBothWays(pipe, count, shared, functools.partial(done.__setitem__, "attn"))
    for k in range(count):
        while k not in mlp_shards:
            normed_two = pipe.step(normed_two)
        out = mlp(
            chip_array,
            normed_two,
            grad_feed,
            mlp_shards[k],
            hidden,
            whole_places,
            whole_order,
            sums,
            k == count - 1,
        )
        out = pipe.step(out)
        sums = out[:-2]
        pipe.launch(scatter_chain(*out[-2:], whole, functools.partial(mlp_sums.ready, k), 0 if k else DELAY))
    grad_normed_two = sums[2] + other_core(sums[3]).astype(F32)
    feed = sums[0] + other_core(sums[1]).astype(F32)
    grad_middle = norm_back(grad_normed_two, unit_two, scale_two, gain_mlp)
    grad_attended = both_cores((gate * grad_rows + grad_middle).astype(BF16))
    delta = attended + feed
    returned = (gate * delta).astype(BF16)
    grad_logit = jnp.sum(grad_rows * delta, axis=-1, keepdims=True) * gate * (1.0 - gate)
    router_part = jnp.sum(grad_logit * picked, axis=0)
    mlp_gain_part = jnp.sum(grad_normed_two * unit_two, axis=0)

    grad_sum = None
    for at, k in enumerate(far[::-1] + near[::-1] + [0]):
        out = attention_backward(
            chip_array,
            grad_attended,
            normed_one,
            saved[k],
            attn_shards[k],
            shared_places,
            shared_order,
            grad_sum,
            at == count - 1,
        )
        out = pipe.step(out)
        grad_sum = out[0]
        if at == count - 1:
            other = other_core(out[1])
        pipe.launch(scatter_chain(*out[-2:], shared, functools.partial(attn_sums.ready, k)))
        if at == max(0, count - 2):
            pipe.launch(to_position(returned, "out"))
    grad_normed_one = grad_sum + other.astype(F32)
    attn_gain_part = jnp.sum(grad_normed_one * unit_one, axis=0)
    small = sum_axis(jnp.stack([attn_gain_part, mlp_gain_part, router_part]), "seq", [1])
    small = sum_axis(small, "seq", bits_of(ranks, 1))
    grad_picked = (
        grad_middle
        + norm_back(grad_normed_one, unit_one, scale_one, gain_attn)
        + grad_logit * router
    ).astype(BF16)
    layer_out = add_rows(place, tokens, rows["out"])
    grad_picked, layer_out, small = lax.optimization_barrier((grad_picked, layer_out, small))
    pipe.launch(to_position(grad_picked, "back"))
    pipe.drain()
    grad_mlp = place_mlp(both_chips, core_array, done["mlp"], whole_places, whole_order, 2 * hidden)
    last_bits = bits_of(count, 0)
    small = sum_axis(small, "mp", last_bits[:1])
    back, grad_mlp, small = lax.optimization_barrier((rows["back"], grad_mlp, small))
    small = sum_axis(small, "mp", last_bits[1:])
    back, small = lax.optimization_barrier((back, small))
    grad_tokens = add_rows(place, cotangent, back)
    grad_qkv, grad_out = place_attention(
        both_chips, core_array, done["attn"], shared_places, width
    )
    return (
        layer_out,
        grad_tokens,
        small[0],
        small[1],
        small[2],
        grad_qkv,
        grad_out,
        grad_mlp,
    )


def solution(mesh):
    placed = (
        P("mp", "seq", None),
        P("mp", "seq", None),
        P("mp"),
        P("mp", "seq"),
        P(),
        P(),
        P(),
        P(None, None, "mp"),
        P("mp", None),
        P("mp", None, None),
    )
    return jax.shard_map(
        on_device,
        mesh=mesh,
        in_specs=placed,
        out_specs=(
            P("mp", "seq", None),
            P("mp", "seq", None),
            P(),
            P(),
            P(),
            P(None, None, "mp"),
            P("mp", None),
            P("mp", None, None),
        ),
        check_vma=False,
    )
```

```python
import functools

import jax
import jax.numpy as jnp
from jax import lax
from jax.experimental import pallas as pl
from jax.experimental.pallas import tpu as pltpu
from jax.sharding import PartitionSpec as P

HEAD = 64
LANES = 128
EPSILON = 1e-06
NEGATIVE = -1e30
ROOT = 0.7978845608028654
CUBE = 0.044715
SCALE = HEAD**-0.5
LAST = 1
DELAY = 5
F32 = jnp.float32
BF16 = jnp.bfloat16
VMEM_BYTES = 32 * 1024 * 1024

NN = (((1,), (0,)), ((), ()))
NT = (((1,), (1,)), ((), ()))
TN = (((0,), (0,)), ((), ()))

IN_HBM = pl.BlockSpec(memory_space=pltpu.HBM)
IN_VMEM = pl.BlockSpec(memory_space=pltpu.VMEM)
IN_SMEM = pl.BlockSpec(memory_space=pltpu.SMEM)


def mm(left, right, dims):
    return lax.dot_general(left, right, dims, preferred_element_type=F32)


def cost(flops, bytes_accessed, transcendentals=0):
    return pl.CostEstimate(
        flops=int(flops), bytes_accessed=int(bytes_accessed), transcendentals=int(transcendentals)
    )


def in_hbm(arrays):
    return [pltpu.with_memory_space_constraint(array, pltpu.HBM) for array in arrays]


def params(semantics=None):
    return pltpu.CompilerParams(dimension_semantics=semantics, vmem_limit_bytes=VMEM_BYTES)


def combos(bits):
    found = [0]
    for bit in bits:
        found = [i | extra for i in found for extra in (0, 1 << bit)]
    return found


def exchange_plan(chips, shared):
    bits = list(range(chips.bit_length() - 1))
    return (bits[: len(bits) // 2], bits[len(bits) // 2 :]) if shared else (bits, [])


def reversed_bits(chip, chips):
    count = chips.bit_length() - 1
    return sum(((chip >> bit) & 1) << (count - 1 - bit) for bit in range(count))


def across(value, bit):
    ranks = lax.axis_size("seq")
    last = (ranks // 2).bit_length() - 2
    pairs = [(i, i ^ (2 << (last - bit if i % 2 else bit))) for i in range(ranks)]
    return lax.ppermute(value, "seq", pairs)


def other_core(value):
    ranks = lax.axis_size("seq")
    return lax.ppermute(value, "seq", [(i, i ^ 1) for i in range(ranks)])


def ring(value, turn=1):
    depth = lax.axis_size("mp")
    cycle = [0] + list(range(1, depth, 2)) + list(range(2, depth, 2))[::-1]
    pairs = [(cycle[i], cycle[(i + turn) % depth]) for i in range(depth)]
    return lax.ppermute(value, "mp", pairs)


def joined(arrays):
    return arrays[0] if len(arrays) == 1 else jnp.concatenate(arrays, axis=0)


def gather_places(plan):
    bits, kept = plan
    held = [combos(kept)]
    for bit in bits:
        flat = [i for part in held for i in part]
        held = [flat, [i | (1 << bit) for i in flat]]
    return held


def scatter_order(plan):
    return combos(plan[0] + plan[1])


def added(*parts):
    total = parts[0].astype(F32)
    for part in parts[1:]:
        total = total + part.astype(F32)
    return total.astype(BF16)


def swapped(value, at, count):
    shape = value.shape
    parts = value.reshape((2**at, 2, 2 ** (count - at - 1)) + shape[1:])
    return jnp.concatenate([parts[:, 1:], parts[:, :1]], axis=1).reshape(shape)


class Pipe:
    def __init__(self):
        self.slot = 0
        self.flights = []

    def launch(self, chain):
        self.advance(chain, None)

    def advance(self, chain, got):
        try:
            arrays, slots = chain.send(got)
        except StopIteration:
            return
        self.flights.append((chain, arrays, self.slot + slots))

    def step(self, outs):
        self.slot += 1
        due = [f for f in self.flights if f[2] <= self.slot]
        self.flights = [f for f in self.flights if f[2] > self.slot]
        outs, got = lax.optimization_barrier((outs, [f[1] for f in due]))
        for flight, arrays in zip(due, got):
            self.advance(flight[0], arrays)
        return outs

    def drain(self):
        while self.flights:
            due, self.flights = self.flights, []
            self.slot = max(self.slot, min(f[2] for f in due))
            for flight in due:
                self.advance(flight[0], flight[1])


def gather_chain(piece, plan, done, last=1, pause=0):
    held = [piece]
    for at, bit in enumerate(plan[0]):
        if at and pause:
            yield [], pause
        whole = joined(held)
        (got,) = yield [across(whole, bit)], (last if at == len(plan[0]) - 1 else 1)
        held = [whole, got]
    done(held)


def weights_chain(pipe, piece, turn, shards, plan, done, first=1):
    for at, k in enumerate(shards):
        (piece,) = yield [ring(piece, turn)], (1 if at else first)
        pipe.launch(gather_chain(piece, plan, functools.partial(done, k), 1, int(turn < 0)))


def scatter_chain(low, high, plan, done, wait=0):
    if wait:
        low, high = yield [low, high], wait
    lows = [low]
    for at, bit in enumerate(plan[0]):
        (got,) = yield [across(high, bit)], 1
        lows = lows + [got]
        if at + 1 < len(plan[0]):
            half = got.shape[0] // 2
            high = added(*[part[half:] for part in lows])
            lows = [part[:half] for part in lows]
    done(lows)


class Collect:
    def __init__(self, pipe, count, plan, done):
        self.pipe, self.count, self.plan, self.done = pipe, count, plan, done
        self.parts, self.next, self.sums, self.busy = {}, 1 % count, None, False

    def ready(self, k, totals):
        self.parts[k] = totals
        self.go()

    def go(self):
        if self.busy or self.next is None or self.next not in self.parts:
            return
        parts = self.parts[self.next] + ([] if self.sums is None else [self.sums])
        self.sums = added(*parts)
        if self.next == 0:
            self.next = None
            self.finish(self.sums)
            return
        self.next = (self.next + 1) % self.count
        self.busy = True
        self.pipe.launch(self.hop())

    def hop(self):
        (self.sums,) = yield [ring(self.sums)], 1
        self.busy = False
        self.go()

    def finish(self, total):
        self.pipe.launch(self.spread(total))

    def spread(self, total):
        kept = self.plan[1]
        for at, bit in enumerate(kept):
            (got,) = yield [across(total, bit)], 1
            total = added(total, swapped(got, at, len(kept)))
        self.pipe.launch(gather_chain(total, self.plan, self.cores, 1 if kept else LAST))

    def cores(self, held):
        def chain():
            got = yield [other_core(part) for part in held], 1
            self.done(held + got)

        self.pipe.launch(chain())


class CollectBothWays(Collect):
    def __init__(self, pipe, count, plan, done):
        super().__init__(pipe, count, plan, done)
        half = count // 2
        self.ways = [[-1, list(range(half, 0, -1))], [1, list(range(half + 1, count))]]
        self.moving, self.arrived = [None, None], []

    def go(self):
        for way in range(2):
            turn, waiting = self.ways[way]
            if not waiting or waiting[0] not in self.parts or self.moving[way] == "busy":
                continue
            parts = self.parts[waiting.pop(0)]
            parts = parts if self.moving[way] is None else parts + [self.moving[way]]
            self.moving[way] = "busy"
            self.pipe.launch(self.travel(way, turn, parts))
        if not (self.ways[0][1] or self.ways[1][1]) and 0 in self.parts:
            if len(self.arrived) == sum(1 for w in (self.count // 2, self.count - self.count // 2 - 1) if w):
                if self.next is not None:
                    self.next = None
                    self.finish(added(*self.parts[0], *self.arrived))

    def travel(self, way, turn, parts):
        value = parts[0] if len(parts) == 1 else added(*parts)
        (value,) = yield [ring(value, turn)], 1 + way
        self.moving[way] = value
        if not self.ways[way][1]:
            self.arrived.append(value)
        self.go()


def sum_axis(value, axis, bits):
    size = lax.axis_size(axis)
    for first in range(0, len(bits), 2):
        now = bits[first : first + 2]
        offsets = [a ^ b for b in [0, *now[1:]] for a in (0, now[0])]
        parts = [value]
        parts += [lax.ppermute(value, axis, [(i, i ^ o) for i in range(size)]) for o in offsets[1:]]
        while len(parts) > 1:
            parts = [a + b for a, b in zip(parts[::2], parts[1::2])]
        value = parts[0]
    return value


def bits_of(size, first):
    return [1 << bit for bit in range(first, size.bit_length() - 1)]


def select_kernel(place_ref, base_ref, out_ref):
    span = base_ref.shape[1]
    for at in range(base_ref.shape[0]):
        place = place_ref[at]
        hot = lax.broadcasted_iota(jnp.int32, (place.shape[0], span), 1) == place
        out_ref[at] = mm(hot.astype(BF16), base_ref[at], NN).astype(BF16)


def together(group, span):
    size = max(1, min(group, 2048 // span))
    while group % size:
        size -= 1
    return size


def select_rows(place, base):
    group, span, width = base.shape
    slots = place.shape[1]
    size = together(group, span)
    return pl.pallas_call(
        select_kernel,
        grid=(group // size,),
        in_specs=[
            pl.BlockSpec((size, slots, 1), lambda g: (g, 0, 0)),
            pl.BlockSpec((size, span, width), lambda g: (g, 0, 0)),
        ],
        out_specs=pl.BlockSpec((size, slots, width), lambda g: (g, 0, 0)),
        out_shape=jax.ShapeDtypeStruct((group, slots, width), BF16),
        compiler_params=params(("arbitrary",)),
        cost_estimate=cost(2 * group * slots * span * width, 2 * group * (span + slots) * width),
    )(place[:, :, None], pltpu.with_memory_space_constraint(base, pltpu.HBM))


def add_kernel(place_ref, base_ref, rows_ref, out_ref):
    span = base_ref.shape[1]
    for at in range(base_ref.shape[0]):
        place = place_ref[at]
        hot = lax.broadcasted_iota(jnp.int32, (span, place.shape[1]), 0) == place
        moved = mm(hot.astype(BF16), rows_ref[at], NN)
        out_ref[at] = (base_ref[at].astype(F32) + moved).astype(BF16)


def add_rows(place, base, rows):
    group, span, width = base.shape
    slots = place.shape[1]
    size = together(group, span)
    block = pl.BlockSpec((size, span, width), lambda g: (g, 0, 0))
    return pl.pallas_call(
        add_kernel,
        grid=(group // size,),
        in_specs=[
            pl.BlockSpec((size, 1, slots), lambda g: (g, 0, 0)),
            block,
            pl.BlockSpec((size, slots, width), lambda g: (g, 0, 0)),
        ],
        out_specs=block,
        out_shape=jax.ShapeDtypeStruct(base.shape, BF16),
        compiler_params=params(("arbitrary",)),
        cost_estimate=cost(2 * group * slots * span * width, 4 * group * span * width),
    )(place[:, None, :], pltpu.with_memory_space_constraint(base, pltpu.HBM), rows)


def start_all(copies, sems):
    started = []
    for at, (source, target) in enumerate(copies):
        copy = pltpu.make_async_copy(source, target, sems.at[at])
        copy.start()
        started.append(copy)
    return started


def attention_copies(chip, sources, places, target, outward=False):
    if len(sources) == 1:
        return [(sources[0].at[3] if outward else sources[0], target)]
    depth = sources[0].shape[2]
    copies = []
    for source, ids in zip(sources, places):
        for at, index in enumerate(ids):
            rows = pl.ds(pl.multiple_of((chip ^ index) * depth, depth), depth)
            if outward:
                copies.append((source.at[at, 3], target.at[rows, :]))
            else:
                copies.append((source.at[at], target.at[:, rows, :]))
    return copies


def mlp_copies(chip, sources, places, order, targets, own):
    copies = []
    for place, index in enumerate(order):
        for side in range(2):
            target = targets[side]
            depth = target.shape[0] // len(order)
            if own:
                start = pl.multiple_of((chip ^ index) * depth, depth)
                source = sources[side].at[pl.ds(start, depth), :]
            else:
                for array, ids in zip(sources, places):
                    if index in ids:
                        source = array.at[ids.index(index), side]
            copies.append((source, target.at[pl.ds(place * depth, depth), :]))
    return copies


def row_blocks(rows):
    blocks = []
    for start in (0, rows // 2):
        half = rows // 6
        for first, last, low, high in ((0, 1, 0, 1), (1, 2, 0, 2), (2, 3, 2, 3)):
            blocks.append(tuple(start + half * at for at in (first, last, low, high)))
    return blocks


def causal(first, last, low, high):
    shape = (last - first, high - low)
    row = lax.broadcasted_iota(jnp.int32, shape, 0) + (first - low)
    return row >= lax.broadcasted_iota(jnp.int32, shape, 1)


def head_groups(columns):
    lanes = min(LANES, columns)
    return [
        (slice(at, at + lanes), at // HEAD, lanes // HEAD) for at in range(0, columns, lanes)
    ]


def own_lanes(value, side, heads):
    if heads == 1:
        return value
    lane = lax.broadcasted_iota(jnp.int32, (1, value.shape[1]), 1)
    mine = (lane >= HEAD) if side else (lane < HEAD)
    return jnp.where(mine, value, jnp.zeros_like(value))


def finish(total, last, outs):
    if not last:
        outs[0][...] = total
        return
    half = total.shape[0] // 2
    outs[0][...] = total[:half]
    outs[1][...] = total[half:].astype(BF16)


def sum_shapes(rows, width, last):
    if not last:
        return [jax.ShapeDtypeStruct((rows, width), F32)]
    return [
        jax.ShapeDtypeStruct((rows // 2, width), F32),
        jax.ShapeDtypeStruct((rows // 2, width), BF16),
    ]


def attention_forward_kernel(places, counts, chip_ref, normed_ref, *refs):
    sources = []
    for count in counts:
        sources.append(refs[:count])
        refs = refs[count:]
    others, refs = refs[: len(counts) - 1], refs[len(counts) - 1 :]
    heads_ref, mixed_ref, log_ref, *refs = refs
    sums, (held, *out_held, sems) = (refs[:2], refs[2:]) if len(counts) > 1 else ([], refs)
    chip = chip_ref[0]
    copies = attention_copies(chip, sources[-1], places, held)
    n_own = len(copies)
    for at, shard in enumerate(sources[:-1]):
        copies += attention_copies(chip, shard, places, out_held[0].at[at], True)
    copies = start_all(copies, sems)
    for copy in copies[:n_own]:
        copy.wait()
    rows = normed_ref.shape[0]
    columns = held.shape[2]
    heads_all = mm(normed_ref[...], jnp.concatenate([held[c] for c in range(3)], axis=-1), NN)
    for c in range(3):
        heads_ref[c] = heads_all[:, c * columns : (c + 1) * columns].astype(BF16)
    lane = lax.broadcasted_iota(jnp.int32, (1, LANES), 1)
    for first, end, low, high in row_blocks(rows):
        seen = causal(first, end, low, high)
        logs = jnp.zeros((end - first, LANES), F32)
        for lanes, head, heads in head_groups(columns):
            query = heads_ref[0, first:end, lanes]
            keys = heads_ref[1, low:high, lanes]
            values = heads_ref[2, low:high, lanes]
            out = None
            for side in range(heads):
                scores = mm(own_lanes(query, side, heads), keys, NT) * SCALE
                scores = jnp.where(seen, scores, NEGATIVE)
                peak = jnp.max(scores, axis=-1, keepdims=True)
                raised = jnp.exp(scores - peak)
                total = jnp.sum(raised, axis=-1, keepdims=True)
                weights = (raised * (1.0 / total)).astype(BF16)
                part = own_lanes(mm(weights, values, NN), side, heads)
                out = part if out is None else out + part
                logs = jnp.where(lane == head + side, peak + jnp.log(total), logs)
            mixed_ref[first:end, lanes] = out.astype(BF16)
        log_ref[first:end, :] = logs
    for copy in copies[n_own:]:
        copy.wait()
    if len(counts) > 1:
        mixed = [part[...] for part in others] + [mixed_ref[...]]
        outward = [out_held[0][at] for at in range(len(counts) - 1)] + [held[3]]
        attended = mm(
            jnp.concatenate(mixed, axis=-1), jnp.concatenate(outward, axis=-1), NT
        )
        finish(attended, True, sums)


def attention_forward(chip, normed, shards, places, mixed):
    rows, width = normed.shape
    columns = shards[0][0].shape[-1]
    counts = [len(shard) for shard in shards]
    last = len(shards) > 1
    sources = [source for shard in shards for source in shard]
    chips = lax.axis_size("seq") // 2
    flops = 2 * rows * width * columns * (3 + last * len(shards)) + rows * rows * columns
    scratch = [pltpu.VMEM((4, width, columns), BF16)]
    if last:
        scratch.append(pltpu.VMEM((len(shards) - 1, width, columns), BF16))
    return pl.pallas_call(
        functools.partial(attention_forward_kernel, places, counts),
        in_specs=[IN_SMEM, IN_VMEM] + [IN_HBM] * len(sources) + [IN_VMEM] * len(mixed),
        out_specs=[IN_VMEM] * (3 + 2 * last),
        out_shape=[
            jax.ShapeDtypeStruct((3, rows, columns), BF16),
            jax.ShapeDtypeStruct((rows, columns), BF16),
            jax.ShapeDtypeStruct((rows, LANES), F32),
        ]
        + (sum_shapes(rows, width, True) if last else []),
        scratch_shapes=scratch + [pltpu.SemaphoreType.DMA((chips * len(shards),))],
        compiler_params=params(),
        cost_estimate=cost(flops, 2 * rows * width + 8 * width * columns, rows * rows * 2),
    )(chip, normed, *in_hbm(sources), *mixed)


def attention_backward_kernel(
    places,
    order,
    n_sources,
    has_acc,
    last,
    chip_ref,
    grad_ref,
    normed_ref,
    heads_ref,
    mixed_ref,
    log_ref,
    *refs,
):
    sources, refs = refs[:n_sources], refs[n_sources:]
    if has_acc:
        acc_ref, refs = refs[0], refs[1:]
    sums, refs = refs[: 1 + last], refs[1 + last :]
    outs, refs = refs[:2], refs[2:]
    held, grad_held, grad_heads, sems, out_sems = refs
    chip = chip_ref[0]
    copies = start_all(attention_copies(chip, sources, places, held), sems)
    rows = normed_ref.shape[0]
    width = held.shape[2]
    depth = outs[0].shape[2]
    grad_held[3] = mm(mixed_ref[...], grad_ref[...], TN).astype(BF16).T
    for copy in copies:
        copy.wait()
    grad_mixed = mm(grad_ref[...], held[3], NN).astype(BF16)
    lane = lax.broadcasted_iota(jnp.int32, (1, LANES), 1)
    for lanes, head, heads in head_groups(width):
        key_parts, value_parts = [], []
        for first, end, low, high in row_blocks(rows):
            query = heads_ref[0, first:end, lanes]
            keys = heads_ref[1, low:high, lanes]
            values = heads_ref[2, low:high, lanes]
            grad_out = grad_mixed[first:end, lanes]
            logs = log_ref[first:end, :]
            seen = causal(first, end, low, high)
            grad_query = grad_keys = grad_values = None
            for side in range(heads):
                own_query = own_lanes(query, side, heads)
                own_grad = own_lanes(grad_out, side, heads)
                log_total = jnp.sum(
                    jnp.where(lane == head + side, logs, 0.0), axis=-1, keepdims=True
                )
                scores = jnp.where(seen, mm(own_query, keys, NT) * SCALE, NEGATIVE)
                shares = jnp.exp(scores - log_total)
                grad_weights = mm(own_grad, values, NT)
                inner = jnp.sum(shares * grad_weights, axis=-1, keepdims=True)
                grad_scores = (shares * (grad_weights - inner)).astype(BF16)
                weights = shares.astype(BF16)
                part_query = own_lanes(mm(grad_scores, keys, NN), side, heads)
                part_keys = mm(grad_scores, own_query, TN)
                part_values = mm(weights, own_grad, TN)
                if side == 0:
                    grad_query, grad_keys, grad_values = part_query, part_keys, part_values
                else:
                    grad_query = grad_query + part_query
                    grad_keys = grad_keys + part_keys
                    grad_values = grad_values + part_values
            grad_heads[0, first:end, lanes] = (grad_query * SCALE).astype(BF16)
            key_parts.append(grad_keys)
            value_parts.append(grad_values)
        half = rows // 6
        for c, parts, scale in ((1, key_parts, SCALE), (2, value_parts, 1.0)):
            for pair in range(2):
                one, two, three = parts[3 * pair : 3 * pair + 3]
                for at, value in enumerate((one + two[:half], two[half:], three)):
                    start = (3 * pair + at) * half
                    grad_heads[c, start : start + half, lanes] = (value * scale).astype(BF16)
    grad_all = jnp.concatenate([grad_heads[c] for c in range(3)], axis=-1)
    grad_qkv = mm(grad_all, normed_ref[...], TN).astype(BF16)
    for c in range(3):
        grad_held[c] = grad_qkv[c * width : (c + 1) * width].T
    copies = []
    for at, index in enumerate(order):
        start = pl.multiple_of((chip ^ index) * depth, depth)
        high, at = divmod(at, len(order) // 2)
        copies.append((grad_held.at[:, pl.ds(start, depth), :], outs[high].at[at]))
    copies = start_all(copies, out_sems)
    grad_normed = mm(grad_all, jnp.concatenate([held[c] for c in range(3)], axis=-1), NT)
    if has_acc:
        grad_normed = grad_normed + acc_ref[...]
    finish(grad_normed, last, sums)
    for copy in copies:
        copy.wait()


def attention_backward(chip, grad, normed, saved, sources, places, order, acc, last):
    rows, width = normed.shape
    columns = sources[0].shape[-1]
    chips = lax.axis_size("seq") // 2
    has_acc = acc is not None
    n_sources = len(sources)
    n_copies = 1 if n_sources == 1 else chips
    piece = jax.ShapeDtypeStruct((chips // 2, 4, width // chips, columns), BF16)
    flops = 2 * rows * width * columns * 8 + 3 * rows * rows * columns
    return pl.pallas_call(
        functools.partial(
            attention_backward_kernel, places, order, n_sources, has_acc, last
        ),
        in_specs=[IN_SMEM] + [IN_VMEM] * 5 + [IN_HBM] * n_sources + [IN_VMEM] * has_acc,
        out_specs=[IN_VMEM] * (1 + last) + [IN_HBM] * 2,
        out_shape=sum_shapes(rows, width, last) + [piece] * 2,
        scratch_shapes=[
            pltpu.VMEM((4, width, columns), BF16),
            pltpu.VMEM((4, width, columns), BF16),
            pltpu.VMEM((3, rows, columns), BF16),
            pltpu.SemaphoreType.DMA((n_copies,)),
            pltpu.SemaphoreType.DMA((chips,)),
        ],
        input_output_aliases={6 + n_sources: 0} if has_acc and not last else {},
        compiler_params=params(),
        cost_estimate=cost(flops, 12 * rows * width + 16 * width * columns, rows * rows * 2),
    )(chip, grad, normed, *saved, *in_hbm(sources), *([acc] if has_acc else []))


def mlp_kernel(places, order, n_sources, has_acc, last, chip_ref, normed_ref, grad_ref, *refs):
    sources, refs = refs[:n_sources], refs[n_sources:]
    if has_acc:
        acc_in, refs = refs[:2], refs[2:]
    sums, refs = refs[: 2 + 2 * last], refs[2 + 2 * last :]
    outs, refs = refs[:2], refs[2:]
    up_held, down_held, up_grad, down_grad, active_held, upward_held, sems, out_sems = refs
    own = not has_acc
    copies = mlp_copies(chip_ref[0], sources, places, order, (up_held, down_held), own)
    copies = start_all(copies, sems)
    hidden = up_held.shape[0]
    depth = hidden // len(order)
    step = max(depth, min(256, hidden))
    waited = 0
    leaving = []
    for start in range(0, hidden, step):
        ready = 2 * ((start + step) // depth)
        for copy in copies[waited:ready]:
            copy.wait()
        waited = ready
        chunk = slice(start, start + step)
        upward = mm(normed_ref[...], up_held[chunk], NT)
        square = upward * upward
        bent = jnp.tanh(ROOT * upward * (1.0 + CUBE * square))
        active = (0.5 * upward * (1.0 + bent)).astype(BF16)
        slope = 0.5 * (1.0 + bent) + 0.5 * ROOT * upward * (1.0 - bent * bent) * (
            1.0 + 3.0 * CUBE * square
        )
        grad_active = mm(grad_ref[...], down_held[chunk], NT)
        grad_upward = (grad_active * slope).astype(BF16)
        active_held[:, chunk] = active
        upward_held[:, chunk] = grad_upward
        up_grad[chunk] = mm(grad_upward, normed_ref[...], TN).astype(BF16)
        down_grad[chunk] = mm(active, grad_ref[...], TN).astype(BF16)
        for at in range(start // depth, (start + step) // depth):
            for side, grads in enumerate((up_grad, down_grad)):
                high, place = divmod(at, len(order) // 2)
                copy = pltpu.make_async_copy(
                    grads.at[pl.ds(at * depth, depth), :],
                    outs[high].at[place, side],
                    out_sems.at[2 * at + side],
                )
                copy.start()
                leaving.append(copy)
    for i, (left, right) in enumerate(((active_held, down_held), (upward_held, up_held))):
        total = mm(left[...], right[...], NN)
        if has_acc:
            total = total + acc_in[i][...]
        finish(total, last, sums[i * (1 + last) : (i + 1) * (1 + last)])
    for copy in leaving:
        copy.wait()


def mlp(chip, normed, grad, sources, hidden, places, order, acc, last):
    rows, width = normed.shape
    chips = len(order)
    depth = hidden // chips
    has_acc = acc is not None
    n_sources = len(sources)
    piece = jax.ShapeDtypeStruct((chips // 2, 2, depth, width), BF16)
    aliased = {3 + n_sources: 0, 4 + n_sources: 1} if has_acc and not last else {}
    return pl.pallas_call(
        functools.partial(mlp_kernel, places, order, n_sources, has_acc, last),
        in_specs=[IN_SMEM] + [IN_VMEM] * 2 + [IN_HBM] * n_sources + [IN_VMEM] * (2 * has_acc),
        out_specs=[IN_VMEM] * (2 + 2 * last) + [IN_HBM] * 2,
        out_shape=sum_shapes(rows, width, last) * 2 + [piece] * 2,
        scratch_shapes=[pltpu.VMEM((hidden, width), BF16)] * 4
        + [pltpu.VMEM((rows, hidden), BF16)] * 2
        + [
            pltpu.SemaphoreType.DMA((2 * chips,)),
            pltpu.SemaphoreType.DMA((2 * chips,)),
        ],
        input_output_aliases=aliased,
        compiler_params=params(),
        cost_estimate=cost(
            12 * rows * width * hidden, 20 * rows * width + 8 * width * hidden, rows * hidden
        ),
    )(chip, normed, grad, *in_hbm(sources), *(acc if has_acc else []))


def place_attention_kernel(places, n_sources, chip_ref, core_ref, *refs):
    sources, refs = refs[:n_sources], refs[n_sources:]
    qkv_ref, out_ref, held, sems = refs
    half = n_sources // 2
    copies = []
    for which, core in enumerate((core_ref[0], 1 - core_ref[0])):
        copies += attention_copies(
            chip_ref[which], sources[which * half : (which + 1) * half], places, held.at[core]
        )
    for copy in start_all(copies, sems):
        copy.wait()
    columns = held.shape[3]
    for c in range(3):
        qkv_ref[c] = jnp.concatenate([held[0, c], held[1, c]], axis=-1).astype(F32)
    for core in range(2):
        out_ref[core * columns : (core + 1) * columns, :] = held[core, 3].astype(F32).T


def place_attention(chip, core, sources, places, width):
    columns = sources[0].shape[-1]
    n_sources = len(sources)
    return pl.pallas_call(
        functools.partial(place_attention_kernel, places, n_sources),
        in_specs=[IN_SMEM, IN_SMEM] + [IN_HBM] * n_sources,
        out_specs=[IN_VMEM] * 2,
        out_shape=[
            jax.ShapeDtypeStruct((3, width, 2 * columns), F32),
            jax.ShapeDtypeStruct((2 * columns, width), F32),
        ],
        scratch_shapes=[
            pltpu.VMEM((2, 4, width, columns), BF16),
            pltpu.SemaphoreType.DMA((2 * lax.axis_size("seq"),)),
        ],
        compiler_params=params(),
        cost_estimate=cost(0, 48 * width * columns),
    )(chip, core, *in_hbm(sources))


def place_mlp_kernel(places, order, n_sources, chip_ref, core_ref, *refs):
    sources, refs = refs[:n_sources], refs[n_sources:]
    out_ref, up_held, down_held, out_held, sems, out_sems = refs
    core = core_ref[0]
    hidden, width = up_held.shape[1:]
    half = n_sources // 2
    copies = []
    for which in range(2):
        targets = (up_held.at[which], down_held.at[which])
        copies += mlp_copies(
            chip_ref[which],
            sources[which * half : (which + 1) * half],
            places,
            order,
            targets,
            False,
        )
    copies = start_all(copies, sems)
    depth = hidden // len(order)
    tiles = width // LANES
    size = depth * 2 * tiles
    moved = []
    for which in range(2):
        for at, index in enumerate(order):
            base = len(moved)
            for side, part in enumerate((up_held, down_held)):
                copies[2 * base + side].wait()
                rows = part[which, at * depth : (at + 1) * depth, :].astype(F32)
                for tile in range(tiles):
                    out_held[pl.ds(base * size + 2 * tile + side, depth, stride=2 * tiles), :] = (
                        rows[:, tile * LANES : (tile + 1) * LANES]
                    )
            block = ((core if which == 0 else 1 - core) * len(order) + (chip_ref[which] ^ index)) * size
            copy = pltpu.make_async_copy(
                out_held.at[pl.ds(base * size, size), :],
                out_ref.at[pl.ds(pl.multiple_of(block, size), size), :],
                out_sems.at[base],
            )
            copy.start()
            moved.append(copy)
    for copy in moved:
        copy.wait()


def place_mlp(chip, core, sources, places, order, hidden):
    width = sources[0].shape[-1]
    n_sources = len(sources)
    tiles = width // LANES
    chips = len(order)
    rows = pl.pallas_call(
        functools.partial(place_mlp_kernel, places, order, n_sources),
        in_specs=[IN_SMEM, IN_SMEM] + [IN_HBM] * n_sources,
        out_specs=IN_HBM,
        out_shape=jax.ShapeDtypeStruct((hidden * 2 * tiles, LANES), F32),
        scratch_shapes=[
            pltpu.VMEM((2, hidden // 2, width), BF16),
            pltpu.VMEM((2, hidden // 2, width), BF16),
            pltpu.VMEM((hidden * 2 * tiles, LANES), F32),
            pltpu.SemaphoreType.DMA((4 * chips,)),
            pltpu.SemaphoreType.DMA((2 * chips,)),
        ],
        compiler_params=params(),
        cost_estimate=cost(0, 12 * hidden * width),
    )(chip, core, *in_hbm(sources))
    shaped = rows.reshape(hidden, tiles, 2, LANES)
    return shaped.transpose(0, 2, 1, 3).reshape(hidden, 2, width)


def rms_scale(values):
    return lax.rsqrt(jnp.mean(values * values, axis=-1, keepdims=True) + EPSILON)


def norm_back(grad_normed, unit_rows, scale, gain):
    scaled = gain * grad_normed
    return scale * (scaled - unit_rows * jnp.mean(unit_rows * scaled, axis=-1, keepdims=True))


def pack(first_longer, got):
    ranks, held, slots, width = got.shape
    longer = jnp.where(first_longer, got[:, 0], got[:, 1])
    shorter = jnp.where(first_longer, got[: ranks // 2, 1], got[: ranks // 2, 0])
    return jnp.concatenate(
        [longer.reshape(ranks * slots, width), shorter.reshape(ranks * slots // 2, width)]
    )


def unpack(first_longer, packed, ranks):
    rows, width = packed.shape
    half = rows // 3
    longer = packed[: 2 * half]
    shorter = jnp.concatenate([packed[2 * half :], jnp.zeros((half, width), packed.dtype)])
    both = jnp.stack(
        [
            jnp.where(first_longer, longer, shorter),
            jnp.where(first_longer, shorter, longer),
        ]
    )
    return both.reshape(1, 2, ranks, 2 * half // ranks, width)


def on_device(tokens, cotangent, lengths, routed, gain_attn, gain_mlp, router, w_qkv, w_out, w_mlp):
    group, span, width = tokens.shape
    slots = routed.shape[1]
    ranks = lax.axis_size("seq")
    count = lax.axis_size("mp")
    held = group // ranks
    chips = ranks // 2
    columns = w_qkv.shape[2] // 2
    hidden = w_mlp.shape[0] // 2
    me = lax.axis_index("seq").astype(jnp.int32)
    core = me % 2
    turned = reversed_bits(me // 2, chips)
    chip = jnp.where(core == 0, me // 2, turned)
    chip_array, core_array = chip[None], core[None]
    both_chips = jnp.stack([chip, jnp.where(core == 0, turned, me // 2)])
    whole, shared = exchange_plan(chips, False), exchange_plan(chips, True)
    whole_places, shared_places = gather_places(whole), gather_places(shared)
    whole_order, shared_order = scatter_order(whole), scatter_order(shared)
    pipe = Pipe()

    attn_shards, mlp_shards = {}, {}
    own_attn = jnp.concatenate([w_qkv, w_out.T[None]])
    own_attn = lax.dynamic_slice_in_dim(own_attn, core * columns, columns, 2)
    attn_shards[0] = [own_attn]

    def pieces_of(part, axis, plan):
        size = part.shape[axis] // chips
        return jnp.stack(
            [
                lax.dynamic_slice_in_dim(part, (chip ^ i) * size, size, axis)
                for i in combos(plan[1])
            ]
        )

    piece = pieces_of(own_attn, 1, shared)
    near, far = list(range(1, count // 2 + 1)), list(range(count - 1, count // 2, -1))
    for turn, ks in ((1, near), (-1, far)):
        pipe.launch(weights_chain(pipe, piece, turn, ks, shared, attn_shards.__setitem__))

    slot = lax.broadcasted_iota(jnp.int32, routed.shape, 1)
    live = me * slots + slot < (lengths // 8)[:, None]
    place = jnp.where(live, slot * 8 + routed % 8, -1)
    pair = lax.dynamic_slice_in_dim(lengths, me * held, held, 0)
    first_longer = pair[0] >= pair[1]
    rows = {}

    def to_holder(value, name):
        value = value.reshape(ranks, held, slots, width)
        got = yield [lax.all_to_all(value, "seq", split_axis=0, concat_axis=0, tiled=True)], 1
        rows[name] = pack(first_longer, got[0]).astype(F32)

    def to_position(value, name):
        value = unpack(first_longer, value, ranks)
        got = yield [lax.all_to_all(value, "seq", split_axis=2, concat_axis=0, tiled=True)], 1
        rows[name] = got[0].reshape(group, slots, width)

    def both_cores(value):
        return jnp.concatenate([value, other_core(value)])

    pipe.launch(to_holder(select_rows(place, tokens), "picked"))
    own_mlp = lax.dynamic_slice_in_dim(w_mlp, core * hidden, hidden, 0)
    own_up, own_down = own_mlp[:, 0, :], own_mlp[:, 1, :]
    chosen_grad, cotangent, own_up, own_down = pipe.step(
        (select_rows(place, cotangent), cotangent, own_up, own_down)
    )
    piece = jnp.stack([pieces_of(part, 0, whole) for part in (own_up, own_down)], axis=1)

    picked = rows["picked"]
    scale_one = rms_scale(picked)
    unit_one = picked * scale_one
    normed_one = both_cores((unit_one * gain_attn).astype(BF16))
    gate = jax.nn.sigmoid(jnp.sum(picked * router, axis=-1, keepdims=True))
    mlp_shards[0] = [own_up, own_down]
    saved, grad_feed = {}, None
    fetched = [[0]] + [[k, count - k] if count - k > k else [k] for k in near]
    for at, batch in enumerate(fetched):
        while not all(k in attn_shards for k in batch):
            normed_one = pipe.step(normed_one)
        outs = []
        for k in batch:
            final = k == fetched[-1][-1]
            before = list(saved) if final else []
            shards = [attn_shards[other] for other in before] + [attn_shards[k]]
            mixed = [saved[other][1] for other in before]
            out = attention_forward(chip_array, normed_one, shards, shared_places, mixed)
            saved[k] = out[:3]
            outs.append(out)
        if at == 0:
            outs, piece, chosen_grad, normed_one = pipe.step((outs, piece, chosen_grad, normed_one))
            for turn, ks in ((1, near), (-1, far)):
                pipe.launch(weights_chain(pipe, piece, turn, ks, whole, mlp_shards.__setitem__))
            pipe.launch(to_holder(chosen_grad, "grads"))
        elif at == len(fetched) - 1:
            grad_feed = both_cores((gate * rows["grads"]).astype(BF16))
            outs, grad_feed = pipe.step((outs, grad_feed))
        else:
            outs, normed_one = pipe.step((outs, normed_one))
        for k, out in zip(batch, outs):
            saved[k] = out[:3]
    attended, sent = outs[-1][3:]
    grad_rows = rows["grads"]
    attended = attended + other_core(sent).astype(F32)
    middle = picked + attended
    scale_two = rms_scale(middle)
    unit_two = middle * scale_two
    normed_two = both_cores((unit_two * gain_mlp).astype(BF16))

    sums, done = None, {}
    mlp_sums = Collect(pipe, count, whole, functools.partial(done.__setitem__, "mlp"))
    attn_sums = CollectBothWays(pipe, count, shared, functools.partial(done.__setitem__, "attn"))
    for k in range(count):
        while k not in mlp_shards:
            normed_two = pipe.step(normed_two)
        out = mlp(
            chip_array,
            normed_two,
            grad_feed,
            mlp_shards[k],
            hidden,
            whole_places,
            whole_order,
            sums,
            k == count - 1,
        )
        out = pipe.step(out)
        sums = out[:-2]
        pipe.launch(scatter_chain(*out[-2:], whole, functools.partial(mlp_sums.ready, k), 0 if k else DELAY))
    grad_normed_two = sums[2] + other_core(sums[3]).astype(F32)
    feed = sums[0] + other_core(sums[1]).astype(F32)
    grad_middle = norm_back(grad_normed_two, unit_two, scale_two, gain_mlp)
    grad_attended = both_cores((gate * grad_rows + grad_middle).astype(BF16))
    delta = attended + feed
    returned = (gate * delta).astype(BF16)
    grad_logit = jnp.sum(grad_rows * delta, axis=-1, keepdims=True) * gate * (1.0 - gate)
    router_part = jnp.sum(grad_logit * picked, axis=0)
    mlp_gain_part = jnp.sum(grad_normed_two * unit_two, axis=0)

    grad_sum = None
    for at, k in enumerate(far[::-1] + near[::-1] + [0]):
        out = attention_backward(
            chip_array,
            grad_attended,
            normed_one,
            saved[k],
            attn_shards[k],
            shared_places,
            shared_order,
            grad_sum,
            at == count - 1,
        )
        out = pipe.step(out)
        grad_sum = out[0]
        if at == count - 1:
            other = other_core(out[1])
        pipe.launch(scatter_chain(*out[-2:], shared, functools.partial(attn_sums.ready, k)))
        if at == max(0, count - 2):
            pipe.launch(to_position(returned, "out"))
    grad_normed_one = grad_sum + other.astype(F32)
    attn_gain_part = jnp.sum(grad_normed_one * unit_one, axis=0)
    small = sum_axis(jnp.stack([attn_gain_part, mlp_gain_part, router_part]), "seq", [1])
    small = sum_axis(small, "seq", bits_of(ranks, 1))
    grad_picked = (
        grad_middle
        + norm_back(grad_normed_one, unit_one, scale_one, gain_attn)
        + grad_logit * router
    ).astype(BF16)
    layer_out = add_rows(place, tokens, rows["out"])
    grad_picked, layer_out, small = lax.optimization_barrier((grad_picked, layer_out, small))
    pipe.launch(to_position(grad_picked, "back"))
    pipe.drain()
    grad_mlp = place_mlp(both_chips, core_array, done["mlp"], whole_places, whole_order, 2 * hidden)
    last_bits = bits_of(count, 0)
    small = sum_axis(small, "mp", last_bits[:1])
    back, grad_mlp, small = lax.optimization_barrier((rows["back"], grad_mlp, small))
    small = sum_axis(small, "mp", last_bits[1:])
    back, small = lax.optimization_barrier((back, small))
    grad_tokens = add_rows(place, cotangent, back)
    grad_qkv, grad_out = place_attention(
        both_chips, core_array, done["attn"], shared_places, width
    )
    return (
        layer_out,
        grad_tokens,
        small[0],
        small[1],
        small[2],
        grad_qkv,
        grad_out,
        grad_mlp,
    )


def solution(mesh):
    placed = (
        P("mp", "seq", None),
        P("mp", "seq", None),
        P("mp"),
        P("mp", "seq"),
        P(),
        P(),
        P(),
        P(None, None, "mp"),
        P("mp", None),
        P("mp", None, None),
    )
    return jax.shard_map(
        on_device,
        mesh=mesh,
        in_specs=placed,
        out_specs=(
            P("mp", "seq", None),
            P("mp", "seq", None),
            P(),
            P(),
            P(),
            P(None, None, "mp"),
            P("mp", None),
            P("mp", None, None),
        ),
        check_vma=False,
    )
```

```python
import functools

import jax
import jax.numpy as jnp
from jax import lax
from jax.experimental import pallas as pl
from jax.experimental.pallas import tpu as pltpu
from jax.sharding import PartitionSpec as P

HEAD = 64
LANES = 128
EPSILON = 1e-06
NEGATIVE = -1e30
ROOT = 0.7978845608028654
CUBE = 0.044715
SCALE = HEAD**-0.5
LAST = 1
DELAY = 5
F32 = jnp.float32
BF16 = jnp.bfloat16
VMEM_BYTES = 32 * 1024 * 1024

NN = (((1,), (0,)), ((), ()))
NT = (((1,), (1,)), ((), ()))
TN = (((0,), (0,)), ((), ()))

IN_HBM = pl.BlockSpec(memory_space=pltpu.HBM)
IN_VMEM = pl.BlockSpec(memory_space=pltpu.VMEM)
IN_SMEM = pl.BlockSpec(memory_space=pltpu.SMEM)


def mm(left, right, dims):
    return lax.dot_general(left, right, dims, preferred_element_type=F32)


def cost(flops, bytes_accessed, transcendentals=0):
    return pl.CostEstimate(
        flops=int(flops), bytes_accessed=int(bytes_accessed), transcendentals=int(transcendentals)
    )


def in_hbm(arrays):
    return [pltpu.with_memory_space_constraint(array, pltpu.HBM) for array in arrays]


def params(semantics=None):
    return pltpu.CompilerParams(dimension_semantics=semantics, vmem_limit_bytes=VMEM_BYTES)


def combos(bits):
    found = [0]
    for bit in bits:
        found = [i | extra for i in found for extra in (0, 1 << bit)]
    return found


def exchange_plan(chips, shared):
    bits = list(range(chips.bit_length() - 1))
    return (bits[: len(bits) // 2], bits[len(bits) // 2 :]) if shared else (bits, [])


def reversed_bits(chip, chips):
    count = chips.bit_length() - 1
    return sum(((chip >> bit) & 1) << (count - 1 - bit) for bit in range(count))


def across(value, bit):
    ranks = lax.axis_size("seq")
    last = (ranks // 2).bit_length() - 2
    pairs = [(i, i ^ (2 << (last - bit if i % 2 else bit))) for i in range(ranks)]
    return lax.ppermute(value, "seq", pairs)


def other_core(value):
    ranks = lax.axis_size("seq")
    return lax.ppermute(value, "seq", [(i, i ^ 1) for i in range(ranks)])


def ring(value, turn=1):
    depth = lax.axis_size("mp")
    cycle = [0] + list(range(1, depth, 2)) + list(range(2, depth, 2))[::-1]
    pairs = [(cycle[i], cycle[(i + turn) % depth]) for i in range(depth)]
    return lax.ppermute(value, "mp", pairs)


def joined(arrays):
    return arrays[0] if len(arrays) == 1 else jnp.concatenate(arrays, axis=0)


def gather_places(plan):
    bits, kept = plan
    held = [combos(kept)]
    for bit in bits:
        flat = [i for part in held for i in part]
        held = [flat, [i | (1 << bit) for i in flat]]
    return held


def scatter_order(plan):
    return combos(plan[0] + plan[1])


def added(*parts):
    total = parts[0].astype(F32)
    for part in parts[1:]:
        total = total + part.astype(F32)
    return total.astype(BF16)


def swapped(value, at, count):
    shape = value.shape
    parts = value.reshape((2**at, 2, 2 ** (count - at - 1)) + shape[1:])
    return jnp.concatenate([parts[:, 1:], parts[:, :1]], axis=1).reshape(shape)


class Pipe:
    def __init__(self):
        self.slot = 0
        self.flights = []

    def launch(self, chain):
        self.advance(chain, None)

    def advance(self, chain, got):
        try:
            arrays, slots = chain.send(got)
        except StopIteration:
            return
        self.flights.append((chain, arrays, self.slot + slots))

    def step(self, outs):
        self.slot += 1
        due = [f for f in self.flights if f[2] <= self.slot]
        self.flights = [f for f in self.flights if f[2] > self.slot]
        outs, got = lax.optimization_barrier((outs, [f[1] for f in due]))
        for flight, arrays in zip(due, got):
            self.advance(flight[0], arrays)
        return outs

    def drain(self):
        while self.flights:
            due, self.flights = self.flights, []
            self.slot = max(self.slot, min(f[2] for f in due))
            for flight in due:
                self.advance(flight[0], flight[1])


def gather_chain(piece, plan, done, last=1, pause=0):
    held = [piece]
    for at, bit in enumerate(plan[0]):
        if at and pause:
            yield [], pause
        whole = joined(held)
        (got,) = yield [across(whole, bit)], (last if at == len(plan[0]) - 1 else 1)
        held = [whole, got]
    done(held)


def weights_chain(pipe, piece, turn, shards, plan, done, first=1):
    for at, k in enumerate(shards):
        (piece,) = yield [ring(piece, turn)], (1 if at else first)
        pipe.launch(gather_chain(piece, plan, functools.partial(done, k), 1, int(turn < 0)))


def scatter_chain(low, high, plan, done, wait=0):
    if wait:
        low, high = yield [low, high], wait
    lows = [low]
    for at, bit in enumerate(plan[0]):
        (got,) = yield [across(high, bit)], 1
        lows = lows + [got]
        if at + 1 < len(plan[0]):
            half = got.shape[0] // 2
            high = added(*[part[half:] for part in lows])
            lows = [part[:half] for part in lows]
    done(lows)


class Collect:
    def __init__(self, pipe, count, plan, done):
        self.pipe, self.count, self.plan, self.done = pipe, count, plan, done
        self.parts, self.next, self.sums, self.busy = {}, 1 % count, None, False

    def ready(self, k, totals):
        self.parts[k] = totals
        self.go()

    def go(self):
        if self.busy or self.next is None or self.next not in self.parts:
            return
        parts = self.parts[self.next] + ([] if self.sums is None else [self.sums])
        self.sums = added(*parts)
        if self.next == 0:
            self.next = None
            self.finish(self.sums)
            return
        self.next = (self.next + 1) % self.count
        self.busy = True
        self.pipe.launch(self.hop())

    def hop(self):
        (self.sums,) = yield [ring(self.sums)], 1
        self.busy = False
        self.go()

    def finish(self, total):
        self.pipe.launch(self.spread(total))

    def spread(self, total):
        kept = self.plan[1]
        for at, bit in enumerate(kept):
            (got,) = yield [across(total, bit)], 1
            total = added(total, swapped(got, at, len(kept)))
        self.pipe.launch(gather_chain(total, self.plan, self.cores, 1 if kept else LAST))

    def cores(self, held):
        def chain():
            got = yield [other_core(part) for part in held], 1
            self.done(held + got)

        self.pipe.launch(chain())


class CollectBothWays(Collect):
    def __init__(self, pipe, count, plan, done):
        super().__init__(pipe, count, plan, done)
        half = count // 2
        self.ways = [[-1, list(range(half, 0, -1))], [1, list(range(half + 1, count))]]
        self.moving, self.arrived = [None, None], []

    def go(self):
        for way in range(2):
            turn, waiting = self.ways[way]
            if not waiting or waiting[0] not in self.parts or self.moving[way] == "busy":
                continue
            parts = self.parts[waiting.pop(0)]
            parts = parts if self.moving[way] is None else parts + [self.moving[way]]
            self.moving[way] = "busy"
            self.pipe.launch(self.travel(way, turn, parts))
        if not (self.ways[0][1] or self.ways[1][1]) and 0 in self.parts:
            if len(self.arrived) == sum(1 for w in (self.count // 2, self.count - self.count // 2 - 1) if w):
                if self.next is not None:
                    self.next = None
                    self.finish(added(*self.parts[0], *self.arrived))

    def travel(self, way, turn, parts):
        value = parts[0] if len(parts) == 1 else added(*parts)
        (value,) = yield [ring(value, turn)], 1 + way
        self.moving[way] = value
        if not self.ways[way][1]:
            self.arrived.append(value)
        self.go()


def sum_axis(value, axis, bits):
    size = lax.axis_size(axis)
    for first in range(0, len(bits), 2):
        now = bits[first : first + 2]
        offsets = [a ^ b for b in [0, *now[1:]] for a in (0, now[0])]
        parts = [value]
        parts += [lax.ppermute(value, axis, [(i, i ^ o) for i in range(size)]) for o in offsets[1:]]
        while len(parts) > 1:
            parts = [a + b for a, b in zip(parts[::2], parts[1::2])]
        value = parts[0]
    return value


def bits_of(size, first):
    return [1 << bit for bit in range(first, size.bit_length() - 1)]


def select_kernel(place_ref, base_ref, out_ref):
    span = base_ref.shape[1]
    for at in range(base_ref.shape[0]):
        place = place_ref[at]
        hot = lax.broadcasted_iota(jnp.int32, (place.shape[0], span), 1) == place
        out_ref[at] = mm(hot.astype(BF16), base_ref[at], NN).astype(BF16)


def together(group, span):
    size = max(1, min(group, 2048 // span))
    while group % size:
        size -= 1
    return size


def select_rows(place, base):
    group, span, width = base.shape
    slots = place.shape[1]
    size = together(group, span)
    return pl.pallas_call(
        select_kernel,
        grid=(group // size,),
        in_specs=[
            pl.BlockSpec((size, slots, 1), lambda g: (g, 0, 0)),
            pl.BlockSpec((size, span, width), lambda g: (g, 0, 0)),
        ],
        out_specs=pl.BlockSpec((size, slots, width), lambda g: (g, 0, 0)),
        out_shape=jax.ShapeDtypeStruct((group, slots, width), BF16),
        compiler_params=params(("arbitrary",)),
        cost_estimate=cost(2 * group * slots * span * width, 2 * group * (span + slots) * width),
    )(place[:, :, None], pltpu.with_memory_space_constraint(base, pltpu.HBM))


def add_kernel(place_ref, base_ref, rows_ref, out_ref):
    span = base_ref.shape[1]
    for at in range(base_ref.shape[0]):
        place = place_ref[at]
        hot = lax.broadcasted_iota(jnp.int32, (span, place.shape[1]), 0) == place
        moved = mm(hot.astype(BF16), rows_ref[at], NN)
        out_ref[at] = (base_ref[at].astype(F32) + moved).astype(BF16)


def add_rows(place, base, rows):
    group, span, width = base.shape
    slots = place.shape[1]
    size = together(group, span)
    block = pl.BlockSpec((size, span, width), lambda g: (g, 0, 0))
    return pl.pallas_call(
        add_kernel,
        grid=(group // size,),
        in_specs=[
            pl.BlockSpec((size, 1, slots), lambda g: (g, 0, 0)),
            block,
            pl.BlockSpec((size, slots, width), lambda g: (g, 0, 0)),
        ],
        out_specs=block,
        out_shape=jax.ShapeDtypeStruct(base.shape, BF16),
        compiler_params=params(("arbitrary",)),
        cost_estimate=cost(2 * group * slots * span * width, 4 * group * span * width),
    )(place[:, None, :], pltpu.with_memory_space_constraint(base, pltpu.HBM), rows)


def start_all(copies, sems):
    started = []
    for at, (source, target) in enumerate(copies):
        copy = pltpu.make_async_copy(source, target, sems.at[at])
        copy.start()
        started.append(copy)
    return started


def attention_copies(chip, sources, places, target, outward=False):
    if len(sources) == 1:
        return [(sources[0].at[3] if outward else sources[0], target)]
    depth = sources[0].shape[2]
    copies = []
    for source, ids in zip(sources, places):
        for at, index in enumerate(ids):
            rows = pl.ds(pl.multiple_of((chip ^ index) * depth, depth), depth)
            if outward:
                copies.append((source.at[at, 3], target.at[rows, :]))
            else:
                copies.append((source.at[at], target.at[:, rows, :]))
    return copies


def mlp_copies(chip, sources, places, order, targets, own):
    copies = []
    for place, index in enumerate(order):
        for side in range(2):
            target = targets[side]
            depth = target.shape[0] // len(order)
            if own:
                start = pl.multiple_of((chip ^ index) * depth, depth)
                source = sources[side].at[pl.ds(start, depth), :]
            else:
                for array, ids in zip(sources, places):
                    if index in ids:
                        source = array.at[ids.index(index), side]
            copies.append((source, target.at[pl.ds(place * depth, depth), :]))
    return copies


def row_blocks(rows):
    blocks = []
    for start in (0, rows // 2):
        half = rows // 6
        for first, last, low, high in ((0, 1, 0, 1), (1, 2, 0, 2), (2, 3, 2, 3)):
            blocks.append(tuple(start + half * at for at in (first, last, low, high)))
    return blocks


def causal(first, last, low, high):
    shape = (last - first, high - low)
    row = lax.broadcasted_iota(jnp.int32, shape, 0) + (first - low)
    return row >= lax.broadcasted_iota(jnp.int32, shape, 1)


def head_groups(columns):
    lanes = min(LANES, columns)
    return [
        (slice(at, at + lanes), at // HEAD, lanes // HEAD) for at in range(0, columns, lanes)
    ]


def own_lanes(value, side, heads):
    if heads == 1:
        return value
    lane = lax.broadcasted_iota(jnp.int32, (1, value.shape[1]), 1)
    mine = (lane >= HEAD) if side else (lane < HEAD)
    return jnp.where(mine, value, jnp.zeros_like(value))


def finish(total, last, outs):
    if not last:
        outs[0][...] = total
        return
    half = total.shape[0] // 2
    outs[0][...] = total[:half]
    outs[1][...] = total[half:].astype(BF16)


def sum_shapes(rows, width, last):
    if not last:
        return [jax.ShapeDtypeStruct((rows, width), F32)]
    return [
        jax.ShapeDtypeStruct((rows // 2, width), F32),
        jax.ShapeDtypeStruct((rows // 2, width), BF16),
    ]


def attention_forward_kernel(places, counts, chip_ref, normed_ref, *refs):
    sources = []
    for count in counts:
        sources.append(refs[:count])
        refs = refs[count:]
    others, refs = refs[: len(counts) - 1], refs[len(counts) - 1 :]
    heads_ref, mixed_ref, log_ref, *refs = refs
    sums, (held, *out_held, sems) = (refs[:2], refs[2:]) if len(counts) > 1 else ([], refs)
    chip = chip_ref[0]
    copies = attention_copies(chip, sources[-1], places, held)
    n_own = len(copies)
    for at, shard in enumerate(sources[:-1]):
        copies += attention_copies(chip, shard, places, out_held[0].at[at], True)
    copies = start_all(copies, sems)
    for copy in copies[:n_own]:
        copy.wait()
    rows = normed_ref.shape[0]
    columns = held.shape[2]
    heads_all = mm(normed_ref[...], jnp.concatenate([held[c] for c in range(3)], axis=-1), NN)
    for c in range(3):
        heads_ref[c] = heads_all[:, c * columns : (c + 1) * columns].astype(BF16)
    lane = lax.broadcasted_iota(jnp.int32, (1, LANES), 1)
    for first, end, low, high in row_blocks(rows):
        seen = causal(first, end, low, high)
        logs = jnp.zeros((end - first, LANES), F32)
        for lanes, head, heads in head_groups(columns):
            query = heads_ref[0, first:end, lanes]
            keys = heads_ref[1, low:high, lanes]
            values = heads_ref[2, low:high, lanes]
            out = None
            for side in range(heads):
                scores = mm(own_lanes(query, side, heads), keys, NT) * SCALE
                scores = jnp.where(seen, scores, NEGATIVE)
                peak = jnp.max(scores, axis=-1, keepdims=True)
                raised = jnp.exp(scores - peak)
                total = jnp.sum(raised, axis=-1, keepdims=True)
                weights = (raised * (1.0 / total)).astype(BF16)
                part = own_lanes(mm(weights, values, NN), side, heads)
                out = part if out is None else out + part
                logs = jnp.where(lane == head + side, peak + jnp.log(total), logs)
            mixed_ref[first:end, lanes] = out.astype(BF16)
        log_ref[first:end, :] = logs
    for copy in copies[n_own:]:
        copy.wait()
    if len(counts) > 1:
        mixed = [part[...] for part in others] + [mixed_ref[...]]
        outward = [out_held[0][at] for at in range(len(counts) - 1)] + [held[3]]
        attended = mm(
            jnp.concatenate(mixed, axis=-1), jnp.concatenate(outward, axis=-1), NT
        )
        finish(attended, True, sums)


def attention_forward(chip, normed, shards, places, mixed):
    rows, width = normed.shape
    columns = shards[0][0].shape[-1]
    counts = [len(shard) for shard in shards]
    last = len(shards) > 1
    sources = [source for shard in shards for source in shard]
    chips = lax.axis_size("seq") // 2
    flops = 2 * rows * width * columns * (3 + last * len(shards)) + rows * rows * columns
    scratch = [pltpu.VMEM((4, width, columns), BF16)]
    if last:
        scratch.append(pltpu.VMEM((len(shards) - 1, width, columns), BF16))
    return pl.pallas_call(
        functools.partial(attention_forward_kernel, places, counts),
        in_specs=[IN_SMEM, IN_VMEM] + [IN_HBM] * len(sources) + [IN_VMEM] * len(mixed),
        out_specs=[IN_VMEM] * (3 + 2 * last),
        out_shape=[
            jax.ShapeDtypeStruct((3, rows, columns), BF16),
            jax.ShapeDtypeStruct((rows, columns), BF16),
            jax.ShapeDtypeStruct((rows, LANES), F32),
        ]
        + (sum_shapes(rows, width, True) if last else []),
        scratch_shapes=scratch + [pltpu.SemaphoreType.DMA((chips * len(shards),))],
        compiler_params=params(),
        cost_estimate=cost(flops, 2 * rows * width + 8 * width * columns, rows * rows * 2),
    )(chip, normed, *in_hbm(sources), *mixed)


def attention_backward_kernel(
    places,
    order,
    n_sources,
    has_acc,
    last,
    chip_ref,
    grad_ref,
    normed_ref,
    heads_ref,
    mixed_ref,
    log_ref,
    *refs,
):
    sources, refs = refs[:n_sources], refs[n_sources:]
    if has_acc:
        acc_ref, refs = refs[0], refs[1:]
    sums, refs = refs[: 1 + last], refs[1 + last :]
    outs, refs = refs[:2], refs[2:]
    held, grad_held, grad_heads, sems, out_sems = refs
    chip = chip_ref[0]
    copies = start_all(attention_copies(chip, sources, places, held), sems)
    rows = normed_ref.shape[0]
    width = held.shape[2]
    depth = outs[0].shape[2]
    grad_held[3] = mm(mixed_ref[...], grad_ref[...], TN).astype(BF16).T
    for copy in copies:
        copy.wait()
    grad_mixed = mm(grad_ref[...], held[3], NN).astype(BF16)
    lane = lax.broadcasted_iota(jnp.int32, (1, LANES), 1)
    for lanes, head, heads in head_groups(width):
        key_parts, value_parts = [], []
        for first, end, low, high in row_blocks(rows):
            query = heads_ref[0, first:end, lanes]
            keys = heads_ref[1, low:high, lanes]
            values = heads_ref[2, low:high, lanes]
            grad_out = grad_mixed[first:end, lanes]
            logs = log_ref[first:end, :]
            seen = causal(first, end, low, high)
            grad_query = grad_keys = grad_values = None
            for side in range(heads):
                own_query = own_lanes(query, side, heads)
                own_grad = own_lanes(grad_out, side, heads)
                log_total = jnp.sum(
                    jnp.where(lane == head + side, logs, 0.0), axis=-1, keepdims=True
                )
                scores = jnp.where(seen, mm(own_query, keys, NT) * SCALE, NEGATIVE)
                shares = jnp.exp(scores - log_total)
                grad_weights = mm(own_grad, values, NT)
                inner = jnp.sum(shares * grad_weights, axis=-1, keepdims=True)
                grad_scores = (shares * (grad_weights - inner)).astype(BF16)
                weights = shares.astype(BF16)
                part_query = own_lanes(mm(grad_scores, keys, NN), side, heads)
                part_keys = mm(grad_scores, own_query, TN)
                part_values = mm(weights, own_grad, TN)
                if side == 0:
                    grad_query, grad_keys, grad_values = part_query, part_keys, part_values
                else:
                    grad_query = grad_query + part_query
                    grad_keys = grad_keys + part_keys
                    grad_values = grad_values + part_values
            grad_heads[0, first:end, lanes] = (grad_query * SCALE).astype(BF16)
            key_parts.append(grad_keys)
            value_parts.append(grad_values)
        half = rows // 6
        for c, parts, scale in ((1, key_parts, SCALE), (2, value_parts, 1.0)):
            for pair in range(2):
                one, two, three = parts[3 * pair : 3 * pair + 3]
                for at, value in enumerate((one + two[:half], two[half:], three)):
                    start = (3 * pair + at) * half
                    grad_heads[c, start : start + half, lanes] = (value * scale).astype(BF16)
    grad_all = jnp.concatenate([grad_heads[c] for c in range(3)], axis=-1)
    grad_qkv = mm(grad_all, normed_ref[...], TN).astype(BF16)
    for c in range(3):
        grad_held[c] = grad_qkv[c * width : (c + 1) * width].T
    copies = []
    for at, index in enumerate(order):
        start = pl.multiple_of((chip ^ index) * depth, depth)
        high, at = divmod(at, len(order) // 2)
        copies.append((grad_held.at[:, pl.ds(start, depth), :], outs[high].at[at]))
    copies = start_all(copies, out_sems)
    grad_normed = mm(grad_all, jnp.concatenate([held[c] for c in range(3)], axis=-1), NT)
    if has_acc:
        grad_normed = grad_normed + acc_ref[...]
    finish(grad_normed, last, sums)
    for copy in copies:
        copy.wait()


def attention_backward(chip, grad, normed, saved, sources, places, order, acc, last):
    rows, width = normed.shape
    columns = sources[0].shape[-1]
    chips = lax.axis_size("seq") // 2
    has_acc = acc is not None
    n_sources = len(sources)
    n_copies = 1 if n_sources == 1 else chips
    piece = jax.ShapeDtypeStruct((chips // 2, 4, width // chips, columns), BF16)
    flops = 2 * rows * width * columns * 8 + 3 * rows * rows * columns
    return pl.pallas_call(
        functools.partial(
            attention_backward_kernel, places, order, n_sources, has_acc, last
        ),
        in_specs=[IN_SMEM] + [IN_VMEM] * 5 + [IN_HBM] * n_sources + [IN_VMEM] * has_acc,
        out_specs=[IN_VMEM] * (1 + last) + [IN_HBM] * 2,
        out_shape=sum_shapes(rows, width, last) + [piece] * 2,
        scratch_shapes=[
            pltpu.VMEM((4, width, columns), BF16),
            pltpu.VMEM((4, width, columns), BF16),
            pltpu.VMEM((3, rows, columns), BF16),
            pltpu.SemaphoreType.DMA((n_copies,)),
            pltpu.SemaphoreType.DMA((chips,)),
        ],
        input_output_aliases={6 + n_sources: 0} if has_acc and not last else {},
        compiler_params=params(),
        cost_estimate=cost(flops, 12 * rows * width + 16 * width * columns, rows * rows * 2),
    )(chip, grad, normed, *saved, *in_hbm(sources), *([acc] if has_acc else []))


def mlp_kernel(places, order, n_sources, has_acc, last, chip_ref, normed_ref, grad_ref, *refs):
    sources, refs = refs[:n_sources], refs[n_sources:]
    if has_acc:
        acc_in, refs = refs[:2], refs[2:]
    sums, refs = refs[: 2 + 2 * last], refs[2 + 2 * last :]
    outs, refs = refs[:2], refs[2:]
    up_held, down_held, up_grad, down_grad, active_held, upward_held, sems, out_sems = refs
    own = not has_acc
    copies = mlp_copies(chip_ref[0], sources, places, order, (up_held, down_held), own)
    copies = start_all(copies, sems)
    hidden = up_held.shape[0]
    depth = hidden // len(order)
    step = max(depth, min(256, hidden))
    waited = 0
    leaving = []
    for start in range(0, hidden, step):
        ready = 2 * ((start + step) // depth)
        for copy in copies[waited:ready]:
            copy.wait()
        waited = ready
        chunk = slice(start, start + step)
        upward = mm(normed_ref[...], up_held[chunk], NT)
        square = upward * upward
        bent = jnp.tanh(ROOT * upward * (1.0 + CUBE * square))
        active = (0.5 * upward * (1.0 + bent)).astype(BF16)
        slope = 0.5 * (1.0 + bent) + 0.5 * ROOT * upward * (1.0 - bent * bent) * (
            1.0 + 3.0 * CUBE * square
        )
        grad_active = mm(grad_ref[...], down_held[chunk], NT)
        grad_upward = (grad_active * slope).astype(BF16)
        active_held[:, chunk] = active
        upward_held[:, chunk] = grad_upward
        up_grad[chunk] = mm(grad_upward, normed_ref[...], TN).astype(BF16)
        down_grad[chunk] = mm(active, grad_ref[...], TN).astype(BF16)
        for at in range(start // depth, (start + step) // depth):
            for side, grads in enumerate((up_grad, down_grad)):
                high, place = divmod(at, len(order) // 2)
                copy = pltpu.make_async_copy(
                    grads.at[pl.ds(at * depth, depth), :],
                    outs[high].at[place, side],
                    out_sems.at[2 * at + side],
                )
                copy.start()
                leaving.append(copy)
    for i, (left, right) in enumerate(((active_held, down_held), (upward_held, up_held))):
        total = mm(left[...], right[...], NN)
        if has_acc:
            total = total + acc_in[i][...]
        finish(total, last, sums[i * (1 + last) : (i + 1) * (1 + last)])
    for copy in leaving:
        copy.wait()


def mlp(chip, normed, grad, sources, hidden, places, order, acc, last):
    rows, width = normed.shape
    chips = len(order)
    depth = hidden // chips
    has_acc = acc is not None
    n_sources = len(sources)
    piece = jax.ShapeDtypeStruct((chips // 2, 2, depth, width), BF16)
    aliased = {3 + n_sources: 0, 4 + n_sources: 1} if has_acc and not last else {}
    return pl.pallas_call(
        functools.partial(mlp_kernel, places, order, n_sources, has_acc, last),
        in_specs=[IN_SMEM] + [IN_VMEM] * 2 + [IN_HBM] * n_sources + [IN_VMEM] * (2 * has_acc),
        out_specs=[IN_VMEM] * (2 + 2 * last) + [IN_HBM] * 2,
        out_shape=sum_shapes(rows, width, last) * 2 + [piece] * 2,
        scratch_shapes=[pltpu.VMEM((hidden, width), BF16)] * 4
        + [pltpu.VMEM((rows, hidden), BF16)] * 2
        + [
            pltpu.SemaphoreType.DMA((2 * chips,)),
            pltpu.SemaphoreType.DMA((2 * chips,)),
        ],
        input_output_aliases=aliased,
        compiler_params=params(),
        cost_estimate=cost(
            12 * rows * width * hidden, 20 * rows * width + 8 * width * hidden, rows * hidden
        ),
    )(chip, normed, grad, *in_hbm(sources), *(acc if has_acc else []))


def place_attention_kernel(places, n_sources, chip_ref, core_ref, *refs):
    sources, refs = refs[:n_sources], refs[n_sources:]
    qkv_ref, out_ref, held, sems = refs
    half = n_sources // 2
    copies = []
    for which, core in enumerate((core_ref[0], 1 - core_ref[0])):
        copies += attention_copies(
            chip_ref[which], sources[which * half : (which + 1) * half], places, held.at[core]
        )
    for copy in start_all(copies, sems):
        copy.wait()
    columns = held.shape[3]
    for c in range(3):
        qkv_ref[c] = jnp.concatenate([held[0, c], held[1, c]], axis=-1).astype(F32)
    for core in range(2):
        out_ref[core * columns : (core + 1) * columns, :] = held[core, 3].astype(F32).T


def place_attention(chip, core, sources, places, width):
    columns = sources[0].shape[-1]
    n_sources = len(sources)
    return pl.pallas_call(
        functools.partial(place_attention_kernel, places, n_sources),
        in_specs=[IN_SMEM, IN_SMEM] + [IN_HBM] * n_sources,
        out_specs=[IN_VMEM] * 2,
        out_shape=[
            jax.ShapeDtypeStruct((3, width, 2 * columns), F32),
            jax.ShapeDtypeStruct((2 * columns, width), F32),
        ],
        scratch_shapes=[
            pltpu.VMEM((2, 4, width, columns), BF16),
            pltpu.SemaphoreType.DMA((2 * lax.axis_size("seq"),)),
        ],
        compiler_params=params(),
        cost_estimate=cost(0, 48 * width * columns),
    )(chip, core, *sources)


def place_mlp_kernel(places, order, n_sources, chip_ref, core_ref, *refs):
    sources, refs = refs[:n_sources], refs[n_sources:]
    out_ref, up_held, down_held, out_held, sems, out_sems = refs
    core = core_ref[0]
    hidden, width = up_held.shape[1:]
    half = n_sources // 2
    copies = []
    for which in range(2):
        targets = (up_held.at[which], down_held.at[which])
        copies += mlp_copies(
            chip_ref[which],
            sources[which * half : (which + 1) * half],
            places,
            order,
            targets,
            False,
        )
    copies = start_all(copies, sems)
    depth = hidden // len(order)
    tiles = width // LANES
    size = depth * 2 * tiles
    moved = []
    for which in range(2):
        for at, index in enumerate(order):
            base = len(moved)
            for side, part in enumerate((up_held, down_held)):
                copies[2 * base + side].wait()
                rows = part[which, at * depth : (at + 1) * depth, :].astype(F32)
                for tile in range(tiles):
                    out_held[pl.ds(base * size + 2 * tile + side, depth, stride=2 * tiles), :] = (
                        rows[:, tile * LANES : (tile + 1) * LANES]
                    )
            block = ((core if which == 0 else 1 - core) * len(order) + (chip_ref[which] ^ index)) * size
            copy = pltpu.make_async_copy(
                out_held.at[pl.ds(base * size, size), :],
                out_ref.at[pl.ds(pl.multiple_of(block, size), size), :],
                out_sems.at[base],
            )
            copy.start()
            moved.append(copy)
    for copy in moved:
        copy.wait()


def place_mlp(chip, core, sources, places, order, hidden):
    width = sources[0].shape[-1]
    n_sources = len(sources)
    tiles = width // LANES
    chips = len(order)
    rows = pl.pallas_call(
        functools.partial(place_mlp_kernel, places, order, n_sources),
        in_specs=[IN_SMEM, IN_SMEM] + [IN_HBM] * n_sources,
        out_specs=IN_HBM,
        out_shape=jax.ShapeDtypeStruct((hidden * 2 * tiles, LANES), F32),
        scratch_shapes=[
            pltpu.VMEM((2, hidden // 2, width), BF16),
            pltpu.VMEM((2, hidden // 2, width), BF16),
            pltpu.VMEM((hidden * 2 * tiles, LANES), F32),
            pltpu.SemaphoreType.DMA((4 * chips,)),
            pltpu.SemaphoreType.DMA((2 * chips,)),
        ],
        compiler_params=params(),
        cost_estimate=cost(0, 12 * hidden * width),
    )(chip, core, *sources)
    shaped = rows.reshape(hidden, tiles, 2, LANES)
    return shaped.transpose(0, 2, 1, 3).reshape(hidden, 2, width)


def rms_scale(values):
    return lax.rsqrt(jnp.mean(values * values, axis=-1, keepdims=True) + EPSILON)


def norm_back(grad_normed, unit_rows, scale, gain):
    scaled = gain * grad_normed
    return scale * (scaled - unit_rows * jnp.mean(unit_rows * scaled, axis=-1, keepdims=True))


def pack(first_longer, got):
    ranks, held, slots, width = got.shape
    longer = jnp.where(first_longer, got[:, 0], got[:, 1])
    shorter = jnp.where(first_longer, got[: ranks // 2, 1], got[: ranks // 2, 0])
    return jnp.concatenate(
        [longer.reshape(ranks * slots, width), shorter.reshape(ranks * slots // 2, width)]
    )


def unpack(first_longer, packed, ranks):
    rows, width = packed.shape
    half = rows // 3
    longer = packed[: 2 * half]
    shorter = jnp.concatenate([packed[2 * half :], jnp.zeros((half, width), packed.dtype)])
    both = jnp.stack(
        [
            jnp.where(first_longer, longer, shorter),
            jnp.where(first_longer, shorter, longer),
        ]
    )
    return both.reshape(1, 2, ranks, 2 * half // ranks, width)


def on_device(tokens, cotangent, lengths, routed, gain_attn, gain_mlp, router, w_qkv, w_out, w_mlp):
    group, span, width = tokens.shape
    slots = routed.shape[1]
    ranks = lax.axis_size("seq")
    count = lax.axis_size("mp")
    held = group // ranks
    chips = ranks // 2
    columns = w_qkv.shape[2] // 2
    hidden = w_mlp.shape[0] // 2
    me = lax.axis_index("seq").astype(jnp.int32)
    core = me % 2
    turned = reversed_bits(me // 2, chips)
    chip = jnp.where(core == 0, me // 2, turned)
    chip_array, core_array = chip[None], core[None]
    both_chips = jnp.stack([chip, jnp.where(core == 0, turned, me // 2)])
    whole, shared = exchange_plan(chips, False), exchange_plan(chips, True)
    whole_places, shared_places = gather_places(whole), gather_places(shared)
    whole_order, shared_order = scatter_order(whole), scatter_order(shared)
    pipe = Pipe()

    attn_shards, mlp_shards = {}, {}
    own_attn = jnp.concatenate([w_qkv, w_out.T[None]])
    own_attn = lax.dynamic_slice_in_dim(own_attn, core * columns, columns, 2)
    attn_shards[0] = [own_attn]

    def pieces_of(part, axis, plan):
        size = part.shape[axis] // chips
        return jnp.stack(
            [
                lax.dynamic_slice_in_dim(part, (chip ^ i) * size, size, axis)
                for i in combos(plan[1])
            ]
        )

    piece = pieces_of(own_attn, 1, shared)
    near, far = list(range(1, count // 2 + 1)), list(range(count - 1, count // 2, -1))
    for turn, ks in ((1, near), (-1, far)):
        pipe.launch(weights_chain(pipe, piece, turn, ks, shared, attn_shards.__setitem__))

    slot = lax.broadcasted_iota(jnp.int32, routed.shape, 1)
    live = me * slots + slot < (lengths // 8)[:, None]
    place = jnp.where(live, slot * 8 + routed % 8, -1)
    pair = lax.dynamic_slice_in_dim(lengths, me * held, held, 0)
    first_longer = pair[0] >= pair[1]
    rows = {}

    def to_holder(value, name):
        value = value.reshape(ranks, held, slots, width)
        got = yield [lax.all_to_all(value, "seq", split_axis=0, concat_axis=0, tiled=True)], 1
        rows[name] = pack(first_longer, got[0]).astype(F32)

    def to_position(value, name):
        value = unpack(first_longer, value, ranks)
        got = yield [lax.all_to_all(value, "seq", split_axis=2, concat_axis=0, tiled=True)], 1
        rows[name] = got[0].reshape(group, slots, width)

    def both_cores(value):
        return jnp.concatenate([value, other_core(value)])

    pipe.launch(to_holder(select_rows(place, tokens), "picked"))
    own_mlp = lax.dynamic_slice_in_dim(w_mlp, core * hidden, hidden, 0)
    own_up, own_down = own_mlp[:, 0, :], own_mlp[:, 1, :]
    chosen_grad, cotangent, own_up, own_down = pipe.step(
        (select_rows(place, cotangent), cotangent, own_up, own_down)
    )
    piece = jnp.stack([pieces_of(part, 0, whole) for part in (own_up, own_down)], axis=1)

    picked = rows["picked"]
    scale_one = rms_scale(picked)
    unit_one = picked * scale_one
    normed_one = both_cores((unit_one * gain_attn).astype(BF16))
    gate = jax.nn.sigmoid(jnp.sum(picked * router, axis=-1, keepdims=True))
    mlp_shards[0] = [own_up, own_down]
    saved, grad_feed = {}, None
    fetched = [[0]] + [[k, count - k] if count - k > k else [k] for k in near]
    for at, batch in enumerate(fetched):
        while not all(k in attn_shards for k in batch):
            normed_one = pipe.step(normed_one)
        outs = []
        for k in batch:
            final = k == fetched[-1][-1]
            before = list(saved) if final else []
            shards = [attn_shards[other] for other in before] + [attn_shards[k]]
            mixed = [saved[other][1] for other in before]
            out = attention_forward(chip_array, normed_one, shards, shared_places, mixed)
            saved[k] = out[:3]
            outs.append(out)
        if at == 0:
            outs, piece, chosen_grad, normed_one = pipe.step((outs, piece, chosen_grad, normed_one))
            for turn, ks in ((1, near), (-1, far)):
                pipe.launch(weights_chain(pipe, piece, turn, ks, whole, mlp_shards.__setitem__))
            pipe.launch(to_holder(chosen_grad, "grads"))
        elif at == len(fetched) - 1:
            grad_feed = both_cores((gate * rows["grads"]).astype(BF16))
            outs, grad_feed = pipe.step((outs, grad_feed))
        else:
            outs, normed_one = pipe.step((outs, normed_one))
        for k, out in zip(batch, outs):
            saved[k] = out[:3]
    attended, sent = outs[-1][3:]
    grad_rows = rows["grads"]
    attended = attended + other_core(sent).astype(F32)
    middle = picked + attended
    scale_two = rms_scale(middle)
    unit_two = middle * scale_two
    normed_two = both_cores((unit_two * gain_mlp).astype(BF16))

    sums, done = None, {}
    mlp_sums = Collect(pipe, count, whole, functools.partial(done.__setitem__, "mlp"))
    attn_sums = CollectBothWays(pipe, count, shared, functools.partial(done.__setitem__, "attn"))
    for k in range(count):
        while k not in mlp_shards:
            normed_two = pipe.step(normed_two)
        out = mlp(
            chip_array,
            normed_two,
            grad_feed,
            mlp_shards[k],
            hidden,
            whole_places,
            whole_order,
            sums,
            k == count - 1,
        )
        out = pipe.step(out)
        sums = out[:-2]
        pipe.launch(scatter_chain(*out[-2:], whole, functools.partial(mlp_sums.ready, k), 0 if k else DELAY))
    grad_normed_two = sums[2] + other_core(sums[3]).astype(F32)
    feed = sums[0] + other_core(sums[1]).astype(F32)
    grad_middle = norm_back(grad_normed_two, unit_two, scale_two, gain_mlp)
    grad_attended = both_cores((gate * grad_rows + grad_middle).astype(BF16))
    delta = attended + feed
    returned = (gate * delta).astype(BF16)
    grad_logit = jnp.sum(grad_rows * delta, axis=-1, keepdims=True) * gate * (1.0 - gate)
    router_part = jnp.sum(grad_logit * picked, axis=0)
    mlp_gain_part = jnp.sum(grad_normed_two * unit_two, axis=0)

    grad_sum = None
    for at, k in enumerate(far[::-1] + near[::-1] + [0]):
        out = attention_backward(
            chip_array,
            grad_attended,
            normed_one,
            saved[k],
            attn_shards[k],
            shared_places,
            shared_order,
            grad_sum,
            at == count - 1,
        )
        out = pipe.step(out)
        grad_sum = out[0]
        if at == count - 1:
            other = other_core(out[1])
        pipe.launch(scatter_chain(*out[-2:], shared, functools.partial(attn_sums.ready, k)))
        if at == max(0, count - 2):
            pipe.launch(to_position(returned, "out"))
    grad_normed_one = grad_sum + other.astype(F32)
    attn_gain_part = jnp.sum(grad_normed_one * unit_one, axis=0)
    small = sum_axis(jnp.stack([attn_gain_part, mlp_gain_part, router_part]), "seq", [1])
    small = sum_axis(small, "seq", bits_of(ranks, 1))
    grad_picked = (
        grad_middle
        + norm_back(grad_normed_one, unit_one, scale_one, gain_attn)
        + grad_logit * router
    ).astype(BF16)
    layer_out = add_rows(place, tokens, rows["out"])
    grad_picked, layer_out, small = lax.optimization_barrier((grad_picked, layer_out, small))
    pipe.launch(to_position(grad_picked, "back"))
    pipe.drain()
    grad_mlp = place_mlp(both_chips, core_array, done["mlp"], whole_places, whole_order, 2 * hidden)
    last_bits = bits_of(count, 0)
    small = sum_axis(small, "mp", last_bits[:1])
    back, grad_mlp, small = lax.optimization_barrier((rows["back"], grad_mlp, small))
    small = sum_axis(small, "mp", last_bits[1:])
    grad_tokens = add_rows(place, cotangent, back)
    grad_qkv, grad_out = place_attention(
        both_chips, core_array, done["attn"], shared_places, width
    )
    return (
        layer_out,
        grad_tokens,
        small[0],
        small[1],
        small[2],
        grad_qkv,
        grad_out,
        grad_mlp,
    )


def solution(mesh):
    placed = (
        P("mp", "seq", None),
        P("mp", "seq", None),
        P("mp"),
        P("mp", "seq"),
        P(),
        P(),
        P(),
        P(None, None, "mp"),
        P("mp", None),
        P("mp", None, None),
    )
    return jax.shard_map(
        on_device,
        mesh=mesh,
        in_specs=placed,
        out_specs=(
            P("mp", "seq", None),
            P("mp", "seq", None),
            P(),
            P(),
            P(),
            P(None, None, "mp"),
            P("mp", None),
            P("mp", None, None),
        ),
        check_vma=False,
    )
```

```python
import functools

import jax
import jax.numpy as jnp
from jax import lax
from jax.experimental import pallas as pl
from jax.experimental.pallas import tpu as pltpu
from jax.sharding import PartitionSpec as P

HEAD = 64
LANES = 128
EPSILON = 1e-06
NEGATIVE = -1e30
ROOT = 0.7978845608028654
CUBE = 0.044715
SCALE = HEAD**-0.5
LAST = 1
DELAY = 5
F32 = jnp.float32
BF16 = jnp.bfloat16
VMEM_BYTES = 32 * 1024 * 1024

NN = (((1,), (0,)), ((), ()))
NT = (((1,), (1,)), ((), ()))
TN = (((0,), (0,)), ((), ()))

IN_HBM = pl.BlockSpec(memory_space=pltpu.HBM)
IN_VMEM = pl.BlockSpec(memory_space=pltpu.VMEM)
IN_SMEM = pl.BlockSpec(memory_space=pltpu.SMEM)


def mm(left, right, dims):
    return lax.dot_general(left, right, dims, preferred_element_type=F32)


def cost(flops, bytes_accessed, transcendentals=0):
    return pl.CostEstimate(
        flops=int(flops), bytes_accessed=int(bytes_accessed), transcendentals=int(transcendentals)
    )


def in_hbm(arrays):
    return [pltpu.with_memory_space_constraint(array, pltpu.HBM) for array in arrays]


def params(semantics=None):
    return pltpu.CompilerParams(dimension_semantics=semantics, vmem_limit_bytes=VMEM_BYTES)


def combos(bits):
    found = [0]
    for bit in bits:
        found = [i | extra for i in found for extra in (0, 1 << bit)]
    return found


def exchange_plan(chips, shared):
    bits = list(range(chips.bit_length() - 1))
    return (bits[: len(bits) // 2], bits[len(bits) // 2 :]) if shared else (bits, [])


def reversed_bits(chip, chips):
    count = chips.bit_length() - 1
    return sum(((chip >> bit) & 1) << (count - 1 - bit) for bit in range(count))


def across(value, bit):
    ranks = lax.axis_size("seq")
    last = (ranks // 2).bit_length() - 2
    pairs = [(i, i ^ (2 << (last - bit if i % 2 else bit))) for i in range(ranks)]
    return lax.ppermute(value, "seq", pairs)


def other_core(value):
    ranks = lax.axis_size("seq")
    return lax.ppermute(value, "seq", [(i, i ^ 1) for i in range(ranks)])


def ring(value, turn=1):
    depth = lax.axis_size("mp")
    cycle = [0] + list(range(1, depth, 2)) + list(range(2, depth, 2))[::-1]
    pairs = [(cycle[i], cycle[(i + turn) % depth]) for i in range(depth)]
    return lax.ppermute(value, "mp", pairs)


def joined(arrays):
    return arrays[0] if len(arrays) == 1 else jnp.concatenate(arrays, axis=0)


def gather_places(plan):
    bits, kept = plan
    held = [combos(kept)]
    for bit in bits:
        flat = [i for part in held for i in part]
        held = [flat, [i | (1 << bit) for i in flat]]
    return held


def scatter_order(plan):
    return combos(plan[0] + plan[1])


def added(*parts):
    total = parts[0].astype(F32)
    for part in parts[1:]:
        total = total + part.astype(F32)
    return total.astype(BF16)


def swapped(value, at, count):
    shape = value.shape
    parts = value.reshape((2**at, 2, 2 ** (count - at - 1)) + shape[1:])
    return jnp.concatenate([parts[:, 1:], parts[:, :1]], axis=1).reshape(shape)


class Pipe:
    def __init__(self):
        self.slot = 0
        self.flights = []

    def launch(self, chain):
        self.advance(chain, None)

    def advance(self, chain, got):
        try:
            arrays, slots = chain.send(got)
        except StopIteration:
            return
        self.flights.append((chain, arrays, self.slot + slots))

    def step(self, outs):
        self.slot += 1
        due = [f for f in self.flights if f[2] <= self.slot]
        self.flights = [f for f in self.flights if f[2] > self.slot]
        outs, got = lax.optimization_barrier((outs, [f[1] for f in due]))
        for flight, arrays in zip(due, got):
            self.advance(flight[0], arrays)
        return outs

    def drain(self):
        while self.flights:
            due, self.flights = self.flights, []
            self.slot = max(self.slot, min(f[2] for f in due))
            for flight in due:
                self.advance(flight[0], flight[1])


def gather_chain(piece, plan, done, last=1, pause=0):
    held = [piece]
    for at, bit in enumerate(plan[0]):
        if at and pause:
            yield [], pause
        whole = joined(held)
        (got,) = yield [across(whole, bit)], (last if at == len(plan[0]) - 1 else 1)
        held = [whole, got]
    done(held)


def weights_chain(pipe, piece, turn, shards, plan, done, first=1):
    for at, k in enumerate(shards):
        (piece,) = yield [ring(piece, turn)], (1 if at else first)
        pipe.launch(gather_chain(piece, plan, functools.partial(done, k), 1, int(turn < 0)))


def scatter_chain(low, high, plan, done, wait=0):
    if wait:
        low, high = yield [low, high], wait
    lows = [low]
    for at, bit in enumerate(plan[0]):
        (got,) = yield [across(high, bit)], 1
        lows = lows + [got]
        if at + 1 < len(plan[0]):
            half = got.shape[0] // 2
            high = added(*[part[half:] for part in lows])
            lows = [part[:half] for part in lows]
    done(lows)


class Collect:
    def __init__(self, pipe, count, plan, done):
        self.pipe, self.count, self.plan, self.done = pipe, count, plan, done
        self.parts, self.next, self.sums, self.busy = {}, 1 % count, None, False

    def ready(self, k, totals):
        self.parts[k] = totals
        self.go()

    def go(self):
        if self.busy or self.next is None or self.next not in self.parts:
            return
        parts = self.parts[self.next] + ([] if self.sums is None else [self.sums])
        self.sums = added(*parts)
        if self.next == 0:
            self.next = None
            self.finish(self.sums)
            return
        self.next = (self.next + 1) % self.count
        self.busy = True
        self.pipe.launch(self.hop())

    def hop(self):
        (self.sums,) = yield [ring(self.sums)], 1
        self.busy = False
        self.go()

    def finish(self, total):
        self.pipe.launch(self.spread(total))

    def spread(self, total):
        kept = self.plan[1]
        for at, bit in enumerate(kept):
            (got,) = yield [across(total, bit)], 1
            total = added(total, swapped(got, at, len(kept)))
        self.pipe.launch(gather_chain(total, self.plan, self.cores, 1 if kept else LAST))

    def cores(self, held):
        def chain():
            got = yield [other_core(part) for part in held], 1
            self.done(held + got)

        self.pipe.launch(chain())


class CollectBothWays(Collect):
    def __init__(self, pipe, count, plan, done):
        super().__init__(pipe, count, plan, done)
        half = count // 2
        self.ways = [[-1, list(range(half, 0, -1))], [1, list(range(half + 1, count))]]
        self.moving, self.arrived = [None, None], []

    def go(self):
        for way in range(2):
            turn, waiting = self.ways[way]
            if not waiting or waiting[0] not in self.parts or self.moving[way] == "busy":
                continue
            parts = self.parts[waiting.pop(0)]
            parts = parts if self.moving[way] is None else parts + [self.moving[way]]
            self.moving[way] = "busy"
            self.pipe.launch(self.travel(way, turn, parts))
        if not (self.ways[0][1] or self.ways[1][1]) and 0 in self.parts:
            if len(self.arrived) == sum(1 for w in (self.count // 2, self.count - self.count // 2 - 1) if w):
                if self.next is not None:
                    self.next = None
                    self.finish(added(*self.parts[0], *self.arrived))

    def travel(self, way, turn, parts):
        value = parts[0] if len(parts) == 1 else added(*parts)
        (value,) = yield [ring(value, turn)], 1 + way
        self.moving[way] = value
        if not self.ways[way][1]:
            self.arrived.append(value)
        self.go()


def sum_axis(value, axis, bits):
    size = lax.axis_size(axis)
    for first in range(0, len(bits), 2):
        now = bits[first : first + 2]
        offsets = [a ^ b for b in [0, *now[1:]] for a in (0, now[0])]
        parts = [value]
        parts += [lax.ppermute(value, axis, [(i, i ^ o) for i in range(size)]) for o in offsets[1:]]
        while len(parts) > 1:
            parts = [a + b for a, b in zip(parts[::2], parts[1::2])]
        value = parts[0]
    return value


def bits_of(size, first):
    return [1 << bit for bit in range(first, size.bit_length() - 1)]


def select_kernel(place_ref, base_ref, out_ref):
    span = base_ref.shape[1]
    for at in range(base_ref.shape[0]):
        place = place_ref[at]
        hot = lax.broadcasted_iota(jnp.int32, (place.shape[0], span), 1) == place
        out_ref[at] = mm(hot.astype(BF16), base_ref[at], NN).astype(BF16)


def together(group, span):
    size = max(1, min(group, 2048 // span))
    while group % size:
        size -= 1
    return size


def select_rows(place, base):
    group, span, width = base.shape
    slots = place.shape[1]
    size = together(group, span)
    return pl.pallas_call(
        select_kernel,
        grid=(group // size,),
        in_specs=[
            pl.BlockSpec((size, slots, 1), lambda g: (g, 0, 0)),
            pl.BlockSpec((size, span, width), lambda g: (g, 0, 0)),
        ],
        out_specs=pl.BlockSpec((size, slots, width), lambda g: (g, 0, 0)),
        out_shape=jax.ShapeDtypeStruct((group, slots, width), BF16),
        compiler_params=params(("arbitrary",)),
        cost_estimate=cost(2 * group * slots * span * width, 2 * group * (span + slots) * width),
    )(place[:, :, None], pltpu.with_memory_space_constraint(base, pltpu.HBM))


def add_kernel(place_ref, base_ref, rows_ref, out_ref):
    span = base_ref.shape[1]
    for at in range(base_ref.shape[0]):
        place = place_ref[at]
        hot = lax.broadcasted_iota(jnp.int32, (span, place.shape[1]), 0) == place
        moved = mm(hot.astype(BF16), rows_ref[at], NN)
        out_ref[at] = (base_ref[at].astype(F32) + moved).astype(BF16)


def add_rows(place, base, rows):
    group, span, width = base.shape
    slots = place.shape[1]
    size = together(group, span)
    block = pl.BlockSpec((size, span, width), lambda g: (g, 0, 0))
    return pl.pallas_call(
        add_kernel,
        grid=(group // size,),
        in_specs=[
            pl.BlockSpec((size, 1, slots), lambda g: (g, 0, 0)),
            block,
            pl.BlockSpec((size, slots, width), lambda g: (g, 0, 0)),
        ],
        out_specs=block,
        out_shape=jax.ShapeDtypeStruct(base.shape, BF16),
        compiler_params=params(("arbitrary",)),
        cost_estimate=cost(2 * group * slots * span * width, 4 * group * span * width),
    )(place[:, None, :], pltpu.with_memory_space_constraint(base, pltpu.HBM), rows)


def start_all(copies, sems):
    started = []
    for at, (source, target) in enumerate(copies):
        copy = pltpu.make_async_copy(source, target, sems.at[at])
        copy.start()
        started.append(copy)
    return started


def attention_copies(chip, sources, places, target, outward=False):
    if len(sources) == 1:
        return [(sources[0].at[3] if outward else sources[0], target)]
    depth = sources[0].shape[2]
    copies = []
    for source, ids in zip(sources, places):
        for at, index in enumerate(ids):
            rows = pl.ds(pl.multiple_of((chip ^ index) * depth, depth), depth)
            if outward:
                copies.append((source.at[at, 3], target.at[rows, :]))
            else:
                copies.append((source.at[at], target.at[:, rows, :]))
    return copies


def mlp_copies(chip, sources, places, order, targets, own):
    copies = []
    for place, index in enumerate(order):
        for side in range(2):
            target = targets[side]
            depth = target.shape[0] // len(order)
            if own:
                start = pl.multiple_of((chip ^ index) * depth, depth)
                source = sources[side].at[pl.ds(start, depth), :]
            else:
                for array, ids in zip(sources, places):
                    if index in ids:
                        source = array.at[ids.index(index), side]
            copies.append((source, target.at[pl.ds(place * depth, depth), :]))
    return copies


def row_blocks(rows):
    blocks = []
    for start in (0, rows // 2):
        half = rows // 6
        for first, last, low, high in ((0, 1, 0, 1), (1, 2, 0, 2), (2, 3, 2, 3)):
            blocks.append(tuple(start + half * at for at in (first, last, low, high)))
    return blocks


def causal(first, last, low, high):
    shape = (last - first, high - low)
    row = lax.broadcasted_iota(jnp.int32, shape, 0) + (first - low)
    return row >= lax.broadcasted_iota(jnp.int32, shape, 1)


def head_groups(columns):
    lanes = min(LANES, columns)
    return [
        (slice(at, at + lanes), at // HEAD, lanes // HEAD) for at in range(0, columns, lanes)
    ]


def own_lanes(value, side, heads):
    if heads == 1:
        return value
    lane = lax.broadcasted_iota(jnp.int32, (1, value.shape[1]), 1)
    mine = (lane >= HEAD) if side else (lane < HEAD)
    return jnp.where(mine, value, jnp.zeros_like(value))


def finish(total, last, outs):
    if not last:
        outs[0][...] = total
        return
    half = total.shape[0] // 2
    outs[0][...] = total[:half]
    outs[1][...] = total[half:].astype(BF16)


def sum_shapes(rows, width, last):
    if not last:
        return [jax.ShapeDtypeStruct((rows, width), F32)]
    return [
        jax.ShapeDtypeStruct((rows // 2, width), F32),
        jax.ShapeDtypeStruct((rows // 2, width), BF16),
    ]


def attention_forward_kernel(places, counts, chip_ref, normed_ref, *refs):
    sources = []
    for count in counts:
        sources.append(refs[:count])
        refs = refs[count:]
    others, refs = refs[: len(counts) - 1], refs[len(counts) - 1 :]
    heads_ref, mixed_ref, log_ref, *refs = refs
    sums, (held, *out_held, sems) = (refs[:2], refs[2:]) if len(counts) > 1 else ([], refs)
    chip = chip_ref[0]
    copies = attention_copies(chip, sources[-1], places, held)
    n_own = len(copies)
    for at, shard in enumerate(sources[:-1]):
        copies += attention_copies(chip, shard, places, out_held[0].at[at], True)
    copies = start_all(copies, sems)
    for copy in copies[:n_own]:
        copy.wait()
    rows = normed_ref.shape[0]
    columns = held.shape[2]
    heads_all = mm(normed_ref[...], jnp.concatenate([held[c] for c in range(3)], axis=-1), NN)
    for c in range(3):
        heads_ref[c] = heads_all[:, c * columns : (c + 1) * columns].astype(BF16)
    lane = lax.broadcasted_iota(jnp.int32, (1, LANES), 1)
    for first, end, low, high in row_blocks(rows):
        seen = causal(first, end, low, high)
        logs = jnp.zeros((end - first, LANES), F32)
        for lanes, head, heads in head_groups(columns):
            query = heads_ref[0, first:end, lanes]
            keys = heads_ref[1, low:high, lanes]
            values = heads_ref[2, low:high, lanes]
            out = None
            for side in range(heads):
                scores = mm(own_lanes(query, side, heads), keys, NT) * SCALE
                scores = jnp.where(seen, scores, NEGATIVE)
                peak = jnp.max(scores, axis=-1, keepdims=True)
                raised = jnp.exp(scores - peak)
                total = jnp.sum(raised, axis=-1, keepdims=True)
                weights = (raised * (1.0 / total)).astype(BF16)
                part = own_lanes(mm(weights, values, NN), side, heads)
                out = part if out is None else out + part
                logs = jnp.where(lane == head + side, peak + jnp.log(total), logs)
            mixed_ref[first:end, lanes] = out.astype(BF16)
        log_ref[first:end, :] = logs
    for copy in copies[n_own:]:
        copy.wait()
    if len(counts) > 1:
        mixed = [part[...] for part in others] + [mixed_ref[...]]
        outward = [out_held[0][at] for at in range(len(counts) - 1)] + [held[3]]
        attended = mm(
            jnp.concatenate(mixed, axis=-1), jnp.concatenate(outward, axis=-1), NT
        )
        finish(attended, True, sums)


def attention_forward(chip, normed, shards, places, mixed):
    rows, width = normed.shape
    columns = shards[0][0].shape[-1]
    counts = [len(shard) for shard in shards]
    last = len(shards) > 1
    sources = [source for shard in shards for source in shard]
    chips = lax.axis_size("seq") // 2
    flops = 2 * rows * width * columns * (3 + last * len(shards)) + rows * rows * columns
    scratch = [pltpu.VMEM((4, width, columns), BF16)]
    if last:
        scratch.append(pltpu.VMEM((len(shards) - 1, width, columns), BF16))
    return pl.pallas_call(
        functools.partial(attention_forward_kernel, places, counts),
        in_specs=[IN_SMEM, IN_VMEM] + [IN_HBM] * len(sources) + [IN_VMEM] * len(mixed),
        out_specs=[IN_VMEM] * (3 + 2 * last),
        out_shape=[
            jax.ShapeDtypeStruct((3, rows, columns), BF16),
            jax.ShapeDtypeStruct((rows, columns), BF16),
            jax.ShapeDtypeStruct((rows, LANES), F32),
        ]
        + (sum_shapes(rows, width, True) if last else []),
        scratch_shapes=scratch + [pltpu.SemaphoreType.DMA((chips * len(shards),))],
        compiler_params=params(),
        cost_estimate=cost(flops, 2 * rows * width + 8 * width * columns, rows * rows * 2),
    )(chip, normed, *in_hbm(sources), *mixed)


def attention_backward_kernel(
    places,
    order,
    n_sources,
    has_acc,
    last,
    chip_ref,
    grad_ref,
    normed_ref,
    heads_ref,
    mixed_ref,
    log_ref,
    *refs,
):
    sources, refs = refs[:n_sources], refs[n_sources:]
    if has_acc:
        acc_ref, refs = refs[0], refs[1:]
    sums, refs = refs[: 1 + last], refs[1 + last :]
    outs, refs = refs[:2], refs[2:]
    held, grad_held, grad_heads, sems, out_sems = refs
    chip = chip_ref[0]
    copies = start_all(attention_copies(chip, sources, places, held), sems)
    rows = normed_ref.shape[0]
    width = held.shape[2]
    depth = outs[0].shape[2]
    grad_held[3] = mm(mixed_ref[...], grad_ref[...], TN).astype(BF16).T
    for copy in copies:
        copy.wait()
    grad_mixed = mm(grad_ref[...], held[3], NN).astype(BF16)
    lane = lax.broadcasted_iota(jnp.int32, (1, LANES), 1)
    for lanes, head, heads in head_groups(width):
        key_parts, value_parts = [], []
        for first, end, low, high in row_blocks(rows):
            query = heads_ref[0, first:end, lanes]
            keys = heads_ref[1, low:high, lanes]
            values = heads_ref[2, low:high, lanes]
            grad_out = grad_mixed[first:end, lanes]
            logs = log_ref[first:end, :]
            seen = causal(first, end, low, high)
            grad_query = grad_keys = grad_values = None
            for side in range(heads):
                own_query = own_lanes(query, side, heads)
                own_grad = own_lanes(grad_out, side, heads)
                log_total = jnp.sum(
                    jnp.where(lane == head + side, logs, 0.0), axis=-1, keepdims=True
                )
                scores = jnp.where(seen, mm(own_query, keys, NT) * SCALE, NEGATIVE)
                shares = jnp.exp(scores - log_total)
                grad_weights = mm(own_grad, values, NT)
                inner = jnp.sum(shares * grad_weights, axis=-1, keepdims=True)
                grad_scores = (shares * (grad_weights - inner)).astype(BF16)
                weights = shares.astype(BF16)
                part_query = own_lanes(mm(grad_scores, keys, NN), side, heads)
                part_keys = mm(grad_scores, own_query, TN)
                part_values = mm(weights, own_grad, TN)
                if side == 0:
                    grad_query, grad_keys, grad_values = part_query, part_keys, part_values
                else:
                    grad_query = grad_query + part_query
                    grad_keys = grad_keys + part_keys
                    grad_values = grad_values + part_values
            grad_heads[0, first:end, lanes] = (grad_query * SCALE).astype(BF16)
            key_parts.append(grad_keys)
            value_parts.append(grad_values)
        half = rows // 6
        for c, parts, scale in ((1, key_parts, SCALE), (2, value_parts, 1.0)):
            for pair in range(2):
                one, two, three = parts[3 * pair : 3 * pair + 3]
                for at, value in enumerate((one + two[:half], two[half:], three)):
                    start = (3 * pair + at) * half
                    grad_heads[c, start : start + half, lanes] = (value * scale).astype(BF16)
    grad_all = jnp.concatenate([grad_heads[c] for c in range(3)], axis=-1)
    grad_qkv = mm(grad_all, normed_ref[...], TN).astype(BF16)
    for c in range(3):
        grad_held[c] = grad_qkv[c * width : (c + 1) * width].T
    copies = []
    for at, index in enumerate(order):
        start = pl.multiple_of((chip ^ index) * depth, depth)
        high, at = divmod(at, len(order) // 2)
        copies.append((grad_held.at[:, pl.ds(start, depth), :], outs[high].at[at]))
    copies = start_all(copies, out_sems)
    grad_normed = mm(grad_all, jnp.concatenate([held[c] for c in range(3)], axis=-1), NT)
    if has_acc:
        grad_normed = grad_normed + acc_ref[...]
    finish(grad_normed, last, sums)
    for copy in copies:
        copy.wait()


def attention_backward(chip, grad, normed, saved, sources, places, order, acc, last):
    rows, width = normed.shape
    columns = sources[0].shape[-1]
    chips = lax.axis_size("seq") // 2
    has_acc = acc is not None
    n_sources = len(sources)
    n_copies = 1 if n_sources == 1 else chips
    piece = jax.ShapeDtypeStruct((chips // 2, 4, width // chips, columns), BF16)
    flops = 2 * rows * width * columns * 8 + 3 * rows * rows * columns
    return pl.pallas_call(
        functools.partial(
            attention_backward_kernel, places, order, n_sources, has_acc, last
        ),
        in_specs=[IN_SMEM] + [IN_VMEM] * 5 + [IN_HBM] * n_sources + [IN_VMEM] * has_acc,
        out_specs=[IN_VMEM] * (1 + last) + [IN_HBM] * 2,
        out_shape=sum_shapes(rows, width, last) + [piece] * 2,
        scratch_shapes=[
            pltpu.VMEM((4, width, columns), BF16),
            pltpu.VMEM((4, width, columns), BF16),
            pltpu.VMEM((3, rows, columns), BF16),
            pltpu.SemaphoreType.DMA((n_copies,)),
            pltpu.SemaphoreType.DMA((chips,)),
        ],
        input_output_aliases={6 + n_sources: 0} if has_acc and not last else {},
        compiler_params=params(),
        cost_estimate=cost(flops, 12 * rows * width + 16 * width * columns, rows * rows * 2),
    )(chip, grad, normed, *saved, *in_hbm(sources), *([acc] if has_acc else []))


def mlp_kernel(places, order, n_sources, has_acc, last, chip_ref, normed_ref, grad_ref, *refs):
    sources, refs = refs[:n_sources], refs[n_sources:]
    if has_acc:
        acc_in, refs = refs[:2], refs[2:]
    sums, refs = refs[: 2 + 2 * last], refs[2 + 2 * last :]
    outs, refs = refs[:2], refs[2:]
    up_held, down_held, up_grad, down_grad, active_held, upward_held, sems, out_sems = refs
    own = not has_acc
    copies = mlp_copies(chip_ref[0], sources, places, order, (up_held, down_held), own)
    copies = start_all(copies, sems)
    hidden = up_held.shape[0]
    depth = hidden // len(order)
    step = max(depth, min(256, hidden))
    waited = 0
    leaving = []
    for start in range(0, hidden, step):
        ready = 2 * ((start + step) // depth)
        for copy in copies[waited:ready]:
            copy.wait()
        waited = ready
        chunk = slice(start, start + step)
        upward = mm(normed_ref[...], up_held[chunk], NT)
        square = upward * upward
        bent = jnp.tanh(ROOT * upward * (1.0 + CUBE * square))
        active = (0.5 * upward * (1.0 + bent)).astype(BF16)
        slope = 0.5 * (1.0 + bent) + 0.5 * ROOT * upward * (1.0 - bent * bent) * (
            1.0 + 3.0 * CUBE * square
        )
        grad_active = mm(grad_ref[...], down_held[chunk], NT)
        grad_upward = (grad_active * slope).astype(BF16)
        active_held[:, chunk] = active
        upward_held[:, chunk] = grad_upward
        up_grad[chunk] = mm(grad_upward, normed_ref[...], TN).astype(BF16)
        down_grad[chunk] = mm(active, grad_ref[...], TN).astype(BF16)
        for at in range(start // depth, (start + step) // depth):
            for side, grads in enumerate((up_grad, down_grad)):
                high, place = divmod(at, len(order) // 2)
                copy = pltpu.make_async_copy(
                    grads.at[pl.ds(at * depth, depth), :],
                    outs[high].at[place, side],
                    out_sems.at[2 * at + side],
                )
                copy.start()
                leaving.append(copy)
    for i, (left, right) in enumerate(((active_held, down_held), (upward_held, up_held))):
        total = mm(left[...], right[...], NN)
        if has_acc:
            total = total + acc_in[i][...]
        finish(total, last, sums[i * (1 + last) : (i + 1) * (1 + last)])
    for copy in leaving:
        copy.wait()


def mlp(chip, normed, grad, sources, hidden, places, order, acc, last):
    rows, width = normed.shape
    chips = len(order)
    depth = hidden // chips
    has_acc = acc is not None
    n_sources = len(sources)
    piece = jax.ShapeDtypeStruct((chips // 2, 2, depth, width), BF16)
    aliased = {3 + n_sources: 0, 4 + n_sources: 1} if has_acc and not last else {}
    return pl.pallas_call(
        functools.partial(mlp_kernel, places, order, n_sources, has_acc, last),
        in_specs=[IN_SMEM] + [IN_VMEM] * 2 + [IN_HBM] * n_sources + [IN_VMEM] * (2 * has_acc),
        out_specs=[IN_VMEM] * (2 + 2 * last) + [IN_HBM] * 2,
        out_shape=sum_shapes(rows, width, last) * 2 + [piece] * 2,
        scratch_shapes=[pltpu.VMEM((hidden, width), BF16)] * 4
        + [pltpu.VMEM((rows, hidden), BF16)] * 2
        + [
            pltpu.SemaphoreType.DMA((2 * chips,)),
            pltpu.SemaphoreType.DMA((2 * chips,)),
        ],
        input_output_aliases=aliased,
        compiler_params=params(),
        cost_estimate=cost(
            12 * rows * width * hidden, 20 * rows * width + 8 * width * hidden, rows * hidden
        ),
    )(chip, normed, grad, *in_hbm(sources), *(acc if has_acc else []))


def place_attention_kernel(places, n_sources, chip_ref, core_ref, *refs):
    sources, refs = refs[:n_sources], refs[n_sources:]
    qkv_ref, out_ref, held, qkv_held, out_held, sems, out_sems = refs
    half = n_sources // 2
    copies = []
    for which, core in enumerate((core_ref[0], 1 - core_ref[0])):
        copies += attention_copies(
            chip_ref[which], sources[which * half : (which + 1) * half], places, held.at[core]
        )
    for copy in start_all(copies, sems):
        copy.wait()
    columns = held.shape[3]
    leaving = []
    for c in range(3):
        qkv_held[c] = jnp.concatenate([held[0, c], held[1, c]], axis=-1).astype(F32)
        leaving.append(pltpu.make_async_copy(qkv_held.at[c], qkv_ref.at[c], out_sems.at[c]))
        leaving[-1].start()
    for core in range(2):
        out_held[core * columns : (core + 1) * columns, :] = held[core, 3].astype(F32).T
    leaving.append(pltpu.make_async_copy(out_held, out_ref, out_sems.at[3]))
    leaving[-1].start()
    for copy in leaving:
        copy.wait()


def place_attention(chip, core, sources, places, width):
    columns = sources[0].shape[-1]
    n_sources = len(sources)
    return pl.pallas_call(
        functools.partial(place_attention_kernel, places, n_sources),
        in_specs=[IN_SMEM, IN_SMEM] + [IN_HBM] * n_sources,
        out_specs=[IN_HBM] * 2,
        out_shape=[
            jax.ShapeDtypeStruct((3, width, 2 * columns), F32),
            jax.ShapeDtypeStruct((2 * columns, width), F32),
        ],
        scratch_shapes=[
            pltpu.VMEM((2, 4, width, columns), BF16),
            pltpu.VMEM((3, width, 2 * columns), F32),
            pltpu.VMEM((2 * columns, width), F32),
            pltpu.SemaphoreType.DMA((2 * lax.axis_size("seq"),)),
            pltpu.SemaphoreType.DMA((4,)),
        ],
        compiler_params=params(),
        cost_estimate=cost(0, 48 * width * columns),
    )(chip, core, *sources)


def place_mlp_kernel(places, order, n_sources, chip_ref, core_ref, *refs):
    sources, refs = refs[:n_sources], refs[n_sources:]
    out_ref, up_held, down_held, out_held, sems, out_sems = refs
    core = core_ref[0]
    hidden, width = up_held.shape[1:]
    half = n_sources // 2
    copies = []
    for which in range(2):
        targets = (up_held.at[which], down_held.at[which])
        copies += mlp_copies(
            chip_ref[which],
            sources[which * half : (which + 1) * half],
            places,
            order,
            targets,
            False,
        )
    copies = start_all(copies, sems)
    depth = hidden // len(order)
    tiles = width // LANES
    size = depth * 2 * tiles
    moved = []
    for which in range(2):
        for at, index in enumerate(order):
            base = len(moved)
            for side, part in enumerate((up_held, down_held)):
                copies[2 * base + side].wait()
                rows = part[which, at * depth : (at + 1) * depth, :].astype(F32)
                for tile in range(tiles):
                    out_held[pl.ds(base * size + 2 * tile + side, depth, stride=2 * tiles), :] = (
                        rows[:, tile * LANES : (tile + 1) * LANES]
                    )
            block = ((core if which == 0 else 1 - core) * len(order) + (chip_ref[which] ^ index)) * size
            copy = pltpu.make_async_copy(
                out_held.at[pl.ds(base * size, size), :],
                out_ref.at[pl.ds(pl.multiple_of(block, size), size), :],
                out_sems.at[base],
            )
            copy.start()
            moved.append(copy)
    for copy in moved:
        copy.wait()


def place_mlp(chip, core, sources, places, order, hidden):
    width = sources[0].shape[-1]
    n_sources = len(sources)
    tiles = width // LANES
    chips = len(order)
    rows = pl.pallas_call(
        functools.partial(place_mlp_kernel, places, order, n_sources),
        in_specs=[IN_SMEM, IN_SMEM] + [IN_HBM] * n_sources,
        out_specs=IN_HBM,
        out_shape=jax.ShapeDtypeStruct((hidden * 2 * tiles, LANES), F32),
        scratch_shapes=[
            pltpu.VMEM((2, hidden // 2, width), BF16),
            pltpu.VMEM((2, hidden // 2, width), BF16),
            pltpu.VMEM((hidden * 2 * tiles, LANES), F32),
            pltpu.SemaphoreType.DMA((4 * chips,)),
            pltpu.SemaphoreType.DMA((2 * chips,)),
        ],
        compiler_params=params(),
        cost_estimate=cost(0, 12 * hidden * width),
    )(chip, core, *sources)
    shaped = rows.reshape(hidden, tiles, 2, LANES)
    return shaped.transpose(0, 2, 1, 3).reshape(hidden, 2, width)


def rms_scale(values):
    return lax.rsqrt(jnp.mean(values * values, axis=-1, keepdims=True) + EPSILON)


def norm_back(grad_normed, unit_rows, scale, gain):
    scaled = gain * grad_normed
    return scale * (scaled - unit_rows * jnp.mean(unit_rows * scaled, axis=-1, keepdims=True))


def pack(first_longer, got):
    ranks, held, slots, width = got.shape
    longer = jnp.where(first_longer, got[:, 0], got[:, 1])
    shorter = jnp.where(first_longer, got[: ranks // 2, 1], got[: ranks // 2, 0])
    return jnp.concatenate(
        [longer.reshape(ranks * slots, width), shorter.reshape(ranks * slots // 2, width)]
    )


def unpack(first_longer, packed, ranks):
    rows, width = packed.shape
    half = rows // 3
    longer = packed[: 2 * half]
    shorter = jnp.concatenate([packed[2 * half :], jnp.zeros((half, width), packed.dtype)])
    both = jnp.stack(
        [
            jnp.where(first_longer, longer, shorter),
            jnp.where(first_longer, shorter, longer),
        ]
    )
    return both.reshape(1, 2, ranks, 2 * half // ranks, width)


def on_device(tokens, cotangent, lengths, routed, gain_attn, gain_mlp, router, w_qkv, w_out, w_mlp):
    group, span, width = tokens.shape
    slots = routed.shape[1]
    ranks = lax.axis_size("seq")
    count = lax.axis_size("mp")
    held = group // ranks
    chips = ranks // 2
    columns = w_qkv.shape[2] // 2
    hidden = w_mlp.shape[0] // 2
    me = lax.axis_index("seq").astype(jnp.int32)
    core = me % 2
    turned = reversed_bits(me // 2, chips)
    chip = jnp.where(core == 0, me // 2, turned)
    chip_array, core_array = chip[None], core[None]
    both_chips = jnp.stack([chip, jnp.where(core == 0, turned, me // 2)])
    whole, shared = exchange_plan(chips, False), exchange_plan(chips, True)
    whole_places, shared_places = gather_places(whole), gather_places(shared)
    whole_order, shared_order = scatter_order(whole), scatter_order(shared)
    pipe = Pipe()

    attn_shards, mlp_shards = {}, {}
    own_attn = jnp.concatenate([w_qkv, w_out.T[None]])
    own_attn = lax.dynamic_slice_in_dim(own_attn, core * columns, columns, 2)
    attn_shards[0] = [own_attn]

    def pieces_of(part, axis, plan):
        size = part.shape[axis] // chips
        return jnp.stack(
            [
                lax.dynamic_slice_in_dim(part, (chip ^ i) * size, size, axis)
                for i in combos(plan[1])
            ]
        )

    piece = pieces_of(own_attn, 1, shared)
    near, far = list(range(1, count // 2 + 1)), list(range(count - 1, count // 2, -1))
    for turn, ks in ((1, near), (-1, far)):
        pipe.launch(weights_chain(pipe, piece, turn, ks, shared, attn_shards.__setitem__))

    slot = lax.broadcasted_iota(jnp.int32, routed.shape, 1)
    live = me * slots + slot < (lengths // 8)[:, None]
    place = jnp.where(live, slot * 8 + routed % 8, -1)
    pair = lax.dynamic_slice_in_dim(lengths, me * held, held, 0)
    first_longer = pair[0] >= pair[1]
    rows = {}

    def to_holder(value, name):
        value = value.reshape(ranks, held, slots, width)
        got = yield [lax.all_to_all(value, "seq", split_axis=0, concat_axis=0, tiled=True)], 1
        rows[name] = pack(first_longer, got[0]).astype(F32)

    def to_position(value, name):
        value = unpack(first_longer, value, ranks)
        got = yield [lax.all_to_all(value, "seq", split_axis=2, concat_axis=0, tiled=True)], 1
        rows[name] = got[0].reshape(group, slots, width)

    def both_cores(value):
        return jnp.concatenate([value, other_core(value)])

    pipe.launch(to_holder(select_rows(place, tokens), "picked"))
    own_mlp = lax.dynamic_slice_in_dim(w_mlp, core * hidden, hidden, 0)
    own_up, own_down = own_mlp[:, 0, :], own_mlp[:, 1, :]
    chosen_grad, cotangent, own_up, own_down = pipe.step(
        (select_rows(place, cotangent), cotangent, own_up, own_down)
    )
    piece = jnp.stack([pieces_of(part, 0, whole) for part in (own_up, own_down)], axis=1)

    picked = rows["picked"]
    scale_one = rms_scale(picked)
    unit_one = picked * scale_one
    normed_one = both_cores((unit_one * gain_attn).astype(BF16))
    gate = jax.nn.sigmoid(jnp.sum(picked * router, axis=-1, keepdims=True))
    mlp_shards[0] = [own_up, own_down]
    saved, grad_feed = {}, None
    fetched = [[0]] + [[k, count - k] if count - k > k else [k] for k in near]
    for at, batch in enumerate(fetched):
        while not all(k in attn_shards for k in batch):
            normed_one = pipe.step(normed_one)
        outs = []
        for k in batch:
            final = k == fetched[-1][-1]
            before = list(saved) if final else []
            shards = [attn_shards[other] for other in before] + [attn_shards[k]]
            mixed = [saved[other][1] for other in before]
            out = attention_forward(chip_array, normed_one, shards, shared_places, mixed)
            saved[k] = out[:3]
            outs.append(out)
        if at == 0:
            outs, piece, chosen_grad, normed_one = pipe.step((outs, piece, chosen_grad, normed_one))
            for turn, ks in ((1, near), (-1, far)):
                pipe.launch(weights_chain(pipe, piece, turn, ks, whole, mlp_shards.__setitem__))
            pipe.launch(to_holder(chosen_grad, "grads"))
        elif at == len(fetched) - 1:
            grad_feed = both_cores((gate * rows["grads"]).astype(BF16))
            outs, grad_feed = pipe.step((outs, grad_feed))
        else:
            outs, normed_one = pipe.step((outs, normed_one))
        for k, out in zip(batch, outs):
            saved[k] = out[:3]
    attended, sent = outs[-1][3:]
    grad_rows = rows["grads"]
    attended = attended + other_core(sent).astype(F32)
    middle = picked + attended
    scale_two = rms_scale(middle)
    unit_two = middle * scale_two
    normed_two = both_cores((unit_two * gain_mlp).astype(BF16))

    sums, done = None, {}
    mlp_sums = Collect(pipe, count, whole, functools.partial(done.__setitem__, "mlp"))
    attn_sums = CollectBothWays(pipe, count, shared, functools.partial(done.__setitem__, "attn"))
    for k in range(count):
        while k not in mlp_shards:
            normed_two = pipe.step(normed_two)
        out = mlp(
            chip_array,
            normed_two,
            grad_feed,
            mlp_shards[k],
            hidden,
            whole_places,
            whole_order,
            sums,
            k == count - 1,
        )
        out = pipe.step(out)
        sums = out[:-2]
        pipe.launch(scatter_chain(*out[-2:], whole, functools.partial(mlp_sums.ready, k), 0 if k else DELAY))
    grad_normed_two = sums[2] + other_core(sums[3]).astype(F32)
    feed = sums[0] + other_core(sums[1]).astype(F32)
    grad_middle = norm_back(grad_normed_two, unit_two, scale_two, gain_mlp)
    grad_attended = both_cores((gate * grad_rows + grad_middle).astype(BF16))
    delta = attended + feed
    returned = (gate * delta).astype(BF16)
    grad_logit = jnp.sum(grad_rows * delta, axis=-1, keepdims=True) * gate * (1.0 - gate)
    router_part = jnp.sum(grad_logit * picked, axis=0)
    mlp_gain_part = jnp.sum(grad_normed_two * unit_two, axis=0)

    grad_sum = None
    for at, k in enumerate(far[::-1] + near[::-1] + [0]):
        out = attention_backward(
            chip_array,
            grad_attended,
            normed_one,
            saved[k],
            attn_shards[k],
            shared_places,
            shared_order,
            grad_sum,
            at == count - 1,
        )
        out = pipe.step(out)
        grad_sum = out[0]
        if at == count - 1:
            other = other_core(out[1])
        pipe.launch(scatter_chain(*out[-2:], shared, functools.partial(attn_sums.ready, k)))
        if at == max(0, count - 2):
            pipe.launch(to_position(returned, "out"))
    grad_normed_one = grad_sum + other.astype(F32)
    attn_gain_part = jnp.sum(grad_normed_one * unit_one, axis=0)
    small = sum_axis(jnp.stack([attn_gain_part, mlp_gain_part, router_part]), "seq", [1])
    small = sum_axis(small, "seq", bits_of(ranks, 1))
    grad_picked = (
        grad_middle
        + norm_back(grad_normed_one, unit_one, scale_one, gain_attn)
        + grad_logit * router
    ).astype(BF16)
    layer_out = add_rows(place, tokens, rows["out"])
    grad_picked, layer_out, small = lax.optimization_barrier((grad_picked, layer_out, small))
    pipe.launch(to_position(grad_picked, "back"))
    pipe.drain()
    grad_mlp = place_mlp(both_chips, core_array, done["mlp"], whole_places, whole_order, 2 * hidden)
    last_bits = bits_of(count, 0)
    small = sum_axis(small, "mp", last_bits[:1])
    back, grad_mlp, small = lax.optimization_barrier((rows["back"], grad_mlp, small))
    small = sum_axis(small, "mp", last_bits[1:])
    grad_tokens = add_rows(place, cotangent, back)
    grad_qkv, grad_out = place_attention(
        both_chips, core_array, done["attn"], shared_places, width
    )
    return (
        layer_out,
        grad_tokens,
        small[0],
        small[1],
        small[2],
        grad_qkv,
        grad_out,
        grad_mlp,
    )


def solution(mesh):
    placed = (
        P("mp", "seq", None),
        P("mp", "seq", None),
        P("mp"),
        P("mp", "seq"),
        P(),
        P(),
        P(),
        P(None, None, "mp"),
        P("mp", None),
        P("mp", None, None),
    )
    return jax.shard_map(
        on_device,
        mesh=mesh,
        in_specs=placed,
        out_specs=(
            P("mp", "seq", None),
            P("mp", "seq", None),
            P(),
            P(),
            P(),
            P(None, None, "mp"),
            P("mp", None),
            P("mp", None, None),
        ),
        check_vma=False,
    )
```
